32 devices in a mesh: dp: 4 (over y, x), segment: 2 (over core), band: 4 (over z).
Axes of the slice: x: 2, y: 2, z: 4, core: 2. Of those that a mesh axis runs over, the one named last changes fastest.
Arguments:
- fields: bfloat16 [4, 2, 32, 16, 512], P('dp', None, 'band'), may hold values from -6 to 6
- cell_mask: int32 [4, 2, 32, 16], P('dp', None, 'band'), may hold values 0 or 1
- merge_weight: bfloat16 [2, 1024, 512], P('segment', 'dp'), may hold values from -0.1875 to 0.1875
- qkv_weight: bfloat16 [2, 512, 1536], P('segment', 'dp')
- out_weight: bfloat16 [2, 512, 512], P('segment', 'dp'), may hold values from -1 to 1
- norm_gain: bfloat16 [2, 512], P('segment', 'dp'), may hold values from 0.099609375 to 1.8984375
- out_cotangent: bfloat16 [4, 2, 32, 16, 512], P('dp', None, 'band'), may hold values from -6 to 6
Outputs:
- section_out: bfloat16 [2, 4, 2, 32, 16, 512], P('segment', 'dp', None, 'band')
- merge_grad: float32 [2, 1024, 512], P('segment', 'dp')
- qkv_grad: float32 [2, 512, 1536], P('segment', 'dp')
- out_grad: float32 [2, 512, 512], P('segment', 'dp')
- gain_grad: float32 [2, 512], P('segment', 'dp')
The draws below stay inside these ranges and needn't reach their ends.
Inputs may be any that keep to these rules, and one draw needn't show every extreme that they name: `cell_mask`: 1 marks a cell whose keys may be attended.
All inputs are finite; a program needn't handle non-finite values. No bound on the sum of `cell_mask` on one device may be relied on, other than what follows from the above.
Results may differ from the reference program's by a relative error of at most 0.03.
Values may be sent and summed in bfloat16 or wider, within the bound.
No kernel may reach another device: no remote copies, remote signals or barrier semaphores. Data moves between devices by JAX's collectives and lax.ppermute only.
A program may use at most 128 MiB of HBM per device.

```python
import jax
import jax.numpy as jnp
from jax import lax

D = 512
HEADS = 8
WH = 8
WW = 16
SH = 4
SW = 8
W_LON = 16
MICRO = 2
SECTIONS = 2
SAMPLES = 4
NLAT = 32
N_BAND = 4


def draw_qkv_weight(key, part):
    first_key = jax.random.fold_in(key, 0)
    drawn = jax.random.normal(first_key, (SECTIONS, D, 3 * D), jnp.float32) * D ** (-0.5)
    return drawn.astype(jnp.bfloat16)


def set_ends(values, key, low, high):
    index_at = [jax.random.randint(jax.random.fold_in(key, axis), (), 0, length) for axis, length in enumerate(values.shape)]
    main_axis = values.shape.index(max(values.shape))
    next_to = index_at[:main_axis] + [(index_at[main_axis] + 1) % values.shape[main_axis]] + index_at[main_axis + 1:]
    return values.at[tuple(index_at)].set(low).at[tuple(next_to)].set(high)


def levels(key, shape, pieces, least, top_value):
    gain = 1.0
    for axis_at, blocks in pieces:
        heights = jax.random.uniform(jax.random.fold_in(jax.random.fold_in(key, 6), axis_at), (blocks,), jnp.float32, least / len(pieces), top_value / len(pieces))
        gain = gain * jnp.repeat(jnp.exp(heights), shape[axis_at] // blocks).reshape((-1,) + (1,) * (len(shape) - 1 - axis_at))
    return gain


def centred(own_key, extent, scale, reach, shards=(), kind=jnp.bfloat16):
    values = scale * jax.random.normal(own_key, extent, jnp.float32)
    if shards:
        values = values * levels(own_key, extent, shards, -0.22, 0.18)
    return jnp.clip(values, -reach, reach).astype(kind)


def setup_inputs(seed: int = 0) -> dict:
    splits = jax.random.split(jax.random.key(seed), 8)
    fields = centred(splits[0], (SAMPLES, MICRO, NLAT, W_LON, D), 1.0, 6.0, ((0, 4), (2, 4)))
    cell_mask = set_ends((jax.random.randint(splits[1], (SAMPLES, MICRO, NLAT, W_LON), 0, 8) < 7).astype(jnp.int32), jax.random.fold_in(splits[1], 1), 0, 1)
    merge_weight = centred(splits[2], (SECTIONS, 2 * D, D), (2 * D) ** -0.5, 0.1875, ((0, 2), (1, 4)))
    qkv_weight = draw_qkv_weight(jax.random.fold_in(splits[7], 71), 0)
    out_weight = centred(splits[4], (SECTIONS, D, D), (D // 16) ** -0.5, 1.0, ((0, 2), (1, 4)))
    norm_gain = jnp.clip(1.0 + 0.18 * jax.random.normal(splits[5], (SECTIONS, D), jnp.float32), 0.099609375, 1.8984375).astype(jnp.bfloat16)
    out_cotangent = centred(splits[6], (SAMPLES, MICRO, NLAT, W_LON, D), 1.0, 6.0, ((0, 4), (2, 4)))
    return dict(fields=fields, cell_mask=cell_mask, merge_weight=merge_weight, qkv_weight=qkv_weight, out_weight=out_weight, norm_gain=norm_gain, out_cotangent=out_cotangent)


EPSILON = 1e-05
MASKED = -1e+30

def normalize(update):
    average = lax.optimization_barrier(jnp.mean(update, axis=-1, keepdims=True))
    centered = update - average
    spread = lax.optimization_barrier(jnp.mean(centered * centered, axis=-1, keepdims=True))
    inverse = lax.rsqrt(spread + EPSILON)
    return (centered * inverse, inverse)

def window_pattern(lon_count):
    query_index = jnp.arange(WH * lon_count, dtype=jnp.int32)
    key_index = jnp.arange(2 * WH * lon_count, dtype=jnp.int32)
    query_row = query_index // lon_count
    query_col = query_index % lon_count
    key_row = key_index // lon_count
    key_col = key_index % lon_count
    lat_same = ((query_row + SH) // WH)[:, None] == (key_row // WH)[None, :]
    lon_same = ((query_col + SW) // WW)[:, None] == ((key_col + SW) // WW)[None, :]
    self_key = ((query_row + SH)[:, None] == key_row[None, :]) & (query_col[:, None] == key_col[None, :])
    return (lat_same & lon_same, self_key)

def attend(queries, keyvals, usable):
    row_count, lon_count, feature = queries.shape
    blocks = row_count // WH
    head_dim = feature // HEADS
    query_blocks = queries.reshape(blocks, WH * lon_count, HEADS, head_dim).astype(jnp.float32)
    kv_blocks = keyvals.reshape(blocks + 1, WH * lon_count, 2, HEADS, head_dim)
    key_pairs = jnp.concatenate([kv_blocks[:-1], kv_blocks[1:]], axis=1).astype(jnp.float32)
    use_blocks = usable.reshape(blocks + 1, WH * lon_count)
    use_pairs = jnp.concatenate([use_blocks[:-1], use_blocks[1:]], axis=1)
    inside, self_key = window_pattern(lon_count)
    allowed = inside[None] & (use_pairs[:, None, :] | self_key[None])
    scores = jnp.einsum('nqhd,nkhd->nhqk', query_blocks, key_pairs[:, :, 0]) * head_dim ** (-0.5)
    scores = jnp.where(allowed[:, None], scores, MASKED)
    highest = lax.optimization_barrier(jnp.max(scores, axis=-1, keepdims=True))
    weights = jnp.exp(scores - highest)
    attn_prob = (weights / lax.optimization_barrier(jnp.sum(weights, axis=-1, keepdims=True))).astype(jnp.bfloat16)
    mixture = jnp.einsum('nhqk,nkhd->nqhd', attn_prob.astype(jnp.float32), key_pairs[:, :, 1])
    return mixture.reshape(row_count, lon_count, feature).astype(jnp.bfloat16)

def band_terms(left, right):
    left_bands = left.reshape(MICRO, N_BAND, -1, left.shape[-1]).astype(jnp.float32)
    right_bands = right.reshape(MICRO, N_BAND, -1, right.shape[-1]).astype(jnp.float32)
    return jnp.einsum('mbta,mbtc->bac', left_bands, right_bands)

def rounded_sum(partials):
    return lax.optimization_barrier(jnp.sum(lax.optimization_barrier(partials.astype(jnp.bfloat16)).astype(jnp.float32), axis=0))

def reference(fields, cell_mask, merge_weight, qkv_weight, out_weight, norm_gain, out_cotangent):
    sections = merge_weight.shape[0]
    half_count = sections // 2

    def forward_section(index, chain_in, side_in, usable):
        joined = jnp.concatenate([chain_in, side_in], axis=-1)
        update = jnp.dot(joined, merge_weight[index], preferred_element_type=jnp.float32)
        normed, inverse = normalize(update)
        hidden = (normed * norm_gain[index].astype(jnp.float32)).astype(jnp.bfloat16)
        projected = jnp.dot(hidden, qkv_weight[index], preferred_element_type=jnp.float32)
        queries = projected[..., :D].astype(jnp.bfloat16)
        keyvals = projected[..., D:].astype(jnp.bfloat16)
        padded = jnp.pad(keyvals, ((SH, SH), (0, 0), (0, 0)))
        mixture = attend(queries, padded, usable)
        result = (update + jnp.dot(mixture, out_weight[index], preferred_element_type=jnp.float32)).astype(jnp.bfloat16)
        return (result, (joined, normed, inverse, hidden, queries, padded, mixture))

    def backward_section(index, grad_out, record, usable):
        joined, normed, inverse, hidden, queries, padded, mixture = record
        row_total = queries.shape[0]
        grad_mixture = jnp.dot(grad_out, out_weight[index].T, preferred_element_type=jnp.float32).astype(jnp.bfloat16)
        unused, pull_back = jax.vjp(lambda query_in, keyval_in: attend(query_in, keyval_in, usable), queries, padded)
        grad_query, grad_keyval = pull_back(grad_mixture)
        grad_proj = jnp.concatenate([grad_query, grad_keyval[SH:SH + row_total]], axis=-1)
        grad_hidden = jnp.dot(grad_proj, qkv_weight[index].T, preferred_element_type=jnp.float32)
        grad_normed = grad_hidden * norm_gain[index].astype(jnp.float32)
        grad_update = (grad_out.astype(jnp.float32) + inverse * (grad_normed - lax.optimization_barrier(jnp.mean(grad_normed, axis=-1, keepdims=True)) - normed * lax.optimization_barrier(jnp.mean(grad_normed * normed, axis=-1, keepdims=True)))).astype(jnp.bfloat16)
        grad_joined = jnp.dot(grad_update, merge_weight[index].T, preferred_element_type=jnp.float32)
        terms = (joined, grad_update, hidden, grad_proj, mixture, grad_out, grad_hidden, normed)
        return (grad_joined, terms)

    def run_micro(inputs, usable, cotangent):
        outputs = []
        records = []
        for index in range(sections):
            chain_in = inputs if index == 0 else outputs[index - 1]
            side_in = inputs if index < half_count else outputs[sections - 1 - index]
            result, record = forward_section(index, chain_in, side_in, usable)
            outputs.append(result)
            records.append(record)
        flows = [None] * sections
        terms_all = [None] * sections
        for index in range(sections - 1, -1, -1):
            grad_out = cotangent if index == sections - 1 else flows[index].astype(jnp.bfloat16)
            grad_joined, terms = backward_section(index, grad_out, records[index], usable)
            grad_chain = grad_joined[..., :D].astype(jnp.bfloat16).astype(jnp.float32)
            grad_side = grad_joined[..., D:].astype(jnp.bfloat16).astype(jnp.float32)
            if index > 0:
                flows[index - 1] = grad_chain if flows[index - 1] is None else flows[index - 1] + grad_chain
            if index >= half_count:
                target = sections - 1 - index
                flows[target] = grad_side if flows[target] is None else flows[target] + grad_side
            terms_all[index] = terms
        return (jnp.stack(outputs), terms_all)

    def per_sample(totals, sample):
        inputs, mask, cotangent = sample
        usable = jnp.pad(mask == 1, ((0, 0), (SH, SH), (0, 0)))
        section_outs = []
        micro_terms = []
        for micro_no in range(MICRO):
            outputs, terms_all = run_micro(inputs[micro_no], usable[micro_no], cotangent[micro_no])
            section_outs.append(outputs)
            micro_terms.append(terms_all)
        total_merge, total_qkv, total_out, total_gain = totals
        for index in range(sections):
            stacked = [jnp.stack([micro_terms[micro_no][index][position] for micro_no in range(MICRO)]) for position in range(8)]
            total_merge = total_merge.at[index].add(rounded_sum(band_terms(stacked[0], stacked[1])))
            total_qkv = total_qkv.at[index].add(rounded_sum(band_terms(stacked[2], stacked[3])))
            total_out = total_out.at[index].add(rounded_sum(band_terms(stacked[4], stacked[5])))
            gain_parts = lax.optimization_barrier(jnp.sum((stacked[6] * stacked[7]).reshape(MICRO, N_BAND, -1, D), axis=(0, 2)))
            total_gain = total_gain.at[index].add(rounded_sum(gain_parts))
        return ((total_merge, total_qkv, total_out, total_gain), jnp.stack(section_outs, axis=1))
    initial = (jnp.zeros(merge_weight.shape, jnp.float32), jnp.zeros(qkv_weight.shape, jnp.float32), jnp.zeros(out_weight.shape, jnp.float32), jnp.zeros(norm_gain.shape, jnp.float32))
    totals, outputs = lax.scan(per_sample, initial, (fields, cell_mask, out_cotangent))
    section_out = jnp.swapaxes(outputs, 0, 1)
    return (section_out, totals[0], totals[1], totals[2], totals[3])
```

```python
import functools

import jax
import jax.numpy as jnp
from jax import lax
from jax.experimental import pallas as pl
from jax.experimental.pallas import tpu as pltpu
from jax.sharding import PartitionSpec as P

HEADS = 8
WH = 8
WW = 16
SH = 4
SW = 8
PAD = 16

EPSILON = 1e-05
MASKED = -1e30

F32 = jnp.float32
BF16 = jnp.bfloat16


def dot(a, b):
    return lax.dot_general(a, b, (((1,), (0,)), ((), ())), preferred_element_type=F32)


def dot_nt(a, b):
    return lax.dot_general(a, b, (((1,), (1,)), ((), ())), preferred_element_type=F32)


def dot_tn(a, b):
    return lax.dot_general(a, b, (((0,), (0,)), ((), ())), preferred_element_type=F32)


class Copies:
    def __init__(self, sems):
        self.sems = sems
        self.used = 0

    def start(self, src, dst):
        copy = pltpu.make_async_copy(src, dst, self.sems.at[self.used])
        self.used += 1
        copy.start()
        return copy


def wait_all(copies):
    for copy in copies:
        copy.wait()


def layout(feature, shards):
    merge, rows = 2 * feature // shards, feature // shards
    first = {"merge": (0, merge), "q": (merge, rows), "gain": (merge + rows, PAD)}
    second = {"k": (0, rows), "v": (rows, rows), "out": (2 * rows, rows), "pad": (3 * rows, PAD)}
    return (first, second, merge + rows + PAD)


def load_weights(copies, me, pieces, names, dst, feature, shards):
    own, by_low, by_high, both_first, both_second = pieces
    first, second, half = layout(feature, shards)
    started = {}
    for name in names:
        started[name] = []
        for flip, ref in ((0, own), (1, by_low), (shards // 2, by_high), (shards - 1, None)):
            owner = me ^ flip
            base = 0
            if name in first:
                start, rows = first[name]
                source = both_first if ref is None else ref
            else:
                start, rows = second[name]
                source = both_second if ref is None else ref
                base = 0 if ref is None else half
            at = pl.multiple_of(owner * rows, rows)
            started[name].append(
                copies.start(source.at[pl.ds(base + start, rows)], dst[name].at[pl.ds(at, rows)])
            )
    return started


def load_tokens(copies, moved, own, dst):
    started = []
    for m in range(moved.shape[0]):
        part = moved.shape[1]
        size = own.shape[1]
        started.append(copies.start(moved.at[m], dst.at[pl.ds(m * size, part)]))
        started.append(
            copies.start(
                own.at[m, pl.ds(0, size - part)], dst.at[pl.ds(m * size + part, size - part)]
            )
        )
    return started


def full_gain(gain, shards):
    feature = gain.shape[1]
    rows = feature // shards
    parts = [gain[i * PAD : i * PAD + 1, :rows] for i in range(shards)]
    return jnp.concatenate(parts, axis=1).astype(F32)


def window_allowed(mask_row, first_band, lon_count):
    cells = mask_row.shape[1]
    query = lax.broadcasted_iota(jnp.int32, (cells, cells), 0)
    key = lax.broadcasted_iota(jnp.int32, (cells, cells), 1)
    lon_same = (query % lon_count + SW) // WW == (key % lon_count + SW) // WW
    lat_same = (query // lon_count) // SH == (key // lon_count) // SH
    inside = lon_same & (lat_same | jnp.logical_not(first_band))
    usable = jnp.broadcast_to(mask_row, (cells, cells)) == 1
    return inside & (usable | (query == key))


def stacked_heads(pair, head_dim):
    lane = lax.broadcasted_iota(jnp.int32, pair.shape, 1)
    zero = jnp.zeros_like(pair)
    return jnp.concatenate(
        [jnp.where(lane < head_dim, pair, zero), jnp.where(lane < head_dim, zero, pair)], axis=0
    )


def unstacked_heads(stacked, head_dim):
    cells = stacked.shape[0] // 2
    low, high = stacked[:cells], stacked[cells:]
    lane = lax.broadcasted_iota(jnp.int32, low.shape, 1)
    return jnp.where(lane < head_dim, low, high)


def probabilities(q_stack, k, allowed2, head_dim):
    scores = dot_nt(q_stack, k) * head_dim ** (-0.5)
    scores = jnp.where(allowed2, scores, MASKED)
    weights = jnp.exp(scores - jnp.max(scores, axis=-1, keepdims=True))
    return weights / jnp.sum(weights, axis=-1, keepdims=True)


def masks(mask, first_band, lon_count):
    out = []
    for m in range(mask.shape[0]):
        allowed = window_allowed(mask[m : m + 1, :], first_band, lon_count)
        out.append(jnp.concatenate([allowed, allowed], axis=0))
    return out


def pairs(mask_shape, feature):
    micro, cells = mask_shape
    lanes = 2 * (feature // HEADS)
    for m in range(micro):
        for p in range(feature // lanes):
            yield (m, slice(m * cells, (m + 1) * cells), p * lanes, lanes)


def attend(qkv, mix, allowed, mask_shape, feature):
    head_dim = feature // HEADS
    for m, rows, at, lanes in pairs(mask_shape, feature):
        q, k, v = (qkv[rows, i * feature + at : i * feature + at + lanes] for i in range(3))
        probs = probabilities(stacked_heads(q, head_dim), k, allowed[m], head_dim).astype(BF16)
        mixed = unstacked_heads(dot(probs, v), head_dim)
        mix[rows, at : at + lanes] = mixed.astype(BF16)


def attend_back(qkv, grad_mix, grad_proj, allowed, mask_shape, feature):
    head_dim = feature // HEADS
    for m, rows, at, lanes in pairs(mask_shape, feature):
        q, k, v = (qkv[rows, i * feature + at : i * feature + at + lanes] for i in range(3))
        q_stack = stacked_heads(q, head_dim)
        g_stack = stacked_heads(grad_mix[rows, at : at + lanes], head_dim)
        probs = probabilities(q_stack, k, allowed[m], head_dim)
        grad_probs = dot_nt(g_stack, v)
        inner = jnp.sum(grad_probs * probs, axis=-1, keepdims=True)
        grad_scores = (probs * (grad_probs - inner) * head_dim ** (-0.5)).astype(BF16)
        grad_q = unstacked_heads(dot(grad_scores, k), head_dim)
        grad_k = dot_tn(grad_scores, q_stack)
        grad_v = dot_tn(probs.astype(BF16), g_stack)
        for i, grad in enumerate((grad_q, grad_k, grad_v)):
            grad_proj[rows, i * feature + at : i * feature + at + lanes] = grad.astype(BF16)


def normalize(update):
    average = jnp.mean(update, axis=-1, keepdims=True)
    centered = update - average
    spread = jnp.mean(centered * centered, axis=-1, keepdims=True)
    inverse = lax.rsqrt(spread + EPSILON)
    return (centered * inverse, inverse)


def forward(x, w, waits, gain_of, allowed, mask_shape, normed_ref, inverse_ref, hidden, qkv, mix):
    feature = x.shape[1]
    wait_all(waits["merge"])
    tokens = x[...]
    update = dot(tokens, w["merge"][:feature]) + dot(tokens, w["merge"][feature:])
    normed, inverse = normalize(update)
    normed_ref[...] = normed
    inverse_ref[...] = jnp.broadcast_to(inverse, inverse_ref.shape)
    hidden[...] = (normed * gain_of()).astype(BF16)
    for i, name in enumerate(("q", "k", "v")):
        wait_all(waits[name])
        qkv[:, i * feature : (i + 1) * feature] = dot(hidden[...], w[name][...]).astype(BF16)
    attend(qkv, mix, allowed, mask_shape, feature)
    wait_all(waits["out"])
    return update + dot(mix[...], w["out"][...])


def backward(grad_out, w, gain, allowed, mask_shape, normed, inverse, qkv, grad_mix, grad_proj):
    feature = grad_out.shape[1]
    grad_mix[...] = dot_nt(grad_out[...], w["out"][...]).astype(BF16)
    attend_back(qkv, grad_mix, grad_proj, allowed, mask_shape, feature)
    grad_hidden = sum(
        dot_nt(grad_proj[:, i * feature : (i + 1) * feature], w[name][...])
        for i, name in enumerate(("q", "k", "v"))
    )
    normed = normed[...]
    grad_gain = jnp.sum(grad_hidden * normed, axis=0, keepdims=True)
    grad_normed = grad_hidden * gain
    centered = (
        grad_normed
        - jnp.mean(grad_normed, axis=-1, keepdims=True)
        - normed * jnp.mean(grad_normed * normed, axis=-1, keepdims=True)
    )
    grad_update = grad_out[...].astype(F32) + inverse[:, :1] * centered
    return (grad_update.astype(BF16), grad_gain)


def send_grads(copies, me, x, hidden, mix, grad_out, grad_proj, grad_update, grad_gain, dw, outs):
    feature = x.shape[1]
    p_keep, p_send, q_keep, q_send = outs
    shards = 2 * p_keep.shape[0]
    first, second, half = layout(feature, shards)
    low, high = me % 2, me // 2
    rows = feature // shards
    started = []

    def target(name, by_low, by_high):
        if name in first:
            start, size = first[name]
            ref = (p_send if by_high else p_keep).at[by_low]
        else:
            start, size = second[name]
            ref = (q_send if by_low else q_keep).at[by_high]
        return ref.at[pl.ds(start, size)]

    def emit(name, period):
        for by_high in range(2):
            for by_low in range(2):
                owner = (high ^ by_high) * 2 + (low ^ by_low)
                to = target(name, by_low, by_high)
                at = pl.multiple_of((owner * to.shape[0]) % period, to.shape[0])
                started.append(copies.start(dw[name].at[pl.ds(at, to.shape[0])], to))

    dw["out"][...] = dot_tn(mix[...], grad_out[...]).astype(BF16)
    emit("out", feature)
    for i, name in enumerate(("q", "k", "v")):
        part = grad_proj[:, i * feature : (i + 1) * feature]
        dw[name][...] = dot_tn(hidden[...], part).astype(BF16)
        emit(name, feature)
    for i in range(shards):
        part = grad_gain[:, i * rows : (i + 1) * rows].astype(BF16)
        dw["gain"][i * PAD : (i + 1) * PAD, :] = jnp.zeros((PAD, feature), BF16)
        dw["gain"][i * PAD : (i + 1) * PAD, :rows] = jnp.broadcast_to(part, (PAD, rows))
    emit("gain", shards * PAD)
    dw["pad"][...] = jnp.zeros_like(dw["pad"])
    emit("pad", PAD)
    dw["merge"][...] = dot_tn(x[...], grad_update).astype(BF16)
    emit("merge", feature)
    return started


def lon_of(cells):
    return cells // WH


def forward_kernel(place, mask, moved, own, w0, w1, w2, w3, w4, y, normed, inverse, hidden, qkv, mix,
                   x, wm, wq, wk, wv, wo, wg, y_s, normed_s, inverse_s, hidden_s, qkv_s, mix_s, sems):
    shards = wg.shape[0] // PAD
    feature = x.shape[1]

    @pl.when(place[0] == 0)
    def run():
        copies = Copies(sems)
        w = {"merge": wm, "q": wq, "k": wk, "v": wv, "out": wo, "gain": wg}
        tokens = load_tokens(copies, moved, own, x)
        names = ("merge", "gain", "q", "k", "v", "out")
        waits = load_weights(copies, place[1], (w0, w1, w2, w3, w4), names, w, feature, shards)
        allowed = masks(mask, place[2] == 0, lon_of(mask.shape[1]))
        wait_all(tokens)

        def gain_of():
            wait_all(waits["gain"])
            return full_gain(wg, shards)

        result = forward(x, w, waits, gain_of, allowed, mask.shape,
                         normed_s, inverse_s, hidden_s, qkv_s, mix_s)
        y_s[...] = result.astype(BF16)
        done = [
            copies.start(a, b)
            for a, b in ((y_s, y), (normed_s, normed), (inverse_s, inverse), (hidden_s, hidden),
                         (qkv_s, qkv), (mix_s, mix))
        ]
        wait_all(done)


def last_kernel(place, mask, moved, own, y0, w0, w1, w2, w3, w4, y_in, y, g0, pk, ps, qk, qs,
                x, g, wm, wq, wk, wv, wo, wg, y_s, g_s, normed_s, inverse_s, hidden_s, qkv_s, mix_s,
                gmix, gproj, dm, dq, dk, dv, do, dg, dz, sems):
    shards = wg.shape[0] // PAD
    feature = x.shape[1]

    @pl.when(place[0] == 1)
    def run():
        copies = Copies(sems)
        w = {"merge": wm, "q": wq, "k": wk, "v": wv, "out": wo, "gain": wg}
        x_in = copies.start(y0, x)
        names = ("merge", "gain", "q", "k", "v", "out")
        waits = load_weights(copies, place[1], (w0, w1, w2, w3, w4), names, w, feature, shards)
        tokens = load_tokens(copies, moved, own, g)
        allowed = masks(mask, place[2] == 0, lon_of(mask.shape[1]))
        x_in.wait()

        def gain_of():
            wait_all(waits["gain"])
            return full_gain(wg, shards)

        result = forward(x, w, waits, gain_of, allowed, mask.shape,
                         normed_s, inverse_s, hidden_s, qkv_s, mix_s)
        y_s[...] = result.astype(BF16)
        done = [copies.start(y_s, y)]
        wait_all(tokens)
        grad_update, grad_gain = backward(g, w, full_gain(wg, shards), allowed, mask.shape,
                                          normed_s, inverse_s, qkv_s, gmix, gproj)
        chain = dot_nt(grad_update, wm[:feature]).astype(BF16).astype(F32)
        side = dot_nt(grad_update, wm[feature:]).astype(BF16).astype(F32)
        g_s[...] = (chain + side).astype(BF16)
        done.append(copies.start(g_s, g0))
        dw = {"merge": dm, "q": dq, "k": dk, "v": dv, "out": do, "gain": dg, "pad": dz}
        done += send_grads(copies, place[1], x, hidden_s, mix_s, g, gproj, grad_update, grad_gain,
                           dw, (pk, ps, qk, qs))
        wait_all(done)


def first_kernel(place, mask, moved, own, g0, w0, w1, w2, w3, w4, normed, inverse, hidden, qkv, mix,
                 pk_in, ps_in, qk_in, qs_in, pk, ps, qk, qs,
                 x, g, wq, wk, wv, wo, wg, normed_s, inverse_s, hidden_s, qkv_s, mix_s,
                 gmix, gproj, dm, dq, dk, dv, do, dg, dz, sems):
    shards = wg.shape[0] // PAD
    feature = x.shape[1]

    @pl.when(place[0] == 0)
    def run():
        copies = Copies(sems)
        w = {"q": wq, "k": wk, "v": wv, "out": wo, "gain": wg}
        g_in = [copies.start(g0, g)]
        names = ("out", "q", "k", "v", "gain")
        waits = load_weights(copies, place[1], (w0, w1, w2, w3, w4), names, w, feature, shards)
        saved = [
            copies.start(a, b)
            for a, b in ((qkv, qkv_s), (normed, normed_s), (inverse, inverse_s), (hidden, hidden_s),
                         (mix, mix_s))
        ]
        tokens = load_tokens(copies, moved, own, x)
        allowed = masks(mask, place[2] == 0, lon_of(mask.shape[1]))
        wait_all(g_in + saved + tokens)
        for name in names:
            wait_all(waits[name])
        grad_update, grad_gain = backward(g, w, full_gain(wg, shards), allowed, mask.shape,
                                          normed_s, inverse_s, qkv_s, gmix, gproj)
        dw = {"merge": dm, "q": dq, "k": dk, "v": dv, "out": do, "gain": dg, "pad": dz}
        done = send_grads(copies, place[1], x, hidden_s, mix_s, g, gproj, grad_update, grad_gain,
                          dw, (pk, ps, qk, qs))
        wait_all(done)


def final_kernel(place, own, other, merge, qkv, out, gain):
    feature = own.shape[1]
    shards = 2 * feature // merge.shape[1]
    first, second, half = layout(feature, shards)
    even = place[2] % 2 == 0

    def rows(name):
        table, flip = (first, False) if name in first else (second, True)
        start, size = table[name]
        mine, theirs = own[start : start + size, :], other[start : start + size, :]
        a, b = (theirs, mine) if flip else (mine, theirs)
        return jnp.where(even, a.astype(F32), b.astype(F32))

    merge[0] = rows("merge")
    for i, name in enumerate(("q", "k", "v")):
        qkv[0, :, i * feature : (i + 1) * feature] = rows(name)
    out[0] = rows("out")
    gain[...] = rows("gain")[:1, : gain.shape[1]]


ANY = pl.BlockSpec(memory_space=pl.ANY)
SMEM = pl.BlockSpec(memory_space=pltpu.SMEM)
VMEM = pl.BlockSpec(memory_space=pltpu.VMEM)


def call(kernel, ins, outs, scratch, aliases, flops, name):
    moved = sum(a.size * a.dtype.itemsize for a in list(ins) + list(outs))
    return pl.pallas_call(
        kernel,
        out_shape=tuple(outs),
        in_specs=[SMEM, VMEM] + [ANY] * (len(ins) - 2),
        out_specs=tuple([ANY] * len(outs)),
        scratch_shapes=scratch,
        input_output_aliases=aliases,
        cost_estimate=pl.CostEstimate(flops=flops, bytes_accessed=moved, transcendentals=0),
        name=name,
    )(*ins)


def flip(value, axis, bit):
    size = lax.axis_size(axis)
    return lax.ppermute(value, axis, [(i, i ^ bit) for i in range(size)])


def body(fields, cell_mask, merge_weight, qkv_weight, out_weight, norm_gain, out_cotangent):
    _, micro, row_count, lon_count, feature = fields.shape
    shards, bands = lax.axis_size("dp"), lax.axis_size("band")
    assert lax.axis_size("segment") == 2 and row_count == WH and shards == 4
    segment, shard, band = (lax.axis_index(a) for a in ("segment", "dp", "band"))
    place = jnp.stack([segment, shard, band]).astype(jnp.int32)
    cells = row_count * lon_count
    total = micro * cells
    first, second, half = layout(feature, shards)
    rows = feature // shards

    qkv = qkv_weight[0]
    gain_rows = jnp.pad(norm_gain, ((0, PAD - 1), (0, feature - rows)))
    packed = jnp.concatenate(
        [
            merge_weight[0],
            qkv[:, :feature],
            gain_rows,
            qkv[:, feature : 2 * feature],
            qkv[:, 2 * feature :],
            out_weight[0],
            jnp.zeros((PAD, feature), BF16),
        ],
        axis=0,
    )
    by_low = flip(packed, "dp", 1)
    by_high = flip(packed, "dp", shards // 2)
    both_first = flip(by_low[:half], "dp", shards // 2)
    both_second = flip(by_high[half:], "dp", 1)
    pieces = (packed, by_low, by_high, both_first, both_second)

    down = [(i, (i + 1) % bands) for i in range(bands)]
    up = [(j, i) for i, j in down]
    flat = (micro, cells, feature)
    source = jnp.where(segment == 0, fields[0, :, row_count - SH :], out_cotangent[0, :, row_count - SH :])
    moved = lax.ppermute(source, "band", down).reshape(micro, SH * lon_count, feature)
    mask_moved = lax.ppermute(cell_mask[0, :, row_count - SH :], "band", down)
    mask = jnp.concatenate([mask_moved, cell_mask[0, :, : row_count - SH]], axis=1).reshape(micro, cells)
    own_fields = fields.reshape(flat)
    own_cotangent = out_cotangent.reshape(flat)

    def shape(*dims, dtype=BF16):
        return jax.ShapeDtypeStruct(dims, dtype)

    def room(*dims, dtype=BF16):
        return pltpu.VMEM(dims, dtype)

    square = room(feature, feature)
    tokens = room(total, feature)
    weights = [square] * 4 + [room(shards * PAD, feature)]
    merge_room = room(2 * feature, feature)
    record_rooms = [
        room(total, feature, dtype=F32), room(total, 128, dtype=F32), tokens,
        room(total, 3 * feature), tokens,
    ]
    grad_rooms = [tokens, room(total, 3 * feature)] + [square] * 5 + [room(shards * PAD, feature), room(PAD, feature)]
    sems = [pltpu.SemaphoreType.DMA((96,))]
    unit = 2 * total * feature * feature

    y, *records = call(
        forward_kernel,
        (place, mask, moved, own_fields) + pieces,
        [shape(total, feature), shape(total, feature, dtype=F32), shape(total, 128, dtype=F32),
         shape(total, feature), shape(total, 3 * feature), shape(total, feature)],
        [tokens, merge_room] + weights + [tokens] + record_rooms + sems,
        {}, 6 * unit, "fwd_first",
    )
    y0 = lax.ppermute(y, "segment", [(0, 1)])
    shard_shape = shape(2, half, feature)
    y, g_out, *grads = call(
        last_kernel,
        (place, mask, moved, own_cotangent, y0) + pieces + (y,),
        [shape(total, feature), shape(total, feature)] + [shard_shape] * 4,
        [tokens, tokens, merge_room] + weights + [tokens, tokens] + record_rooms + grad_rooms + sems,
        {10: 0}, 18 * unit, "last_section",
    )
    g0 = lax.ppermute(g_out, "segment", [(1, 0)])
    inputs = (place, mask, moved, own_fields, g0) + pieces + tuple(records)
    grads = call(
        first_kernel,
        inputs + tuple(grads),
        [shard_shape] * 4,
        [tokens, tokens] + weights + record_rooms + grad_rooms + sems,
        {len(inputs) + i: i for i in range(4)}, 12 * unit, "bwd_first",
    )

    y = y.reshape(micro, cells, feature)
    part = SH * lon_count
    back = lax.ppermute(y[:, :part], "band", up)
    section_out = jnp.concatenate([y[:, part:], back], axis=1)
    section_out = section_out.reshape(1, 1, micro, row_count, lon_count, feature)

    p_keep, p_send, q_keep, q_send = grads
    high = shards // 2
    p_sum = p_keep.astype(F32) + flip(p_send, "dp", high).astype(F32)
    q_sum = q_keep.astype(F32) + flip(q_send, "dp", 1).astype(F32)
    p_sum = p_sum[0] + flip(p_sum[1].astype(BF16), "dp", 1).astype(F32)
    q_sum = q_sum[0] + flip(q_sum[1].astype(BF16), "dp", high).astype(F32)

    even = band % 2 == 0
    mine = jnp.where(even, p_sum, q_sum)
    theirs = jnp.where(even, q_sum, p_sum).astype(BF16)
    mine = (mine + flip(theirs, "band", 1).astype(F32)).astype(BF16)
    bit = 2
    while bit < bands:
        mine = (mine.astype(F32) + flip(mine, "band", bit).astype(F32)).astype(BF16)
        bit *= 2
    theirs = flip(mine, "band", 1)
    merge_grad, qkv_grad, out_grad, gain_grad = pl.pallas_call(
        final_kernel,
        out_shape=(
            shape(1, 2 * rows, feature, dtype=F32), shape(1, rows, 3 * feature, dtype=F32),
            shape(1, rows, feature, dtype=F32), shape(1, rows, dtype=F32),
        ),
        in_specs=[SMEM, VMEM, VMEM],
        out_specs=(VMEM,) * 4,
        name="unpack",
    )(place, mine, theirs)
    return (section_out, merge_grad, qkv_grad, out_grad, gain_grad)


def solution(mesh):
    return jax.shard_map(
        body,
        mesh=mesh,
        in_specs=(
            P("dp", None, "band", None, None),
            P("dp", None, "band", None),
            P("segment", "dp", None),
            P("segment", "dp", None),
            P("segment", "dp", None),
            P("segment", "dp"),
            P("dp", None, "band", None, None),
        ),
        out_specs=(
            P("segment", "dp", None, "band", None, None),
            P("segment", "dp", None),
            P("segment", "dp", None),
            P("segment", "dp", None),
            P("segment", "dp"),
        ),
        check_vma=False,
    )
```

```python
import jax
import jax.numpy as jnp
from jax import lax
from jax.experimental import pallas as pl
from jax.experimental.pallas import tpu as pltpu
from jax.sharding import PartitionSpec as P


HEADS = 8
WH = 8
WW = 16
SH = 4
SW = 8
PAD = 16

EPSILON = 1e-05
MASKED = -1e30


F32 = jnp.float32
BF16 = jnp.bfloat16


def dot(a, b):
    return lax.dot_general(a, b, (((1,), (0,)), ((), ())), preferred_element_type=F32)


def dot_nt(a, b):
    return lax.dot_general(a, b, (((1,), (1,)), ((), ())), preferred_element_type=F32)


def dot_tn(a, b):
    return lax.dot_general(a, b, (((0,), (0,)), ((), ())), preferred_element_type=F32)


class Copies:
    def __init__(self, sems):
        self.sems = sems
        self.used = 0

    def start(self, src, dst):
        copy = pltpu.make_async_copy(src, dst, self.sems.at[self.used])
        self.used += 1
        copy.start()
        return copy


def wait_all(copies):
    for copy in copies:
        copy.wait()


def layout(feature, shards):
    merge, rows = 2 * feature // shards, feature // shards
    first = {"merge": (0, merge), "q": (merge, rows), "gain": (merge + rows, PAD)}
    second = {"k": (0, rows), "v": (rows, rows), "out": (2 * rows, rows), "pad": (3 * rows, PAD)}
    return (first, second, merge + rows + PAD)


def load_weights(copies, pieces, names, dst):
    me = lax.axis_index("dp")
    shards = 4
    started = {}
    for name in names:
        kind, column = WHERE[name]
        arrays = pieces[kind]
        started[name] = []
        for flip, ref in zip((0, 1, shards // 2, shards - 1), arrays):
            rows = dst[name].shape[0] // shards
            at = pl.multiple_of((me ^ flip) * rows, rows)
            if kind == "rest":
                base = 0 if name == "out" else ref.shape[0] - PAD
                source = ref.at[pl.ds(base, rows)]
            elif kind == "qkv":
                width = dst[name].shape[1]
                source = ref.at[:, pl.ds(column * width, width)]
            else:
                source = ref
            started[name].append(copies.start(source, dst[name].at[pl.ds(at, rows)]))
    return started


WHERE = {
    "merge": ("merge", 0), "q": ("qkv", 0), "k": ("qkv", 1), "v": ("qkv", 2),
    "out": ("rest", 0), "gain": ("rest", 1),
}


def pieces_of(refs):
    return {"merge": refs[0:4], "qkv": refs[4:8], "rest": refs[8:12]}


def load_tokens(copies, moved, own, dst):
    started = []
    for m in range(moved.shape[0]):
        part = moved.shape[1]
        size = own.shape[1]
        started.append(copies.start(moved.at[m], dst.at[pl.ds(m * size, part)]))
        started.append(
            copies.start(
                own.at[m, pl.ds(0, size - part)], dst.at[pl.ds(m * size + part, size - part)]
            )
        )
    return started


def full_gain(gain, shards):
    feature = gain.shape[1]
    rows = feature // shards
    parts = [gain[i * PAD : i * PAD + 1, :rows] for i in range(shards)]
    return jnp.concatenate(parts, axis=1).astype(F32)


def window_allowed(mask_row, first_band, lon_count):
    cells = mask_row.shape[1]
    query = lax.broadcasted_iota(jnp.int32, (cells, cells), 0)
    key = lax.broadcasted_iota(jnp.int32, (cells, cells), 1)
    lon_same = (query % lon_count + SW) // WW == (key % lon_count + SW) // WW
    lat_same = (query // lon_count) // SH == (key // lon_count) // SH
    inside = lon_same & (lat_same | jnp.logical_not(first_band))
    usable = jnp.broadcast_to(mask_row, (cells, cells)) == 1
    return inside & (usable | (query == key))


def stacked_heads(pair, head_dim):
    lane = lax.broadcasted_iota(jnp.int32, pair.shape, 1)
    zero = jnp.zeros_like(pair)
    return jnp.concatenate(
        [jnp.where(lane < head_dim, pair, zero), jnp.where(lane < head_dim, zero, pair)], axis=0
    )


def unstacked_heads(stacked, head_dim):
    cells = stacked.shape[0] // 2
    low, high = stacked[:cells], stacked[cells:]
    lane = lax.broadcasted_iota(jnp.int32, low.shape, 1)
    return jnp.where(lane < head_dim, low, high)


def probabilities(q_stack, k, allowed2, head_dim):
    scores = dot_nt(q_stack, k) * head_dim ** (-0.5)
    scores = jnp.where(allowed2, scores, MASKED)
    weights = jnp.exp(scores - jnp.max(scores, axis=-1, keepdims=True))
    return weights / jnp.sum(weights, axis=-1, keepdims=True)


def masks(mask, first_band, lon_count):
    out = []
    for m in range(mask.shape[0]):
        allowed = window_allowed(mask[m : m + 1, :], first_band, lon_count)
        out.append(jnp.concatenate([allowed, allowed], axis=0))
    return out


def pairs(mask_shape, feature):
    micro, cells = mask_shape
    lanes = 2 * (feature // HEADS)
    for m in range(micro):
        for p in range(feature // lanes):
            yield (m, slice(m * cells, (m + 1) * cells), p * lanes, lanes)


def attend(qkv, mix, allowed, mask_shape, feature):
    head_dim = feature // HEADS
    for m, rows, at, lanes in pairs(mask_shape, feature):
        q, k, v = (qkv[rows, i * feature + at : i * feature + at + lanes] for i in range(3))
        probs = probabilities(stacked_heads(q, head_dim), k, allowed[m], head_dim).astype(BF16)
        mixed = unstacked_heads(dot(probs, v), head_dim)
        mix[rows, at : at + lanes] = mixed.astype(BF16)


def attend_back(qkv, grad_mix, grad_proj, allowed, mask_shape, feature):
    head_dim = feature // HEADS
    for m, rows, at, lanes in pairs(mask_shape, feature):
        q, k, v = (qkv[rows, i * feature + at : i * feature + at + lanes] for i in range(3))
        q_stack = stacked_heads(q, head_dim)
        g_stack = stacked_heads(grad_mix[rows, at : at + lanes], head_dim)
        probs = probabilities(q_stack, k, allowed[m], head_dim)
        grad_probs = dot_nt(g_stack, v)
        inner = jnp.sum(grad_probs * probs, axis=-1, keepdims=True)
        grad_scores = (probs * (grad_probs - inner) * head_dim ** (-0.5)).astype(BF16)
        grad_q = unstacked_heads(dot(grad_scores, k), head_dim)
        grad_k = dot_tn(grad_scores, q_stack)
        grad_v = dot_tn(probs.astype(BF16), g_stack)
        for i, grad in enumerate((grad_q, grad_k, grad_v)):
            grad_proj[rows, i * feature + at : i * feature + at + lanes] = grad.astype(BF16)


def normalize(update):
    average = jnp.mean(update, axis=-1, keepdims=True)
    centered = update - average
    spread = jnp.mean(centered * centered, axis=-1, keepdims=True)
    inverse = lax.rsqrt(spread + EPSILON)
    return (centered * inverse, inverse)


def forward(x, w, waits, gain_of, allowed, mask_shape, normed_ref, inverse_ref, hidden, qkv, mix):
    feature = x.shape[1]
    wait_all(waits["merge"])
    tokens = x[...]
    update = dot(tokens, w["merge"][:feature]) + dot(tokens, w["merge"][feature:])
    normed, inverse = normalize(update)
    normed_ref[...] = normed
    inverse_ref[...] = jnp.broadcast_to(inverse, inverse_ref.shape)
    hidden[...] = (normed * gain_of()).astype(BF16)
    for i, name in enumerate(("q", "k", "v")):
        wait_all(waits[name])
        qkv[:, i * feature : (i + 1) * feature] = dot(hidden[...], w[name][...]).astype(BF16)
    attend(qkv, mix, allowed, mask_shape, feature)
    wait_all(waits["out"])
    return update + dot(mix[...], w["out"][...])


def backward(grad_out, w, gain, allowed, mask_shape, normed, inverse, qkv, grad_mix, grad_proj):
    feature = grad_out.shape[1]
    grad_mix[...] = dot_nt(grad_out[...], w["out"][...]).astype(BF16)
    attend_back(qkv, grad_mix, grad_proj, allowed, mask_shape, feature)
    grad_hidden = sum(
        dot_nt(grad_proj[:, i * feature : (i + 1) * feature], w[name][...])
        for i, name in enumerate(("q", "k", "v"))
    )
    normed = normed[...]
    grad_gain = jnp.sum(grad_hidden * normed, axis=0, keepdims=True)
    grad_normed = grad_hidden * gain
    centered = (
        grad_normed
        - jnp.mean(grad_normed, axis=-1, keepdims=True)
        - normed * jnp.mean(grad_normed * normed, axis=-1, keepdims=True)
    )
    grad_update = grad_out[...].astype(F32) + inverse[:, :1] * centered
    return (grad_update.astype(BF16), grad_gain)


def send_grads(copies, x, hidden, mix, grad_out, grad_proj, grad_update, grad_gain, dw, outs):
    feature = x.shape[1]
    p_keep, p_send, q_keep, q_send = outs
    shards = 2 * p_keep.shape[0]
    first, second, _ = layout(feature, shards)
    me = lax.axis_index("dp")
    low, high = me % 2, me // 2
    rows = feature // shards
    started = []

    def target(name, by_low, by_high):
        if name in first:
            start, size = first[name]
            ref = (p_send if by_high else p_keep).at[by_low]
        else:
            start, size = second[name]
            ref = (q_send if by_low else q_keep).at[by_high]
        return ref.at[pl.ds(start, size)]

    def emit(name, period):
        for by_high in range(2):
            for by_low in range(2):
                owner = (high ^ by_high) * 2 + (low ^ by_low)
                to = target(name, by_low, by_high)
                at = pl.multiple_of((owner * to.shape[0]) % period, to.shape[0])
                started.append(copies.start(dw[name].at[pl.ds(at, to.shape[0])], to))

    dw["out"][...] = dot_tn(mix[...], grad_out[...]).astype(BF16)
    emit("out", feature)
    for i, name in enumerate(("q", "k", "v")):
        part = grad_proj[:, i * feature : (i + 1) * feature]
        dw[name][...] = dot_tn(hidden[...], part).astype(BF16)
        emit(name, feature)
    for i in range(shards):
        part = grad_gain[:, i * rows : (i + 1) * rows].astype(BF16)
        dw["gain"][i * PAD : (i + 1) * PAD, :] = jnp.zeros((PAD, feature), BF16)
        dw["gain"][i * PAD : (i + 1) * PAD, :rows] = jnp.broadcast_to(part, (PAD, rows))
    emit("gain", shards * PAD)
    dw["pad"][...] = jnp.zeros_like(dw["pad"])
    emit("pad", PAD)
    dw["merge"][...] = dot_tn(x[...], grad_update[...]).astype(BF16)
    emit("merge", feature)
    return started


def lon_of(cells):
    return cells // WH


def role(segment):
    return pl.when(lax.axis_index("segment") == segment)


def forward_kernel(*refs):
    mask_in, moved, own, *rest = refs
    pieces, rest = rest[:12], rest[12:]
    y, normed, inverse, hidden, qkv, mix, *rest = rest
    mask, x, wm, wq, wk, wv, wo, wg, y_s, normed_s, inverse_s, hidden_s, qkv_s, mix_s, sems = rest

    @role(0)
    def run():
        shards = wg.shape[0] // PAD
        copies = Copies(sems)
        w = {"merge": wm, "q": wq, "k": wk, "v": wv, "out": wo, "gain": wg}
        mask_copy = copies.start(mask_in, mask)
        tokens = load_tokens(copies, moved, own, x)
        names = ("merge", "gain", "q", "k", "v", "out")
        waits = load_weights(copies, pieces_of(pieces), names, w)
        mask_copy.wait()
        allowed = masks(mask, lax.axis_index("band") == 0, lon_of(mask.shape[1]))
        wait_all(tokens)

        def gain_of():
            wait_all(waits["gain"])
            return full_gain(wg, shards)

        result = forward(x, w, waits, gain_of, allowed, mask.shape,
                         normed_s, inverse_s, hidden_s, qkv_s, mix_s)
        y_s[...] = result.astype(BF16)
        done = [
            copies.start(a, b)
            for a, b in ((y_s, y), (normed_s, normed), (inverse_s, inverse), (hidden_s, hidden),
                         (qkv_s, qkv), (mix_s, mix))
        ]
        wait_all(done)


def last_kernel(*refs):
    mask_in, moved, own, y0, *rest = refs
    pieces, rest = rest[:12], rest[14:]
    y, g0, gain_out, g_out, hidden, mix, proj_out, update_out, *rest = rest
    (mask, x, g, wm, wq, wk, wv, wo, wg, y_s, g_s, normed_s, inverse_s, hidden_s, qkv_s, mix_s,
     gmix, gproj, gain_s, update_s, sems) = rest

    @role(1)
    def run():
        shards = wg.shape[0] // PAD
        feature = x.shape[1]
        copies = Copies(sems)
        w = {"merge": wm, "q": wq, "k": wk, "v": wv, "out": wo, "gain": wg}
        mask_copy = copies.start(mask_in, mask)
        x_in = copies.start(y0, x)
        names = ("merge", "gain", "q", "k", "v", "out")
        waits = load_weights(copies, pieces_of(pieces), names, w)
        tokens = load_tokens(copies, moved, own, g)
        mask_copy.wait()
        allowed = masks(mask, lax.axis_index("band") == 0, lon_of(mask.shape[1]))
        x_in.wait()

        def gain_of():
            wait_all(waits["gain"])
            return full_gain(wg, shards)

        result = forward(x, w, waits, gain_of, allowed, mask.shape,
                         normed_s, inverse_s, hidden_s, qkv_s, mix_s)
        y_s[...] = result.astype(BF16)
        wait_all(tokens)
        done = [copies.start(y_s, y), copies.start(g, g_out), copies.start(hidden_s, hidden),
                copies.start(mix_s, mix)]
        grad_update, grad_gain = backward(g, w, full_gain(wg, shards), allowed, mask.shape,
                                          normed_s, inverse_s, qkv_s, gmix, gproj)
        done.append(copies.start(gproj, proj_out))
        gain_s[...] = jnp.broadcast_to(grad_gain, gain_s.shape)
        update_s[...] = grad_update
        done += [copies.start(gain_s, gain_out), copies.start(update_s, update_out)]
        chain = dot_nt(grad_update, wm[:feature]).astype(BF16).astype(F32)
        side = dot_nt(grad_update, wm[feature:]).astype(BF16).astype(F32)
        g_s[...] = (chain + side).astype(BF16)
        done.append(copies.start(g_s, g0))
        wait_all(done)


def weight_kernel(*refs):
    ins, outs, rest = refs[:7], refs[7:11], refs[11:]
    scratch, dw_refs, sems = rest[:7], rest[7:14], rest[14]

    @role(1)
    def run():
        copies = Copies(sems)
        wait_all([copies.start(a, b) for a, b in zip(ins, scratch)])
        x, gain, g, hidden, mix, gproj, update = scratch
        dw = dict(zip(("merge", "q", "k", "v", "out", "gain", "pad"), dw_refs))
        wait_all(send_grads(copies, x, hidden, mix, g, gproj, update, gain[:1, :], dw, outs))


def first_kernel(*refs):
    mask_in, moved, own, g0, *rest = refs
    pieces, rest = rest[:12], rest[12:]
    normed, inverse, hidden, qkv, mix, *rest = rest
    outs, rest = rest[5:9], rest[9:]
    (mask, x, g, wq, wk, wv, wo, wg, normed_s, inverse_s, hidden_s, qkv_s, mix_s,
     gmix, gproj, *dw_refs, sems) = rest

    @role(0)
    def run():
        shards = wg.shape[0] // PAD
        copies = Copies(sems)
        w = {"q": wq, "k": wk, "v": wv, "out": wo, "gain": wg}
        mask_copy = copies.start(mask_in, mask)
        g_in = [copies.start(g0, g)]
        names = ("out", "q", "k", "v", "gain")
        waits = load_weights(copies, pieces_of(pieces), names, w)
        saved = [
            copies.start(a, b)
            for a, b in ((qkv, qkv_s), (normed, normed_s), (inverse, inverse_s), (hidden, hidden_s),
                         (mix, mix_s))
        ]
        tokens = load_tokens(copies, moved, own, x)
        mask_copy.wait()
        allowed = masks(mask, lax.axis_index("band") == 0, lon_of(mask.shape[1]))
        wait_all(g_in + saved + tokens)
        for name in names:
            wait_all(waits[name])
        grad_update, grad_gain = backward(g, w, full_gain(wg, shards), allowed, mask.shape,
                                          normed_s, inverse_s, qkv_s, gmix, gproj)
        dw = dict(zip(("merge", "q", "k", "v", "out", "gain", "pad"), dw_refs))
        wait_all(send_grads(copies, x, hidden_s, mix_s, g, gproj, grad_update, grad_gain, dw, outs))


def rest_kernel(out, gain, packed):
    rows, width = gain.shape[1], out.shape[1]
    packed[: out.shape[0], :] = out[...]
    packed[out.shape[0] :, :] = jnp.zeros((PAD, width), BF16)
    packed[out.shape[0] :, :rows] = jnp.broadcast_to(gain[...], (PAD, rows))


def final_kernel(own, other, merge, qkv, out, gain):
    feature = own.shape[1]
    shards = 2 * feature // merge.shape[1]
    first, second, _ = layout(feature, shards)
    even = lax.axis_index("band") % 2 == 0

    def rows(name):
        table, flip = (first, False) if name in first else (second, True)
        start, size = table[name]
        mine, theirs = own[start : start + size, :], other[start : start + size, :]
        a, b = (theirs, mine) if flip else (mine, theirs)
        return jnp.where(even, a.astype(F32), b.astype(F32))

    merge[0] = rows("merge")
    for i, name in enumerate(("q", "k", "v")):
        qkv[0, :, i * feature : (i + 1) * feature] = rows(name)
    out[0] = rows("out")
    gain[...] = rows("gain")[:1, : gain.shape[1]]


ANY = pl.BlockSpec(memory_space=pl.ANY)
VMEM = pl.BlockSpec(memory_space=pltpu.VMEM)


def call(kernel, ins, outs, scratch, aliases, flops):
    moved = sum(a.size * a.dtype.itemsize for a in list(ins) + list(outs))
    return pl.pallas_call(
        kernel,
        out_shape=tuple(outs),
        in_specs=[ANY] * len(ins),
        out_specs=tuple([ANY] * len(outs)),
        scratch_shapes=scratch,
        input_output_aliases=aliases,
        cost_estimate=pl.CostEstimate(flops=flops, bytes_accessed=moved, transcendentals=0),
    )(*ins)


def flip(value, axis, bit):
    size = lax.axis_size(axis)
    return lax.ppermute(value, axis, [(i, i ^ bit) for i in range(size)])


def flip_on(value, bit, segment):
    shards, segments = lax.axis_size("dp"), lax.axis_size("segment")
    pairs = [(i * segments + segment, (i ^ bit) * segments + segment) for i in range(shards)]
    return lax.ppermute(value, ("dp", "segment"), pairs)


def gather(merge, qkv, rest, segment):
    high = lax.axis_size("dp") // 2
    merge_low = flip_on(merge, 1, segment)
    merge_high = flip_on(merge, high, segment)
    qkv_low = flip_on(qkv, 1, segment)
    qkv_high = flip_on(qkv, high, segment)
    rest_low = flip_on(rest, 1, segment)
    rest_high = flip_on(rest, high, segment)
    merge_both = flip_on(merge_low, high, segment)
    qkv_both = flip_on(qkv_high, 1, segment)
    rest_both = flip_on(rest_low, high, segment)
    return (merge, merge_low, merge_high, merge_both, qkv, qkv_low, qkv_high, qkv_both,
            rest, rest_low, rest_high, rest_both)


def body(fields, cell_mask, merge_weight, qkv_weight, out_weight, norm_gain, out_cotangent):
    _, micro, row_count, lon_count, feature = fields.shape
    shards, bands = lax.axis_size("dp"), lax.axis_size("band")
    assert lax.axis_size("segment") == 2 and row_count == WH and shards == 4
    segment, band = lax.axis_index("segment"), lax.axis_index("band")
    cells = row_count * lon_count
    total = micro * cells
    _, _, half = layout(feature, shards)
    rows = feature // shards

    def shape(*dims, dtype=BF16):
        return jax.ShapeDtypeStruct(dims, dtype)

    def room(*dims, dtype=BF16):
        return pltpu.VMEM(dims, dtype)

    merge, qkv, out = merge_weight[0], qkv_weight[0], out_weight[0]
    rest = pl.pallas_call(
        rest_kernel,
        out_shape=shape(rows + PAD, feature),
        in_specs=[VMEM, VMEM],
        out_specs=VMEM,
        name="pack",
    )(out, norm_gain)
    pieces0 = gather(merge, qkv, rest, 0)
    token = pieces0[5][:PAD, :128] + pieces0[6][:PAD, :128]
    token = lax.ppermute(token, "segment", [(0, 1)])
    pieces1 = gather(merge, qkv, rest, 1)

    down = [(i, (i + 1) % bands) for i in range(bands)]
    up = [(j, i) for i, j in down]
    flat = (micro, cells, feature)
    source = jnp.where(segment == 0, fields[0, :, row_count - SH :], out_cotangent[0, :, row_count - SH :])
    moved = lax.ppermute(source, "band", down)
    moved = moved.reshape(micro, SH * lon_count, feature)
    mask_moved = lax.ppermute(cell_mask[0, :, row_count - SH :], "band", down)
    mask = jnp.concatenate([mask_moved, cell_mask[0, :, : row_count - SH]], axis=1).reshape(micro, cells)
    own_fields = fields.reshape(flat)
    own_cotangent = out_cotangent.reshape(flat)

    square = room(feature, feature)
    tokens = room(total, feature)
    wide = room(total, 3 * feature)
    mask_room = pltpu.VMEM((micro, cells), jnp.int32)
    weights = [square] * 4 + [room(shards * PAD, feature)]
    merge_room = room(2 * feature, feature)
    record_rooms = [
        room(total, feature, dtype=F32), room(total, 128, dtype=F32), tokens, wide, tokens,
    ]
    grad_rooms = [square] * 5 + [room(shards * PAD, feature), room(PAD, feature)]
    sems = [pltpu.SemaphoreType.DMA((96,))]
    unit = 2 * total * feature * feature
    token_shape, wide_shape = shape(total, feature), shape(total, 3 * feature)

    y, *records = call(
        forward_kernel,
        (mask, moved, own_fields) + pieces0,
        [token_shape, shape(total, feature, dtype=F32), shape(total, 128, dtype=F32),
         token_shape, wide_shape, token_shape],
        [mask_room, tokens, merge_room] + weights + [tokens] + record_rooms + sems,
        {}, 6 * unit,
    )
    y0 = lax.ppermute(y, "segment", [(0, 1)])
    gain_room = room(8, feature, dtype=F32)
    y, g_out, *operands = call(
        last_kernel,
        (mask, moved, own_cotangent, y0) + pieces1 + (token, y),
        [token_shape, token_shape, shape(8, feature, dtype=F32), token_shape, token_shape, token_shape,
         wide_shape, token_shape],
        [mask_room, tokens, tokens, merge_room] + weights + [tokens, tokens] + record_rooms
        + [tokens, wide, gain_room, tokens] + sems,
        {17: 0}, 13 * unit,
    )
    g0 = lax.ppermute(g_out, "segment", [(1, 0)])
    shard_shape = shape(2, half, feature)
    grads = call(
        weight_kernel,
        (y0,) + tuple(operands),
        [shard_shape] * 4,
        [tokens, gain_room, tokens, tokens, tokens, wide, tokens] + grad_rooms + sems,
        {}, 5 * unit,
    )

    y = y.reshape(micro, cells, feature)
    part = SH * lon_count
    back = lax.ppermute(y[:, :part], "band", up)
    section_out = jnp.concatenate([y[:, part:], back], axis=1)
    section_out = section_out.reshape(1, 1, micro, row_count, lon_count, feature)

    inputs = (mask, moved, own_fields, g0) + pieces0 + tuple(records) + (section_out,)
    grads = call(
        first_kernel,
        inputs + tuple(grads),
        [shard_shape] * 4,
        [mask_room, tokens, tokens] + weights + record_rooms + [tokens, wide] + grad_rooms + sems,
        {len(inputs) + i: i for i in range(4)}, 12 * unit,
    )

    p_keep, p_send, q_keep, q_send = grads
    high = shards // 2
    p_sum = p_keep.astype(F32) + flip(p_send, "dp", high).astype(F32)
    q_sum = q_keep.astype(F32) + flip(q_send, "dp", 1).astype(F32)
    p_sum = p_sum[0] + flip(p_sum[1].astype(BF16), "dp", 1).astype(F32)
    q_sum = q_sum[0] + flip(q_sum[1].astype(BF16), "dp", high).astype(F32)

    even = band % 2 == 0
    mine = jnp.where(even, p_sum, q_sum)
    theirs = jnp.where(even, q_sum, p_sum).astype(BF16)
    mine = (mine + flip(theirs, "band", 1).astype(F32)).astype(BF16)
    bit = 2
    while bit < bands:
        mine = (mine.astype(F32) + flip(mine, "band", bit).astype(F32)).astype(BF16)
        bit *= 2
    theirs = flip(mine, "band", 1)
    merge_grad, qkv_grad, out_grad, gain_grad = pl.pallas_call(
        final_kernel,
        out_shape=(
            shape(1, 2 * rows, feature, dtype=F32), shape(1, rows, 3 * feature, dtype=F32),
            shape(1, rows, feature, dtype=F32), shape(1, rows, dtype=F32),
        ),
        in_specs=[VMEM, VMEM],
        out_specs=(VMEM,) * 4,
        name="unpack",
    )(mine, theirs)
    return (section_out, merge_grad, qkv_grad, out_grad, gain_grad)


def solution(mesh):
    return jax.shard_map(
        body,
        mesh=mesh,
        in_specs=(
            P("dp", None, "band", None, None),
            P("dp", None, "band", None),
            P("segment", "dp", None),
            P("segment", "dp", None),
            P("segment", "dp", None),
            P("segment", "dp"),
            P("dp", None, "band", None, None),
        ),
        out_specs=(
            P("segment", "dp", None, "band", None, None),
            P("segment", "dp", None),
            P("segment", "dp", None),
            P("segment", "dp", None),
            P("segment", "dp"),
        ),
        check_vma=False,
    )
```

```python
import jax
import jax.numpy as jnp
from jax import lax
from jax.experimental import pallas as pl
from jax.experimental.pallas import tpu as pltpu
from jax.sharding import PartitionSpec as P


HEADS = 8
WH = 8
WW = 16
SH = 4
SW = 8
PAD = 16
CHUNKS = 2

EPSILON = 1e-05
MASKED = -1e30


F32 = jnp.float32
BF16 = jnp.bfloat16


def dot(a, b):
    return lax.dot_general(a, b, (((1,), (0,)), ((), ())), preferred_element_type=F32)


def dot_nt(a, b):
    return lax.dot_general(a, b, (((1,), (1,)), ((), ())), preferred_element_type=F32)


def dot_tn(a, b):
    return lax.dot_general(a, b, (((0,), (0,)), ((), ())), preferred_element_type=F32)


class Copies:
    def __init__(self, sems):
        self.sems = sems
        self.used = 0

    def start(self, src, dst):
        copy = pltpu.make_async_copy(src, dst, self.sems.at[self.used])
        self.used += 1
        copy.start()
        return copy


def wait_all(copies):
    for copy in copies:
        copy.wait()


def layout(feature, shards):
    merge, rows = 2 * feature // shards, feature // shards
    first = {"merge": (0, merge), "q": (merge, rows), "gain": (merge + rows, PAD)}
    second = {"k": (0, rows), "v": (rows, rows), "out": (2 * rows, rows), "pad": (3 * rows, PAD)}
    return (first, second, merge + rows + PAD)


def load_weights(copies, pieces, names, dst):
    me = lax.axis_index("dp")
    shards = 4
    started = {}
    for name in names:
        kind, column = WHERE[name]
        arrays = pieces[kind]
        started[name] = []
        for flip, ref in zip((0, 1, shards // 2, shards - 1), arrays):
            rows = dst[name].shape[0] // shards
            at = pl.multiple_of((me ^ flip) * rows, rows)
            if kind == "rest":
                base = 0 if name == "out" else ref.shape[0] - PAD
                source = ref.at[pl.ds(base, rows)]
            elif kind == "qkv":
                width = dst[name].shape[1]
                source = ref.at[:, pl.ds(column * width, width)]
            else:
                source = ref
            started[name].append(copies.start(source, dst[name].at[pl.ds(at, rows)]))
    return started


WHERE = {
    "merge": ("merge", 0), "q": ("qkv", 0), "k": ("qkv", 1), "v": ("qkv", 2),
    "out": ("rest", 0), "gain": ("rest", 1),
}


def pieces_of(refs):
    return {"merge": refs[0:4], "qkv": refs[4:8], "rest": refs[8:12]}


def load_tokens(copies, moved, own, dst):
    started = []
    for m in range(moved.shape[0]):
        part = moved.shape[1]
        size = own.shape[1]
        started.append(copies.start(moved.at[m], dst.at[pl.ds(m * size, part)]))
        started.append(
            copies.start(
                own.at[m, pl.ds(0, size - part)], dst.at[pl.ds(m * size + part, size - part)]
            )
        )
    return started


def full_gain(gain, shards):
    feature = gain.shape[1]
    rows = feature // shards
    parts = [gain[i * PAD : i * PAD + 1, :rows] for i in range(shards)]
    return jnp.concatenate(parts, axis=1).astype(F32)


def window_allowed(mask_row, first_band, lon_count):
    cells = mask_row.shape[1]
    query = lax.broadcasted_iota(jnp.int32, (cells, cells), 0)
    key = lax.broadcasted_iota(jnp.int32, (cells, cells), 1)
    lon_same = (query % lon_count + SW) // WW == (key % lon_count + SW) // WW
    lat_same = (query // lon_count) // SH == (key // lon_count) // SH
    inside = lon_same & (lat_same | jnp.logical_not(first_band))
    usable = jnp.broadcast_to(mask_row, (cells, cells)) == 1
    return inside & (usable | (query == key))


def stacked_heads(pair, head_dim):
    lane = lax.broadcasted_iota(jnp.int32, pair.shape, 1)
    zero = jnp.zeros_like(pair)
    return jnp.concatenate(
        [jnp.where(lane < head_dim, pair, zero), jnp.where(lane < head_dim, zero, pair)], axis=0
    )


def unstacked_heads(stacked, head_dim):
    cells = stacked.shape[0] // 2
    low, high = stacked[:cells], stacked[cells:]
    lane = lax.broadcasted_iota(jnp.int32, low.shape, 1)
    return jnp.where(lane < head_dim, low, high)


def probabilities(q_stack, k, allowed2, head_dim):
    scores = dot_nt(q_stack, k) * head_dim ** (-0.5)
    scores = jnp.where(allowed2, scores, MASKED)
    weights = jnp.exp(scores - jnp.max(scores, axis=-1, keepdims=True))
    return weights / jnp.sum(weights, axis=-1, keepdims=True)


def masks(mask, first_band, lon_count):
    out = []
    for m in range(mask.shape[0]):
        allowed = window_allowed(mask[m : m + 1, :], first_band, lon_count)
        out.append(jnp.concatenate([allowed, allowed], axis=0))
    return out


def pairs(mask_shape, feature):
    micro, cells = mask_shape
    lanes = 2 * (feature // HEADS)
    for m in range(micro):
        for p in range(feature // lanes):
            yield (m, slice(m * cells, (m + 1) * cells), p * lanes, lanes)


def attend(qkv, mix, allowed, mask_shape, feature):
    head_dim = feature // HEADS
    for m, rows, at, lanes in pairs(mask_shape, feature):
        q, k, v = (qkv[rows, i * feature + at : i * feature + at + lanes] for i in range(3))
        probs = probabilities(stacked_heads(q, head_dim), k, allowed[m], head_dim).astype(BF16)
        mixed = unstacked_heads(dot(probs, v), head_dim)
        mix[rows, at : at + lanes] = mixed.astype(BF16)


def attend_back(qkv, grad_mix, grad_proj, allowed, mask_shape, feature):
    head_dim = feature // HEADS
    for m, rows, at, lanes in pairs(mask_shape, feature):
        q, k, v = (qkv[rows, i * feature + at : i * feature + at + lanes] for i in range(3))
        q_stack = stacked_heads(q, head_dim)
        g_stack = stacked_heads(grad_mix[rows, at : at + lanes], head_dim)
        probs = probabilities(q_stack, k, allowed[m], head_dim)
        grad_probs = dot_nt(g_stack, v)
        inner = jnp.sum(grad_probs * probs, axis=-1, keepdims=True)
        grad_scores = (probs * (grad_probs - inner) * head_dim ** (-0.5)).astype(BF16)
        grad_q = unstacked_heads(dot(grad_scores, k), head_dim)
        grad_k = dot_tn(grad_scores, q_stack)
        grad_v = dot_tn(probs.astype(BF16), g_stack)
        for i, grad in enumerate((grad_q, grad_k, grad_v)):
            grad_proj[rows, i * feature + at : i * feature + at + lanes] = grad.astype(BF16)


def normalize(update):
    average = jnp.mean(update, axis=-1, keepdims=True)
    centered = update - average
    spread = jnp.mean(centered * centered, axis=-1, keepdims=True)
    inverse = lax.rsqrt(spread + EPSILON)
    return (centered * inverse, inverse)


def forward(x, w, waits, gain_of, allowed, mask_shape, normed_ref, inverse_ref, hidden, qkv, mix):
    feature = x.shape[1]
    wait_all(waits["merge"])
    tokens = x[...]
    update = dot(tokens, w["merge"][:feature]) + dot(tokens, w["merge"][feature:])
    normed, inverse = normalize(update)
    normed_ref[...] = normed
    inverse_ref[...] = jnp.broadcast_to(inverse, inverse_ref.shape)
    hidden[...] = (normed * gain_of()).astype(BF16)
    for i, name in enumerate(("q", "k", "v")):
        wait_all(waits[name])
        qkv[:, i * feature : (i + 1) * feature] = dot(hidden[...], w[name][...]).astype(BF16)
    attend(qkv, mix, allowed, mask_shape, feature)
    wait_all(waits["out"])
    return update + dot(mix[...], w["out"][...])


def backward(grad_out, w, gain, allowed, mask_shape, normed, inverse, qkv, grad_mix, grad_proj):
    feature = grad_out.shape[1]
    grad_mix[...] = dot_nt(grad_out[...], w["out"][...]).astype(BF16)
    attend_back(qkv, grad_mix, grad_proj, allowed, mask_shape, feature)
    grad_hidden = sum(
        dot_nt(grad_proj[:, i * feature : (i + 1) * feature], w[name][...])
        for i, name in enumerate(("q", "k", "v"))
    )
    normed = normed[...]
    grad_gain = jnp.sum(grad_hidden * normed, axis=0, keepdims=True)
    grad_normed = grad_hidden * gain
    centered = (
        grad_normed
        - jnp.mean(grad_normed, axis=-1, keepdims=True)
        - normed * jnp.mean(grad_normed * normed, axis=-1, keepdims=True)
    )
    grad_update = grad_out[...].astype(F32) + inverse[:, :1] * centered
    return (grad_update.astype(BF16), grad_gain)


def send_grads(copies, x, hidden, mix, grad_out, grad_proj, grad_update, grad_gain, dw, outs):
    feature = x.shape[1]
    shards = 2 * outs[0].shape[0]
    first, second, _ = layout(feature, shards)
    me = lax.axis_index("dp")
    low, high = me % 2, me // 2
    rows = feature // shards
    width = feature // CHUNKS
    started = []

    def target(name, chunk, by_low, by_high):
        p_keep, p_send, q_keep, q_send = outs[4 * chunk : 4 * chunk + 4]
        if name in first:
            start, size = first[name]
            ref = (p_send if by_high else p_keep).at[by_low]
        else:
            start, size = second[name]
            ref = (q_send if by_low else q_keep).at[by_high]
        return ref.at[pl.ds(start, size)]

    def emit(name, period):
        for chunk in range(CHUNKS):
            for by_high in range(2):
                for by_low in range(2):
                    owner = (high ^ by_high) * 2 + (low ^ by_low)
                    to = target(name, chunk, by_low, by_high)
                    at = pl.multiple_of((owner * to.shape[0]) % period, to.shape[0])
                    part = dw[name].at[pl.ds(at, to.shape[0]), pl.ds(chunk * width, width)]
                    started.append(copies.start(part, to))

    dw["out"][...] = dot_tn(mix[...], grad_out[...]).astype(BF16)
    emit("out", feature)
    for i, name in enumerate(("q", "k", "v")):
        part = grad_proj[:, i * feature : (i + 1) * feature]
        dw[name][...] = dot_tn(hidden[...], part).astype(BF16)
        emit(name, feature)
    for i in range(shards):
        part = grad_gain[:, i * rows : (i + 1) * rows].astype(BF16)
        dw["gain"][i * PAD : (i + 1) * PAD, :] = jnp.zeros((PAD, feature), BF16)
        dw["gain"][i * PAD : (i + 1) * PAD, :rows] = jnp.broadcast_to(part, (PAD, rows))
    emit("gain", shards * PAD)
    dw["pad"][...] = jnp.zeros_like(dw["pad"])
    emit("pad", PAD)
    dw["merge"][...] = dot_tn(x[...], grad_update[...]).astype(BF16)
    emit("merge", feature)
    return started


def lon_of(cells):
    return cells // WH


def role(segment):
    return pl.when(lax.axis_index("segment") == segment)


def forward_kernel(*refs):
    mask_in, moved, own, *rest = refs
    pieces, rest = rest[:12], rest[12:]
    y, normed, inverse, hidden, qkv, mix, *rest = rest
    mask, x, wm, wq, wk, wv, wo, wg, y_s, normed_s, inverse_s, hidden_s, qkv_s, mix_s, sems = rest

    @role(0)
    def run():
        shards = wg.shape[0] // PAD
        copies = Copies(sems)
        w = {"merge": wm, "q": wq, "k": wk, "v": wv, "out": wo, "gain": wg}
        mask_copy = copies.start(mask_in, mask)
        tokens = load_tokens(copies, moved, own, x)
        names = ("merge", "gain", "q", "k", "v", "out")
        waits = load_weights(copies, pieces_of(pieces), names, w)
        mask_copy.wait()
        allowed = masks(mask, lax.axis_index("band") == 0, lon_of(mask.shape[1]))
        wait_all(tokens)

        def gain_of():
            wait_all(waits["gain"])
            return full_gain(wg, shards)

        result = forward(x, w, waits, gain_of, allowed, mask.shape,
                         normed_s, inverse_s, hidden_s, qkv_s, mix_s)
        y_s[...] = result.astype(BF16)
        done = [
            copies.start(a, b)
            for a, b in ((y_s, y), (normed_s, normed), (inverse_s, inverse), (hidden_s, hidden),
                         (qkv_s, qkv), (mix_s, mix))
        ]
        wait_all(done)


def last_kernel(*refs):
    mask_in, moved, own, y0, *rest = refs
    pieces, rest = rest[:12], rest[13:]
    y, g0, gain_out, g_out, hidden, mix, proj_out, update_out, *rest = rest
    (mask, x, g, wm, wq, wk, wv, wo, wg, y_s, g_s, normed_s, inverse_s, hidden_s, qkv_s, mix_s,
     gmix, gproj, gain_s, update_s, sems) = rest

    @role(1)
    def run():
        shards = wg.shape[0] // PAD
        feature = x.shape[1]
        copies = Copies(sems)
        w = {"merge": wm, "q": wq, "k": wk, "v": wv, "out": wo, "gain": wg}
        mask_copy = copies.start(mask_in, mask)
        x_in = copies.start(y0, x)
        names = ("merge", "gain", "q", "k", "v", "out")
        waits = load_weights(copies, pieces_of(pieces), names, w)
        tokens = load_tokens(copies, moved, own, g)
        mask_copy.wait()
        allowed = masks(mask, lax.axis_index("band") == 0, lon_of(mask.shape[1]))
        x_in.wait()

        def gain_of():
            wait_all(waits["gain"])
            return full_gain(wg, shards)

        result = forward(x, w, waits, gain_of, allowed, mask.shape,
                         normed_s, inverse_s, hidden_s, qkv_s, mix_s)
        y_s[...] = result.astype(BF16)
        wait_all(tokens)
        done = [copies.start(y_s, y), copies.start(g, g_out), copies.start(hidden_s, hidden),
                copies.start(mix_s, mix)]
        grad_update, grad_gain = backward(g, w, full_gain(wg, shards), allowed, mask.shape,
                                          normed_s, inverse_s, qkv_s, gmix, gproj)
        done.append(copies.start(gproj, proj_out))
        gain_s[...] = jnp.broadcast_to(grad_gain, gain_s.shape)
        update_s[...] = grad_update
        done += [copies.start(gain_s, gain_out), copies.start(update_s, update_out)]
        chain = dot_nt(grad_update, wm[:feature]).astype(BF16).astype(F32)
        side = dot_nt(grad_update, wm[feature:]).astype(BF16).astype(F32)
        g_s[...] = (chain + side).astype(BF16)
        done.append(copies.start(g_s, g0))
        wait_all(done)


def weight_kernel(*refs):
    ins, outs, rest = refs[:7], refs[7 : 7 + 4 * CHUNKS], refs[7 + 4 * CHUNKS :]
    scratch, dw_refs, sems = rest[:7], rest[7:14], rest[14]

    @role(1)
    def run():
        copies = Copies(sems)
        wait_all([copies.start(a, b) for a, b in zip(ins, scratch)])
        x, gain, g, hidden, mix, gproj, update = scratch
        dw = dict(zip(("merge", "q", "k", "v", "out", "gain", "pad"), dw_refs))
        wait_all(send_grads(copies, x, hidden, mix, g, gproj, update, gain[:1, :], dw, outs))


def first_kernel(*refs):
    mask_in, moved, own, g0, *rest = refs
    pieces, rest = rest[:12], rest[12:]
    normed, inverse, hidden, qkv, mix, *rest = rest
    skip, count = 1 + 4 * CHUNKS, 4 * CHUNKS
    outs, rest = rest[skip : skip + count], rest[skip + count :]
    (mask, x, g, wq, wk, wv, wo, wg, normed_s, inverse_s, hidden_s, qkv_s, mix_s,
     gmix, gproj, *dw_refs, sems) = rest

    @role(0)
    def run():
        shards = wg.shape[0] // PAD
        copies = Copies(sems)
        w = {"q": wq, "k": wk, "v": wv, "out": wo, "gain": wg}
        mask_copy = copies.start(mask_in, mask)
        g_in = [copies.start(g0, g)]
        names = ("out", "q", "k", "v", "gain")
        waits = load_weights(copies, pieces_of(pieces), names, w)
        saved = [
            copies.start(a, b)
            for a, b in ((qkv, qkv_s), (normed, normed_s), (inverse, inverse_s), (hidden, hidden_s),
                         (mix, mix_s))
        ]
        tokens = load_tokens(copies, moved, own, x)
        mask_copy.wait()
        allowed = masks(mask, lax.axis_index("band") == 0, lon_of(mask.shape[1]))
        wait_all(g_in + saved + tokens)
        for name in names:
            wait_all(waits[name])
        grad_update, grad_gain = backward(g, w, full_gain(wg, shards), allowed, mask.shape,
                                          normed_s, inverse_s, qkv_s, gmix, gproj)
        dw = dict(zip(("merge", "q", "k", "v", "out", "gain", "pad"), dw_refs))
        wait_all(send_grads(copies, x, hidden_s, mix_s, g, gproj, grad_update, grad_gain, dw, outs))


def rest_kernel(out, gain, packed):
    rows, width = gain.shape[1], out.shape[1]
    packed[: out.shape[0], :] = out[...]
    packed[out.shape[0] :, :] = jnp.zeros((PAD, width), BF16)
    packed[out.shape[0] :, :rows] = jnp.broadcast_to(gain[...], (PAD, rows))


def final_kernel(*refs):
    halves, (merge, qkv, out, gain) = refs[: 2 * CHUNKS], refs[2 * CHUNKS :]
    feature = merge.shape[2]
    shards = 2 * feature // merge.shape[1]
    first, second, _ = layout(feature, shards)
    even = lax.axis_index("band") % 2 == 0
    width = feature // CHUNKS

    def rows(name, chunk):
        own, other = halves[2 * chunk], halves[2 * chunk + 1]
        table, flip = (first, False) if name in first else (second, True)
        start, size = table[name]
        mine, theirs = own[start : start + size, :], other[start : start + size, :]
        a, b = (theirs, mine) if flip else (mine, theirs)
        return jnp.where(even, a.astype(F32), b.astype(F32))

    for chunk in range(CHUNKS):
        at = chunk * width
        merge[0, :, at : at + width] = rows("merge", chunk)
        for i, name in enumerate(("q", "k", "v")):
            qkv[0, :, i * feature + at : i * feature + at + width] = rows(name, chunk)
        out[0, :, at : at + width] = rows("out", chunk)
    gain[...] = rows("gain", 0)[:1, : gain.shape[1]]


ANY = pl.BlockSpec(memory_space=pl.ANY)
VMEM = pl.BlockSpec(memory_space=pltpu.VMEM)


def call(kernel, ins, outs, scratch, aliases, flops):
    moved = sum(a.size * a.dtype.itemsize for a in list(ins) + list(outs))
    return pl.pallas_call(
        kernel,
        out_shape=tuple(outs),
        in_specs=[ANY] * len(ins),
        out_specs=tuple([ANY] * len(outs)),
        scratch_shapes=scratch,
        input_output_aliases=aliases,
        cost_estimate=pl.CostEstimate(flops=flops, bytes_accessed=moved, transcendentals=0),
    )(*ins)


def flip(value, axis, bit):
    size = lax.axis_size(axis)
    return lax.ppermute(value, axis, [(i, i ^ bit) for i in range(size)])


def gather(merge, qkv, rest):
    high = lax.axis_size("dp") // 2

    def named(value, bit):
        return flip(value, "dp", bit)

    merge_low, merge_high = named(merge, 1), named(merge, high)
    qkv_low, qkv_high = named(qkv, 1), named(qkv, high)
    rest_low, rest_high = named(rest, 1), named(rest, high)
    merge_both = named(merge_low, high)
    qkv_both = named(qkv_high, 1)
    rest_both = named(rest_low, high)
    return (merge, merge_low, merge_high, merge_both, qkv, qkv_low, qkv_high, qkv_both,
            rest, rest_low, rest_high, rest_both)


def body(fields, cell_mask, merge_weight, qkv_weight, out_weight, norm_gain, out_cotangent):
    _, micro, row_count, lon_count, feature = fields.shape
    shards, bands = lax.axis_size("dp"), lax.axis_size("band")
    assert lax.axis_size("segment") == 2 and row_count == WH and shards == 4
    segment, band = lax.axis_index("segment"), lax.axis_index("band")
    cells = row_count * lon_count
    total = micro * cells
    _, _, half = layout(feature, shards)
    rows = feature // shards

    def shape(*dims, dtype=BF16):
        return jax.ShapeDtypeStruct(dims, dtype)

    def room(*dims, dtype=BF16):
        return pltpu.VMEM(dims, dtype)

    merge, qkv, out = merge_weight[0], qkv_weight[0], out_weight[0]
    rest = pl.pallas_call(
        rest_kernel,
        out_shape=shape(rows + PAD, feature),
        in_specs=[VMEM, VMEM],
        out_specs=VMEM,
        name="pack",
    )(out, norm_gain)
    pieces = gather(merge, qkv, rest)

    down = [(i, (i + 1) % bands) for i in range(bands)]
    up = [(j, i) for i, j in down]
    flat = (micro, cells, feature)
    source = jnp.where(segment == 0, fields[0, :, row_count - SH :], out_cotangent[0, :, row_count - SH :])
    moved = lax.ppermute(source, "band", down)
    moved = moved.reshape(micro, SH * lon_count, feature)
    mask_moved = lax.ppermute(cell_mask[0, :, row_count - SH :], "band", down)
    mask = jnp.concatenate([mask_moved, cell_mask[0, :, : row_count - SH]], axis=1).reshape(micro, cells)
    own_fields = fields.reshape(flat)
    own_cotangent = out_cotangent.reshape(flat)

    square = room(feature, feature)
    tokens = room(total, feature)
    wide = room(total, 3 * feature)
    mask_room = pltpu.VMEM((micro, cells), jnp.int32)
    weights = [square] * 4 + [room(shards * PAD, feature)]
    merge_room = room(2 * feature, feature)
    record_rooms = [
        room(total, feature, dtype=F32), room(total, 128, dtype=F32), tokens, wide, tokens,
    ]
    grad_rooms = [square] * 5 + [room(shards * PAD, feature), room(PAD, feature)]
    sems = [pltpu.SemaphoreType.DMA((128,))]
    unit = 2 * total * feature * feature
    token_shape, wide_shape = shape(total, feature), shape(total, 3 * feature)

    y, *records = call(
        forward_kernel,
        (mask, moved, own_fields) + pieces,
        [token_shape, shape(total, feature, dtype=F32), shape(total, 128, dtype=F32),
         token_shape, wide_shape, token_shape],
        [mask_room, tokens, merge_room] + weights + [tokens] + record_rooms + sems,
        {}, 6 * unit,
    )
    y0 = lax.ppermute(y, "segment", [(0, 1)])
    gain_room = room(8, feature, dtype=F32)
    y, g_out, *operands = call(
        last_kernel,
        (mask, moved, own_cotangent, y0) + pieces + (y,),
        [token_shape, token_shape, shape(8, feature, dtype=F32), token_shape, token_shape, token_shape,
         wide_shape, token_shape],
        [mask_room, tokens, tokens, merge_room] + weights + [tokens, tokens] + record_rooms
        + [tokens, wide, gain_room, tokens] + sems,
        {16: 0}, 13 * unit,
    )
    g0 = lax.ppermute(g_out, "segment", [(1, 0)])
    shard_shapes = [shape(2, half, feature // CHUNKS)] * (4 * CHUNKS)
    grads = call(
        weight_kernel,
        (y0,) + tuple(operands),
        shard_shapes,
        [tokens, gain_room, tokens, tokens, tokens, wide, tokens] + grad_rooms + sems,
        {}, 5 * unit,
    )

    y = y.reshape(micro, cells, feature)
    part = SH * lon_count
    back = lax.ppermute(y[:, :part], "band", up)
    section_out = jnp.concatenate([y[:, part:], back], axis=1)
    section_out = section_out.reshape(1, 1, micro, row_count, lon_count, feature)

    inputs = (mask, moved, own_fields, g0) + pieces + tuple(records) + (section_out,)
    grads = call(
        first_kernel,
        inputs + tuple(grads),
        shard_shapes,
        [mask_room, tokens, tokens] + weights + record_rooms + [tokens, wide] + grad_rooms + sems,
        {len(inputs) + i: i for i in range(4 * CHUNKS)}, 12 * unit,
    )

    high = shards // 2
    even = band % 2 == 0
    halves = []

    def named(value, axis, bit):
        return flip(value, axis, bit).astype(F32)

    for chunk in range(CHUNKS):
        p_keep, p_send, q_keep, q_send = grads[4 * chunk : 4 * chunk + 4]
        p_in = named(p_send, "dp", high)
        q_in = named(q_send, "dp", 1)
        p_pass = (p_keep[1].astype(F32) + p_in[1]).astype(BF16)
        q_pass = (q_keep[1].astype(F32) + q_in[1]).astype(BF16)
        p_sum = p_keep[0].astype(F32) + p_in[0] + named(p_pass, "dp", 1)
        q_sum = q_keep[0].astype(F32) + q_in[0] + named(q_pass, "dp", high)
        mine = jnp.where(even, p_sum, q_sum)
        theirs = jnp.where(even, q_sum, p_sum).astype(BF16)
        mine = (mine + named(theirs, "band", 1)).astype(BF16)
        bit = 2
        while bit < bands:
            mine = (mine.astype(F32) + named(mine, "band", bit)).astype(BF16)
            bit *= 2
        halves += [mine, flip(mine, "band", 1)]
    merge_grad, qkv_grad, out_grad, gain_grad = pl.pallas_call(
        final_kernel,
        out_shape=(
            shape(1, 2 * rows, feature, dtype=F32), shape(1, rows, 3 * feature, dtype=F32),
            shape(1, rows, feature, dtype=F32), shape(1, rows, dtype=F32),
        ),
        in_specs=[VMEM] * len(halves),
        out_specs=(VMEM,) * 4,
        name="unpack",
    )(*halves)
    return (section_out, merge_grad, qkv_grad, out_grad, gain_grad)


def solution(mesh):
    return jax.shard_map(
        body,
        mesh=mesh,
        in_specs=(
            P("dp", None, "band", None, None),
            P("dp", None, "band", None),
            P("segment", "dp", None),
            P("segment", "dp", None),
            P("segment", "dp", None),
            P("segment", "dp"),
            P("dp", None, "band", None, None),
        ),
        out_specs=(
            P("segment", "dp", None, "band", None, None),
            P("segment", "dp", None),
            P("segment", "dp", None),
            P("segment", "dp", None),
            P("segment", "dp"),
        ),
        check_vma=False,
    )
```

```python
import jax
import jax.numpy as jnp
from jax import lax
from jax.experimental import pallas as pl
from jax.experimental.pallas import tpu as pltpu
from jax.sharding import PartitionSpec as P


HEADS = 8
WH = 8
WW = 16
SH = 4
SW = 8
PAD = 16
CHUNKS = 4

EPSILON = 1e-05
MASKED = -1e30


F32 = jnp.float32
BF16 = jnp.bfloat16


def dot(a, b):
    return lax.dot_general(a, b, (((1,), (0,)), ((), ())), preferred_element_type=F32)


def dot_nt(a, b):
    return lax.dot_general(a, b, (((1,), (1,)), ((), ())), preferred_element_type=F32)


def dot_tn(a, b):
    return lax.dot_general(a, b, (((0,), (0,)), ((), ())), preferred_element_type=F32)


class Copies:
    def __init__(self, sems):
        self.sems = sems
        self.used = 0

    def start(self, src, dst):
        copy = pltpu.make_async_copy(src, dst, self.sems.at[self.used])
        self.used += 1
        copy.start()
        return copy


def wait_all(copies):
    for copy in copies:
        copy.wait()


def layout(feature, shards):
    merge, rows = 2 * feature // shards, feature // shards
    first = {"merge": (0, merge), "q": (merge, rows), "gain": (merge + rows, PAD)}
    second = {"k": (0, rows), "v": (rows, rows), "out": (2 * rows, rows), "pad": (3 * rows, PAD)}
    return (first, second, merge + rows + PAD)


def load_weights(copies, pieces, names, dst):
    me = lax.axis_index("dp")
    shards = 4
    started = {}
    for name in names:
        kind, column = WHERE[name]
        arrays = pieces[kind]
        started[name] = []
        for flip, ref in zip((0, 1, shards // 2, shards - 1), arrays):
            rows = dst[name].shape[0] // shards
            at = pl.multiple_of((me ^ flip) * rows, rows)
            if kind == "rest":
                base = 0 if name == "out" else ref.shape[0] - PAD
                source = ref.at[pl.ds(base, rows)]
            elif kind == "qkv":
                width = dst[name].shape[1]
                source = ref.at[:, pl.ds(column * width, width)]
            else:
                source = ref
            started[name].append(copies.start(source, dst[name].at[pl.ds(at, rows)]))
    return started


WHERE = {
    "merge": ("merge", 0), "q": ("qkv", 0), "k": ("qkv", 1), "v": ("qkv", 2),
    "out": ("rest", 0), "gain": ("rest", 1),
}


def pieces_of(refs):
    return {"merge": refs[0:4], "qkv": refs[4:8], "rest": refs[8:12]}


def load_tokens(copies, moved, own, dst):
    started = []
    for m in range(moved.shape[0]):
        part = moved.shape[1]
        size = own.shape[1]
        started.append(copies.start(moved.at[m], dst.at[pl.ds(m * size, part)]))
        started.append(
            copies.start(
                own.at[m, pl.ds(0, size - part)], dst.at[pl.ds(m * size + part, size - part)]
            )
        )
    return started


def full_gain(gain, shards):
    feature = gain.shape[1]
    rows = feature // shards
    parts = [gain[i * PAD : i * PAD + 1, :rows] for i in range(shards)]
    return jnp.concatenate(parts, axis=1).astype(F32)


def window_allowed(mask_row, first_band, lon_count):
    cells = mask_row.shape[1]
    query = lax.broadcasted_iota(jnp.int32, (cells, cells), 0)
    key = lax.broadcasted_iota(jnp.int32, (cells, cells), 1)
    lon_same = (query % lon_count + SW) // WW == (key % lon_count + SW) // WW
    lat_same = (query // lon_count) // SH == (key // lon_count) // SH
    inside = lon_same & (lat_same | jnp.logical_not(first_band))
    usable = jnp.broadcast_to(mask_row, (cells, cells)) == 1
    return inside & (usable | (query == key))


def stacked_heads(pair, head_dim):
    lane = lax.broadcasted_iota(jnp.int32, pair.shape, 1)
    zero = jnp.zeros_like(pair)
    return jnp.concatenate(
        [jnp.where(lane < head_dim, pair, zero), jnp.where(lane < head_dim, zero, pair)], axis=0
    )


def unstacked_heads(stacked, head_dim):
    cells = stacked.shape[0] // 2
    low, high = stacked[:cells], stacked[cells:]
    lane = lax.broadcasted_iota(jnp.int32, low.shape, 1)
    return jnp.where(lane < head_dim, low, high)


def probabilities(scores, allowed2, head_dim):
    scores = jnp.where(allowed2, scores * head_dim ** (-0.5), MASKED)
    weights = jnp.exp(scores - jnp.max(scores, axis=-1, keepdims=True))
    return weights * (1.0 / jnp.sum(weights, axis=-1, keepdims=True))


def masks(mask, first_band, lon_count):
    out = []
    for m in range(mask.shape[0]):
        allowed = window_allowed(mask[m : m + 1, :], first_band, lon_count)
        out.append(jnp.concatenate([allowed, allowed], axis=0))
    return out


def pairs(micro, cells, feature):
    lanes = 2 * (feature // HEADS)
    count = feature // lanes
    rows = slice(micro * cells, (micro + 1) * cells)
    return [(micro * count + p, rows, p * lanes, lanes) for p in range(count)]


def part_of(qkv, which, rows, at, lanes):
    feature = qkv.shape[1] // 3
    return qkv[rows, which * feature + at : which * feature + at + lanes]


def attend(qkv, mix, probs, allowed, mask_shape, feature):
    head_dim = feature // HEADS
    for m in range(mask_shape[0]):
        group = pairs(m, mask_shape[1], feature)
        scores = [
            dot_nt(stacked_heads(part_of(qkv, 0, *where), head_dim), part_of(qkv, 1, *where))
            for _, *where in group
        ]
        for (n, *_), score in zip(group, scores):
            probs[n] = probabilities(score, allowed[m], head_dim).astype(BF16)
        for n, rows, at, lanes in group:
            mixed = dot(probs[n], part_of(qkv, 2, rows, at, lanes))
            mix[rows, at : at + lanes] = unstacked_heads(mixed, head_dim).astype(BF16)


def attend_back(qkv, probs, grad_mix, grad_proj, mask_shape, feature):
    head_dim = feature // HEADS

    def put(which, grad, rows, at, lanes):
        grad_proj[rows, which * feature + at : which * feature + at + lanes] = grad.astype(BF16)

    for m in range(mask_shape[0]):
        group = pairs(m, mask_shape[1], feature)
        grad_probs = []
        for n, rows, at, lanes in group:
            g_stack = stacked_heads(grad_mix[rows, at : at + lanes], head_dim)
            grad_probs.append(dot_nt(g_stack, part_of(qkv, 2, rows, at, lanes)))
            put(2, dot_tn(probs[n], g_stack), rows, at, lanes)
        grad_scores = []
        for (n, *_), grad in zip(group, grad_probs):
            prob = probs[n].astype(F32)
            inner = jnp.sum(grad * prob, axis=-1, keepdims=True)
            grad_scores.append((prob * (grad - inner) * head_dim ** (-0.5)).astype(BF16))
        for (n, rows, at, lanes), grad in zip(group, grad_scores):
            q_stack = stacked_heads(part_of(qkv, 0, rows, at, lanes), head_dim)
            put(0, unstacked_heads(dot(grad, part_of(qkv, 1, rows, at, lanes)), head_dim), rows, at, lanes)
            put(1, dot_tn(grad, q_stack), rows, at, lanes)


def normalize(update):
    average = jnp.mean(update, axis=-1, keepdims=True)
    centered = update - average
    spread = jnp.mean(centered * centered, axis=-1, keepdims=True)
    inverse = lax.rsqrt(spread + EPSILON)
    return (centered * inverse, inverse)


def forward(x, w, waits, gain_of, allowed, mask_shape, room, kept):
    feature = x.shape[1]
    wait_all(waits["merge"])
    tokens = x[...]
    update = dot(tokens, w["merge"][:feature]) + dot(tokens, w["merge"][feature:])
    normed, inverse = normalize(update)
    room["normed"][...] = normed
    kept("normed")
    room["inverse"][...] = jnp.broadcast_to(inverse, room["inverse"].shape)
    kept("inverse")
    hidden, qkv, mix = room["hidden"], room["qkv"], room["mix"]
    hidden[...] = (normed * gain_of()).astype(BF16)
    kept("hidden")
    for i, name in enumerate(("q", "k", "v")):
        wait_all(waits[name])
        qkv[:, i * feature : (i + 1) * feature] = dot(hidden[...], w[name][...]).astype(BF16)
    kept("qkv")
    attend(qkv, mix, room["probs"], allowed, mask_shape, feature)
    kept("probs")
    kept("mix")
    wait_all(waits["out"])
    return update + dot(mix[...], w["out"][...])


RECORDS = ("normed", "inverse", "hidden", "qkv", "mix", "probs")


def backward(grad_out, w, gain, mask_shape, room, grad_mix, grad_proj):
    feature = grad_out.shape[1]
    grad_mix[...] = dot_nt(grad_out[...], w["out"][...]).astype(BF16)
    attend_back(room["qkv"], room["probs"], grad_mix, grad_proj, mask_shape, feature)
    grad_hidden = sum(
        dot_nt(grad_proj[:, i * feature : (i + 1) * feature], w[name][...])
        for i, name in enumerate(("q", "k", "v"))
    )
    normed, inverse = room["normed"][...], room["inverse"]
    grad_gain = jnp.sum(grad_hidden * normed, axis=0, keepdims=True)
    grad_normed = grad_hidden * gain
    centered = (
        grad_normed
        - jnp.mean(grad_normed, axis=-1, keepdims=True)
        - normed * jnp.mean(grad_normed * normed, axis=-1, keepdims=True)
    )
    grad_update = grad_out[...].astype(F32) + inverse[:, :1] * centered
    return (grad_update.astype(BF16), grad_gain)


def send_grads(copies, x, hidden, mix, grad_out, grad_proj, grad_update, grad_gain, dw, outs):
    feature = x.shape[1]
    shards = 2 * outs[0].shape[0]
    first, second, half = layout(feature, shards)
    me = lax.axis_index("dp")
    low, high = me % 2, me // 2
    rows = feature // shards
    width = feature // CHUNKS
    dw_first, dw_second = dw
    started = []

    def put(name, value):
        block = dw_first if name in first else dw_second
        start, size = first[name] if name in first else second[name]
        value = value.astype(BF16)
        for i in range(shards):
            at = (i * size) % feature
            block[i, start : start + size, :] = value[at : at + size]

    def emit(which, start, size):
        block = (dw_first, dw_second)[which]
        for chunk in range(CHUNKS):
            p_keep, p_send, q_keep, q_send = outs[4 * chunk : 4 * chunk + 4]
            for by_high in range(2):
                for by_low in range(2):
                    owner = (high ^ by_high) * 2 + (low ^ by_low)
                    if which:
                        ref = (q_send if by_low else q_keep).at[by_high]
                    else:
                        ref = (p_send if by_high else p_keep).at[by_low]
                    part = block.at[owner, pl.ds(start, size), pl.ds(chunk * width, width)]
                    started.append(copies.start(part, ref.at[pl.ds(start, size)]))

    put("out", dot_tn(mix[...], grad_out[...]))
    for i, name in ((1, "k"), (2, "v")):
        put(name, dot_tn(hidden[...], grad_proj[:, i * feature : (i + 1) * feature]))
    dw_second[:, 3 * rows :, :] = jnp.zeros((shards, PAD, feature), BF16)
    emit(1, 0, half)
    put("q", dot_tn(hidden[...], grad_proj[:, :feature]))
    start = first["gain"][0]
    for i in range(shards):
        part = grad_gain[:, i * rows : (i + 1) * rows].astype(BF16)
        dw_first[i, start:, :] = jnp.zeros((PAD, feature), BF16)
        dw_first[i, start:, :rows] = jnp.broadcast_to(part, (PAD, rows))
    emit(0, first["q"][0], half - first["q"][0])
    put("merge", dot_tn(x[...], grad_update[...]))
    emit(0, 0, first["merge"][1])
    return started


def lon_of(cells):
    return cells // WH


def role(segment):
    return pl.when(lax.axis_index("segment") == segment)


def forward_kernel(*refs):
    mask_in, moved, own, *rest = refs
    pieces, rest = rest[:12], rest[12:]
    y, rest = rest[0], rest[1:]
    saved, rest = dict(zip(RECORDS, rest)), rest[len(RECORDS) :]
    mask, x, wm, wq, wk, wv, wo, wg, y_s, *rest = rest
    room, sems = dict(zip(RECORDS, rest)), rest[-1]

    @role(0)
    def run():
        shards = wg.shape[0] // PAD
        copies = Copies(sems)
        w = {"merge": wm, "q": wq, "k": wk, "v": wv, "out": wo, "gain": wg}
        mask_copy = copies.start(mask_in, mask)
        tokens = load_tokens(copies, moved, own, x)
        names = ("merge", "gain", "q", "k", "v", "out")
        waits = load_weights(copies, pieces_of(pieces), names, w)
        mask_copy.wait()
        allowed = masks(mask, lax.axis_index("band") == 0, lon_of(mask.shape[1]))
        wait_all(tokens)

        def gain_of():
            wait_all(waits["gain"])
            return full_gain(wg, shards)

        done = []

        def kept(name):
            done.append(copies.start(room[name], saved[name]))

        result = forward(x, w, waits, gain_of, allowed, mask.shape, room, kept)
        y_s[...] = result.astype(BF16)
        done.append(copies.start(y_s, y))
        wait_all(done)


def last_kernel(*refs):
    mask_in, moved, own, y0, *rest = refs
    pieces, rest = rest[:12], rest[13:]
    y, g0, gain_out, g_out, hidden, mix, proj_out, update_out, *rest = rest
    mask, x, g, wm, wq, wk, wv, wo, wg, y_s, g_s, *rest = rest
    room, rest = dict(zip(RECORDS, rest)), rest[len(RECORDS) :]
    gmix, gproj, gain_s, update_s, sems = rest

    @role(1)
    def run():
        shards = wg.shape[0] // PAD
        feature = x.shape[1]
        copies = Copies(sems)
        w = {"merge": wm, "q": wq, "k": wk, "v": wv, "out": wo, "gain": wg}
        mask_copy = copies.start(mask_in, mask)
        x_in = copies.start(y0, x)
        names = ("merge", "gain", "q", "k", "v", "out")
        waits = load_weights(copies, pieces_of(pieces), names, w)
        tokens = load_tokens(copies, moved, own, g)
        mask_copy.wait()
        allowed = masks(mask, lax.axis_index("band") == 0, lon_of(mask.shape[1]))
        x_in.wait()

        def gain_of():
            wait_all(waits["gain"])
            return full_gain(wg, shards)

        done = []

        def kept(name):
            if name in ("hidden", "mix"):
                done.append(copies.start(room[name], hidden if name == "hidden" else mix))

        result = forward(x, w, waits, gain_of, allowed, mask.shape, room, kept)
        y_s[...] = result.astype(BF16)
        wait_all(tokens)
        done += [copies.start(y_s, y), copies.start(g, g_out)]
        grad_update, grad_gain = backward(g, w, full_gain(wg, shards), mask.shape, room, gmix, gproj)
        done.append(copies.start(gproj, proj_out))
        gain_s[...] = jnp.broadcast_to(grad_gain, gain_s.shape)
        update_s[...] = grad_update
        done += [copies.start(gain_s, gain_out), copies.start(update_s, update_out)]
        chain = dot_nt(grad_update, wm[:feature]).astype(BF16).astype(F32)
        side = dot_nt(grad_update, wm[feature:]).astype(BF16).astype(F32)
        g_s[...] = (chain + side).astype(BF16)
        done.append(copies.start(g_s, g0))
        wait_all(done)


def weight_kernel(*refs):
    ins, outs, rest = refs[:7], refs[7 : 7 + 4 * CHUNKS], refs[7 + 4 * CHUNKS :]
    scratch, dw, sems = rest[:7], rest[7:9], rest[9]

    @role(1)
    def run():
        copies = Copies(sems)
        wait_all([copies.start(a, b) for a, b in zip(ins, scratch)])
        x, gain, g, hidden, mix, gproj, update = scratch
        wait_all(send_grads(copies, x, hidden, mix, g, gproj, update, gain[:1, :], dw, outs))


def first_kernel(*refs):
    cells, moved, own, g0, *rest = refs
    pieces, rest = rest[:12], rest[12:]
    saved, rest = rest[: len(RECORDS)], rest[len(RECORDS) :]
    skip = count = 4 * CHUNKS
    outs, rest = rest[skip : skip + count], rest[skip + count :]
    x, g, wq, wk, wv, wo, wg, *rest = rest
    rooms, rest = rest[: len(RECORDS)], rest[len(RECORDS) :]
    gmix, gproj, dw_first, dw_second, sems = rest

    @role(0)
    def run():
        shards = wg.shape[0] // PAD
        micro, size = own.shape[:2]
        copies = Copies(sems)
        w = {"q": wq, "k": wk, "v": wv, "out": wo, "gain": wg}
        early = [copies.start(g0, g)]
        names = ("out", "q", "k", "v", "gain")
        waits = load_weights(copies, pieces_of(pieces), names, w)
        early += [copies.start(a, b) for a, b in zip(saved, rooms)]
        early += load_tokens(copies, moved, own, x)
        wait_all(early)
        for name in names:
            wait_all(waits[name])
        room = dict(zip(RECORDS, rooms))
        grad_update, grad_gain = backward(g, w, full_gain(wg, shards), (micro, size), room, gmix, gproj)
        wait_all(send_grads(copies, x, room["hidden"], room["mix"], g, gproj, grad_update, grad_gain,
                            (dw_first, dw_second), outs))


def rest_kernel(out, gain, packed):
    rows, width = gain.shape[1], out.shape[1]
    packed[: out.shape[0], :] = out[...]
    packed[out.shape[0] :, :] = jnp.zeros((PAD, width), BF16)
    packed[out.shape[0] :, :rows] = jnp.broadcast_to(gain[...], (PAD, rows))


def final_kernel(*refs):
    halves, (merge, qkv, out, gain) = refs[: 2 * CHUNKS], refs[2 * CHUNKS :]
    feature = merge.shape[2]
    shards = 2 * feature // merge.shape[1]
    first, second, _ = layout(feature, shards)
    even = lax.axis_index("band") % 2 == 0
    width = feature // CHUNKS

    def rows(name, chunk):
        own, other = halves[2 * chunk], halves[2 * chunk + 1]
        table, flip = (first, False) if name in first else (second, True)
        start, size = table[name]
        mine, theirs = own[start : start + size, :], other[start : start + size, :]
        a, b = (theirs, mine) if flip else (mine, theirs)
        return jnp.where(even, a.astype(F32), b.astype(F32))

    for chunk in range(CHUNKS):
        at = chunk * width
        merge[0, :, at : at + width] = rows("merge", chunk)
        for i, name in enumerate(("q", "k", "v")):
            qkv[0, :, i * feature + at : i * feature + at + width] = rows(name, chunk)
        out[0, :, at : at + width] = rows("out", chunk)
    gain[...] = rows("gain", 0)[:1, : gain.shape[1]]


ANY = pl.BlockSpec(memory_space=pl.ANY)
VMEM = pl.BlockSpec(memory_space=pltpu.VMEM)


def call(kernel, ins, outs, scratch, aliases, flops):
    moved = sum(a.size * a.dtype.itemsize for a in list(ins) + list(outs))
    return pl.pallas_call(
        kernel,
        out_shape=tuple(outs),
        in_specs=[ANY] * len(ins),
        out_specs=tuple([ANY] * len(outs)),
        scratch_shapes=scratch,
        input_output_aliases=aliases,
        cost_estimate=pl.CostEstimate(flops=flops, bytes_accessed=moved, transcendentals=0),
    )(*ins)


def flip(value, axis, bit):
    size = lax.axis_size(axis)
    return lax.ppermute(value, axis, [(i, i ^ bit) for i in range(size)])


def gather(merge, qkv, rest):
    high = lax.axis_size("dp") // 2

    def named(value, bit):
        return flip(value, "dp", bit)

    merge_low, merge_high = named(merge, 1), named(merge, high)
    qkv_low, qkv_high = named(qkv, 1), named(qkv, high)
    rest_low, rest_high = named(rest, 1), named(rest, high)
    merge_both = named(merge_low, high)
    qkv_both = named(qkv_high, 1)
    rest_both = named(rest_low, high)
    return (merge, merge_low, merge_high, merge_both, qkv, qkv_low, qkv_high, qkv_both,
            rest, rest_low, rest_high, rest_both)


def body(fields, cell_mask, merge_weight, qkv_weight, out_weight, norm_gain, out_cotangent):
    _, micro, row_count, lon_count, feature = fields.shape
    shards, bands = lax.axis_size("dp"), lax.axis_size("band")
    assert lax.axis_size("segment") == 2 and row_count == WH and shards == 4
    segment, band = lax.axis_index("segment"), lax.axis_index("band")
    cells = row_count * lon_count
    total = micro * cells
    _, _, half = layout(feature, shards)
    rows = feature // shards

    def shape(*dims, dtype=BF16):
        return jax.ShapeDtypeStruct(dims, dtype)

    def room(*dims, dtype=BF16):
        return pltpu.VMEM(dims, dtype)

    merge, qkv, out = merge_weight[0], qkv_weight[0], out_weight[0]
    rest = pl.pallas_call(
        rest_kernel,
        out_shape=shape(rows + PAD, feature),
        in_specs=[VMEM, VMEM],
        out_specs=VMEM,
        name="pack",
    )(out, norm_gain)
    pieces = gather(merge, qkv, rest)

    down = [(i, (i + 1) % bands) for i in range(bands)]
    up = [(j, i) for i, j in down]
    flat = (micro, cells, feature)
    source = jnp.where(segment == 0, fields[0, :, row_count - SH :], out_cotangent[0, :, row_count - SH :])
    moved = lax.ppermute(source, "band", down)
    moved = moved.reshape(micro, SH * lon_count, feature)
    mask_moved = lax.ppermute(cell_mask[0, :, row_count - SH :], "band", down)
    mask = jnp.concatenate([mask_moved, cell_mask[0, :, : row_count - SH]], axis=1).reshape(micro, cells)
    own_fields = fields.reshape(flat)
    own_cotangent = out_cotangent.reshape(flat)

    square = room(feature, feature)
    tokens = room(total, feature)
    wide = room(total, 3 * feature)
    mask_room = pltpu.VMEM((micro, cells), jnp.int32)
    weights = [square] * 4 + [room(shards * PAD, feature)]
    merge_room = room(2 * feature, feature)
    record_rooms = [
        room(total, feature, dtype=F32), room(total, 128, dtype=F32), tokens, wide, tokens,
        room(micro * HEADS // 2, 2 * cells, cells),
    ]
    grad_rooms = [room(shards, half, feature)] * 2
    sems = [pltpu.SemaphoreType.DMA((128,))]
    unit = 2 * total * feature * feature
    token_shape, wide_shape = shape(total, feature), shape(total, 3 * feature)

    y, *records = call(
        forward_kernel,
        (mask, moved, own_fields) + pieces,
        [token_shape, shape(total, feature, dtype=F32), shape(total, 128, dtype=F32),
         token_shape, wide_shape, token_shape, shape(micro * HEADS // 2, 2 * cells, cells)],
        [mask_room, tokens, merge_room] + weights + [tokens] + record_rooms + sems,
        {}, 6 * unit,
    )
    y0 = lax.ppermute(y, "segment", [(0, 1)])
    gain_room = room(8, feature, dtype=F32)
    y, g_out, *operands = call(
        last_kernel,
        (mask, moved, own_cotangent, y0) + pieces + (y,),
        [token_shape, token_shape, shape(8, feature, dtype=F32), token_shape, token_shape, token_shape,
         wide_shape, token_shape],
        [mask_room, tokens, tokens, merge_room] + weights + [tokens, tokens] + record_rooms
        + [tokens, wide, gain_room, tokens] + sems,
        {16: 0}, 13 * unit,
    )
    g0 = lax.ppermute(g_out, "segment", [(1, 0)])
    shard_shapes = [shape(2, half, feature // CHUNKS)] * (4 * CHUNKS)
    grads = call(
        weight_kernel,
        (y0,) + tuple(operands),
        shard_shapes,
        [tokens, gain_room, tokens, tokens, tokens, wide, tokens] + grad_rooms + sems,
        {}, 5 * unit,
    )

    y = y.reshape(micro, cells, feature)
    part = SH * lon_count
    back = lax.ppermute(y[:, :part], "band", up)
    section_out = jnp.concatenate([y[:, part:], back], axis=1)
    section_out = section_out.reshape(1, 1, micro, row_count, lon_count, feature)

    inputs = (mask, moved, own_fields, g0) + pieces + tuple(records)
    grads = call(
        first_kernel,
        inputs + tuple(grads),
        shard_shapes,
        [tokens, tokens] + weights + record_rooms + [tokens, wide] + grad_rooms + sems,
        {len(inputs) + i: i for i in range(4 * CHUNKS)}, 12 * unit,
    )

    high = shards // 2
    even = band % 2 == 0
    halves = []

    def named(value, axis, bit):
        return flip(value, axis, bit).astype(F32)

    for chunk in range(CHUNKS):
        p_keep, p_send, q_keep, q_send = grads[4 * chunk : 4 * chunk + 4]
        p_in = named(p_send, "dp", high)
        q_in = named(q_send, "dp", 1)
        p_pass = (p_keep[1].astype(F32) + p_in[1]).astype(BF16)
        q_pass = (q_keep[1].astype(F32) + q_in[1]).astype(BF16)
        p_sum = p_keep[0].astype(F32) + p_in[0] + named(p_pass, "dp", 1)
        q_sum = q_keep[0].astype(F32) + q_in[0] + named(q_pass, "dp", high)
        mine = jnp.where(even, p_sum, q_sum)
        theirs = jnp.where(even, q_sum, p_sum).astype(BF16)
        mine = (mine + named(theirs, "band", 1)).astype(BF16)
        bit = 2
        while bit < bands:
            mine = (mine.astype(F32) + named(mine, "band", bit)).astype(BF16)
            bit *= 2
        halves += [mine, flip(mine, "band", 1)]
    merge_grad, qkv_grad, out_grad, gain_grad = pl.pallas_call(
        final_kernel,
        out_shape=(
            shape(1, 2 * rows, feature, dtype=F32), shape(1, rows, 3 * feature, dtype=F32),
            shape(1, rows, feature, dtype=F32), shape(1, rows, dtype=F32),
        ),
        in_specs=[VMEM] * len(halves),
        out_specs=(VMEM,) * 4,
        name="unpack",
    )(*halves)
    return (section_out, merge_grad, qkv_grad, out_grad, gain_grad)


def solution(mesh):
    return jax.shard_map(
        body,
        mesh=mesh,
        in_specs=(
            P("dp", None, "band", None, None),
            P("dp", None, "band", None),
            P("segment", "dp", None),
            P("segment", "dp", None),
            P("segment", "dp", None),
            P("segment", "dp"),
            P("dp", None, "band", None, None),
        ),
        out_specs=(
            P("segment", "dp", None, "band", None, None),
            P("segment", "dp", None),
            P("segment", "dp", None),
            P("segment", "dp", None),
            P("segment", "dp"),
        ),
        check_vma=False,
    )
```

```python
import jax
import jax.numpy as jnp
from jax import lax
from jax.experimental import pallas as pl
from jax.experimental.pallas import tpu as pltpu
from jax.sharding import PartitionSpec as P


HEADS = 8
WH = 8
WW = 16
SH = 4
SW = 8
PAD = 16
CHUNKS = 2

EPSILON = 1e-05
MASKED = -1e30


F32 = jnp.float32
BF16 = jnp.bfloat16


def dot(a, b):
    return lax.dot_general(a, b, (((1,), (0,)), ((), ())), preferred_element_type=F32)


def dot_nt(a, b):
    return lax.dot_general(a, b, (((1,), (1,)), ((), ())), preferred_element_type=F32)


def dot_tn(a, b):
    return lax.dot_general(a, b, (((0,), (0,)), ((), ())), preferred_element_type=F32)


class Copies:
    def __init__(self, sems):
        self.sems = sems
        self.used = 0

    def start(self, src, dst):
        copy = pltpu.make_async_copy(src, dst, self.sems.at[self.used])
        self.used += 1
        copy.start()
        return copy


def wait_all(copies):
    for copy in copies:
        copy.wait()


def layout(feature, shards):
    rows = feature // shards
    part = rows // 2
    first = {"merge": (0, rows), "q": (rows, rows), "gain": (2 * rows, PAD), "k0": (2 * rows + PAD, part)}
    second = {"k1": (0, part), "v": (part, rows), "out": (part + rows, rows), "pad": (part + 2 * rows, PAD)}
    return (first, second, 2 * rows + part + PAD)


def load_weights(copies, pieces, names, dst):
    me = lax.axis_index("dp")
    shards = 4
    started = {}
    for name in names:
        kind, column = WHERE[name]
        arrays = pieces[kind]
        started[name] = []
        for flip, ref in zip((0, 1, shards // 2, shards - 1), arrays):
            rows = dst[name].shape[0] // shards
            at = pl.multiple_of((me ^ flip) * rows, rows)
            if kind == "rest":
                base = 0 if name == "out" else ref.shape[0] - PAD
                source = ref.at[pl.ds(base, rows)]
            elif kind == "qkv":
                width = dst[name].shape[1]
                source = ref.at[:, pl.ds(column * width, width)]
            else:
                source = ref
            started[name].append(copies.start(source, dst[name].at[pl.ds(at, rows)]))
    return started


WHERE = {
    "merge": ("merge", 0), "q": ("qkv", 0), "k": ("qkv", 1), "v": ("qkv", 2),
    "out": ("rest", 0), "gain": ("rest", 1),
}


def pieces_of(refs):
    return {"merge": refs[0:4], "qkv": refs[4:8], "rest": refs[8:12]}


def load_tokens(copies, moved, own, dst):
    started = []
    for m in range(moved.shape[0]):
        part = moved.shape[1]
        size = own.shape[1]
        started.append(copies.start(moved.at[m], dst.at[pl.ds(m * size, part)]))
        started.append(
            copies.start(
                own.at[m, pl.ds(0, size - part)], dst.at[pl.ds(m * size + part, size - part)]
            )
        )
    return started


def full_gain(gain, shards):
    feature = gain.shape[1]
    rows = feature // shards
    parts = [gain[i * PAD : i * PAD + 1, :rows] for i in range(shards)]
    return jnp.concatenate(parts, axis=1).astype(F32)


def window_allowed(mask_row, first_band, lon_count):
    cells = mask_row.shape[1]
    query = lax.broadcasted_iota(jnp.int32, (cells, cells), 0)
    key = lax.broadcasted_iota(jnp.int32, (cells, cells), 1)
    lon_same = (query % lon_count + SW) // WW == (key % lon_count + SW) // WW
    lat_same = (query // lon_count) // SH == (key // lon_count) // SH
    inside = lon_same & (lat_same | jnp.logical_not(first_band))
    usable = jnp.broadcast_to(mask_row, (cells, cells)) == 1
    return inside & (usable | (query == key))


def stacked_heads(pair, head_dim):
    lane = lax.broadcasted_iota(jnp.int32, pair.shape, 1)
    zero = jnp.zeros_like(pair)
    return jnp.concatenate(
        [jnp.where(lane < head_dim, pair, zero), jnp.where(lane < head_dim, zero, pair)], axis=0
    )


def unstacked_heads(stacked, head_dim):
    cells = stacked.shape[0] // 2
    low, high = stacked[:cells], stacked[cells:]
    lane = lax.broadcasted_iota(jnp.int32, low.shape, 1)
    return jnp.where(lane < head_dim, low, high)


def probabilities(scores, allowed2, head_dim):
    scores = jnp.where(allowed2, scores * head_dim ** (-0.5), MASKED)
    weights = jnp.exp(scores - jnp.max(scores, axis=-1, keepdims=True))
    return weights * (1.0 / jnp.sum(weights, axis=-1, keepdims=True))


def masks(mask, first_band, lon_count):
    out = []
    for m in range(mask.shape[0]):
        allowed = window_allowed(mask[m : m + 1, :], first_band, lon_count)
        out.append(jnp.concatenate([allowed, allowed], axis=0))
    return out


def pairs(micro, cells, feature):
    lanes = 2 * (feature // HEADS)
    count = feature // lanes
    rows = slice(micro * cells, (micro + 1) * cells)
    return [(micro * count + p, rows, p * lanes, lanes) for p in range(count)]


def part_of(qkv, which, rows, at, lanes):
    feature = qkv.shape[1] // 3
    return qkv[rows, which * feature + at : which * feature + at + lanes]


def attend(qkv, mix, probs, allowed, mask_shape, feature):
    head_dim = feature // HEADS
    for m in range(mask_shape[0]):
        group = pairs(m, mask_shape[1], feature)
        scores = [
            dot_nt(stacked_heads(part_of(qkv, 0, *where), head_dim), part_of(qkv, 1, *where))
            for _, *where in group
        ]
        for (n, *_), score in zip(group, scores):
            probs[n] = probabilities(score, allowed[m], head_dim).astype(BF16)
        for n, rows, at, lanes in group:
            mixed = dot(probs[n], part_of(qkv, 2, rows, at, lanes))
            mix[rows, at : at + lanes] = unstacked_heads(mixed, head_dim).astype(BF16)


def attend_back(qkv, probs, grad_mix, grad_proj, mask_shape, feature):
    head_dim = feature // HEADS

    def put(which, grad, rows, at, lanes):
        grad_proj[rows, which * feature + at : which * feature + at + lanes] = grad.astype(BF16)

    for m in range(mask_shape[0]):
        group = pairs(m, mask_shape[1], feature)
        grad_probs = []
        for n, rows, at, lanes in group:
            g_stack = stacked_heads(grad_mix[rows, at : at + lanes], head_dim)
            grad_probs.append(dot_nt(g_stack, part_of(qkv, 2, rows, at, lanes)))
            put(2, dot_tn(probs[n], g_stack), rows, at, lanes)
        grad_scores = []
        for (n, *_), grad in zip(group, grad_probs):
            prob = probs[n].astype(F32)
            inner = jnp.sum(grad * prob, axis=-1, keepdims=True)
            grad_scores.append((prob * (grad - inner) * head_dim ** (-0.5)).astype(BF16))
        for (n, rows, at, lanes), grad in zip(group, grad_scores):
            q_stack = stacked_heads(part_of(qkv, 0, rows, at, lanes), head_dim)
            put(0, unstacked_heads(dot(grad, part_of(qkv, 1, rows, at, lanes)), head_dim), rows, at, lanes)
            put(1, dot_tn(grad, q_stack), rows, at, lanes)


def normalize(update):
    average = jnp.mean(update, axis=-1, keepdims=True)
    centered = update - average
    spread = jnp.mean(centered * centered, axis=-1, keepdims=True)
    inverse = lax.rsqrt(spread + EPSILON)
    return (centered * inverse, inverse)


def forward(x, w, waits, gain_of, allowed, mask_shape, room, kept):
    feature = x.shape[1]
    wait_all(waits["merge"])
    tokens = x[...]
    update = dot(tokens, w["merge"][:feature]) + dot(tokens, w["merge"][feature:])
    normed, inverse = normalize(update)
    room["normed"][...] = normed
    kept("normed")
    room["inverse"][...] = jnp.broadcast_to(inverse, room["inverse"].shape)
    kept("inverse")
    hidden, qkv, mix = room["hidden"], room["qkv"], room["mix"]
    hidden[...] = (normed * gain_of()).astype(BF16)
    kept("hidden")
    for i, name in enumerate(("q", "k", "v")):
        wait_all(waits[name])
        qkv[:, i * feature : (i + 1) * feature] = dot(hidden[...], w[name][...]).astype(BF16)
    kept("qkv")
    attend(qkv, mix, room["probs"], allowed, mask_shape, feature)
    kept("probs")
    kept("mix")
    wait_all(waits["out"])
    return update + dot(mix[...], w["out"][...])


RECORDS = ("normed", "inverse", "hidden", "qkv", "mix", "probs")


def backward(grad_out, w, gain, mask_shape, room, grad_mix, grad_proj):
    feature = grad_out.shape[1]
    grad_mix[...] = dot_nt(grad_out[...], w["out"][...]).astype(BF16)
    attend_back(room["qkv"], room["probs"], grad_mix, grad_proj, mask_shape, feature)
    grad_hidden = sum(
        dot_nt(grad_proj[:, i * feature : (i + 1) * feature], w[name][...])
        for i, name in enumerate(("q", "k", "v"))
    )
    normed, inverse = room["normed"][...], room["inverse"]
    grad_gain = jnp.sum(grad_hidden * normed, axis=0, keepdims=True)
    grad_normed = grad_hidden * gain
    centered = (
        grad_normed
        - jnp.mean(grad_normed, axis=-1, keepdims=True)
        - normed * jnp.mean(grad_normed * normed, axis=-1, keepdims=True)
    )
    grad_update = grad_out[...].astype(F32) + inverse[:, :1] * centered
    return (grad_update.astype(BF16), grad_gain)


def send_grads(copies, x, hidden, mix, grad_out, grad_proj, grad_update, grad_gain, dw, outs):
    feature = x.shape[1]
    shards = 2 * outs[0].shape[0]
    first, second, half = layout(feature, shards)
    me = lax.axis_index("dp")
    low, high = me % 2, me // 2
    rows = feature // shards
    width = feature // CHUNKS
    dw_first, dw_second = dw
    started = []

    def put(name, value, row_of):
        block = dw_first if name in first else dw_second
        start, size = first[name] if name in first else second[name]
        for i in range(shards):
            block[i, start : start + size, :] = value[row_of(i) : row_of(i) + size]

    def emit(which, start, size):
        block = (dw_first, dw_second)[which]
        for chunk in range(CHUNKS):
            p_keep, p_send, q_keep, q_send = outs[4 * chunk : 4 * chunk + 4]
            for by_high in range(2):
                for by_low in range(2):
                    owner = (high ^ by_high) * 2 + (low ^ by_low)
                    if which:
                        ref = (q_send if by_low else q_keep).at[by_high]
                    else:
                        ref = (p_send if by_high else p_keep).at[by_low]
                    part = block.at[owner, pl.ds(start, size), pl.ds(chunk * width, width)]
                    started.append(copies.start(part, ref.at[pl.ds(start, size)]))

    def of_projection(i):
        part = grad_proj[:, i * feature : (i + 1) * feature]
        return dot_tn(hidden[...], part).astype(BF16)

    put("out", dot_tn(mix[...], grad_out[...]).astype(BF16), lambda i: i * rows)
    grad_k = of_projection(1)
    put("k1", grad_k, lambda i: i * rows + rows // 2)
    put("v", of_projection(2), lambda i: i * rows)
    dw_second[:, second["pad"][0] :, :] = jnp.zeros((shards, PAD, feature), BF16)
    emit(1, 0, half)
    put("k0", grad_k, lambda i: i * rows)
    put("q", of_projection(0), lambda i: i * rows)
    start = first["gain"][0]
    for i in range(shards):
        part = grad_gain[:, i * rows : (i + 1) * rows].astype(BF16)
        dw_first[i, start : start + PAD, :] = jnp.zeros((PAD, feature), BF16)
        dw_first[i, start : start + PAD, :rows] = jnp.broadcast_to(part, (PAD, rows))
    emit(0, first["q"][0], half - first["q"][0])
    put("merge", dot_tn(x[...], grad_update[...]).astype(BF16),
        lambda i: (i % 2) * 2 * rows + (i // 2) * rows)
    emit(0, 0, first["merge"][1])
    return started


def lon_of(cells):
    return cells // WH


def role(segment):
    return pl.when(lax.axis_index("segment") == segment)


def forward_kernel(*refs):
    mask_in, moved, own, *rest = refs
    pieces, rest = rest[:12], rest[12:]
    y, rest = rest[0], rest[1:]
    saved, rest = dict(zip(RECORDS, rest)), rest[len(RECORDS) :]
    mask, x, wm, wq, wk, wv, wo, wg, y_s, *rest = rest
    room, sems = dict(zip(RECORDS, rest)), rest[-1]

    @role(0)
    def run():
        shards = wg.shape[0] // PAD
        copies = Copies(sems)
        w = {"merge": wm, "q": wq, "k": wk, "v": wv, "out": wo, "gain": wg}
        mask_copy = copies.start(mask_in, mask)
        tokens = load_tokens(copies, moved, own, x)
        names = ("merge", "gain", "q", "k", "v", "out")
        waits = load_weights(copies, pieces_of(pieces), names, w)
        mask_copy.wait()
        allowed = masks(mask, lax.axis_index("band") == 0, lon_of(mask.shape[1]))
        wait_all(tokens)

        def gain_of():
            wait_all(waits["gain"])
            return full_gain(wg, shards)

        done = []

        def kept(name):
            done.append(copies.start(room[name], saved[name]))

        result = forward(x, w, waits, gain_of, allowed, mask.shape, room, kept)
        y_s[...] = result.astype(BF16)
        done.append(copies.start(y_s, y))
        wait_all(done)


def last_kernel(*refs):
    mask_in, moved, own, y0, *rest = refs
    pieces, rest = rest[:12], rest[13:]
    y, g0, gain_out, g_out, hidden, mix, proj_out, update_out, *rest = rest
    mask, x, g, wm, wq, wk, wv, wo, wg, y_s, g_s, *rest = rest
    room, rest = dict(zip(RECORDS, rest)), rest[len(RECORDS) :]
    gmix, gproj, gain_s, update_s, sems = rest

    @role(1)
    def run():
        shards = wg.shape[0] // PAD
        feature = x.shape[1]
        copies = Copies(sems)
        w = {"merge": wm, "q": wq, "k": wk, "v": wv, "out": wo, "gain": wg}
        mask_copy = copies.start(mask_in, mask)
        x_in = copies.start(y0, x)
        names = ("merge", "gain", "q", "k", "v", "out")
        waits = load_weights(copies, pieces_of(pieces), names, w)
        tokens = load_tokens(copies, moved, own, g)
        mask_copy.wait()
        allowed = masks(mask, lax.axis_index("band") == 0, lon_of(mask.shape[1]))
        x_in.wait()

        def gain_of():
            wait_all(waits["gain"])
            return full_gain(wg, shards)

        done = []

        def kept(name):
            if name in ("hidden", "mix"):
                done.append(copies.start(room[name], hidden if name == "hidden" else mix))

        result = forward(x, w, waits, gain_of, allowed, mask.shape, room, kept)
        y_s[...] = result.astype(BF16)
        wait_all(tokens)
        done += [copies.start(y_s, y), copies.start(g, g_out)]
        grad_update, grad_gain = backward(g, w, full_gain(wg, shards), mask.shape, room, gmix, gproj)
        done.append(copies.start(gproj, proj_out))
        gain_s[...] = jnp.broadcast_to(grad_gain, gain_s.shape)
        update_s[...] = grad_update
        done += [copies.start(gain_s, gain_out), copies.start(update_s, update_out)]
        chain = dot_nt(grad_update, wm[:feature]).astype(BF16).astype(F32)
        side = dot_nt(grad_update, wm[feature:]).astype(BF16).astype(F32)
        g_s[...] = (chain + side).astype(BF16)
        done.append(copies.start(g_s, g0))
        wait_all(done)


def weight_kernel(*refs):
    ins, outs, rest = refs[:7], refs[7 : 7 + 4 * CHUNKS], refs[7 + 4 * CHUNKS :]
    scratch, dw, sems = rest[:7], rest[7:9], rest[9]

    @role(1)
    def run():
        copies = Copies(sems)
        wait_all([copies.start(a, b) for a, b in zip(ins, scratch)])
        x, gain, g, hidden, mix, gproj, update = scratch
        wait_all(send_grads(copies, x, hidden, mix, g, gproj, update, gain[:1, :], dw, outs))


def first_kernel(*refs):
    cells, moved, own, g0, *rest = refs
    pieces, rest = rest[:12], rest[12:]
    saved, rest = rest[: len(RECORDS)], rest[len(RECORDS) :]
    skip = count = 4 * CHUNKS
    outs, rest = rest[skip : skip + count], rest[skip + count :]
    x, g, wq, wk, wv, wo, wg, *rest = rest
    rooms, rest = rest[: len(RECORDS)], rest[len(RECORDS) :]
    gmix, gproj, dw_first, dw_second, sems = rest

    @role(0)
    def run():
        shards = wg.shape[0] // PAD
        micro, size = own.shape[:2]
        copies = Copies(sems)
        w = {"q": wq, "k": wk, "v": wv, "out": wo, "gain": wg}
        early = [copies.start(g0, g)]
        names = ("out", "q", "k", "v", "gain")
        waits = load_weights(copies, pieces_of(pieces), names, w)
        early += [copies.start(a, b) for a, b in zip(saved, rooms)]
        early += load_tokens(copies, moved, own, x)
        wait_all(early)
        for name in names:
            wait_all(waits[name])
        room = dict(zip(RECORDS, rooms))
        grad_update, grad_gain = backward(g, w, full_gain(wg, shards), (micro, size), room, gmix, gproj)
        wait_all(send_grads(copies, x, room["hidden"], room["mix"], g, gproj, grad_update, grad_gain,
                            (dw_first, dw_second), outs))


def rest_kernel(out, gain, packed):
    rows, width = gain.shape[1], out.shape[1]
    packed[: out.shape[0], :] = out[...]
    packed[out.shape[0] :, :] = jnp.zeros((PAD, width), BF16)
    packed[out.shape[0] :, :rows] = jnp.broadcast_to(gain[...], (PAD, rows))


def final_kernel(*refs):
    halves, (near, far), (merge, qkv, out, gain) = refs[: 4 * CHUNKS], refs[4 * CHUNKS : -4], refs[-4:]
    feature = merge.shape[2]
    size = qkv.shape[1]
    first, second, _ = layout(feature, feature // size)
    even = lax.axis_index("band") % 2 == 0
    upper = lax.axis_index("dp") >= feature // size // 2
    width = feature // CHUNKS

    def chosen(mine, theirs, side):
        a, b = (theirs, mine) if side else (mine, theirs)
        return jnp.where(even, a.astype(F32), b.astype(F32))

    def rows(name, chunk, side):
        which = 0 if name in first else 1
        own, other = halves[4 * chunk + 2 * which : 4 * chunk + 2 * which + 2]
        start, count = (second if which else first)[name]
        return chosen(own[start : start + count, :], other[start : start + count, :], side)

    for chunk in range(CHUNKS):
        for side in range(2):
            low = chunk * width + side * (width // 2)
            high = low + width // 2
            piece = slice(chunk * width // 2, (chunk + 1) * width // 2)
            here, there = rows("merge", chunk, side), chosen(near[:, piece], far[:, piece], side)
            merge[0, :size, low:high] = jnp.where(upper, there, here)
            merge[0, size:, low:high] = jnp.where(upper, here, there)
            for i, (name, begin, count) in enumerate(
                (("q", 0, size), ("k0", 0, size // 2), ("k1", size // 2, size // 2), ("v", 0, size))
            ):
                at = (0, 1, 1, 2)[i] * feature
                qkv[0, begin : begin + count, at + low : at + high] = rows(name, chunk, side)
            out[0, :, low:high] = rows("out", chunk, side)
    gain[...] = rows("gain", 0, 0)[:1, : gain.shape[1]]


ANY = pl.BlockSpec(memory_space=pl.ANY)
VMEM = pl.BlockSpec(memory_space=pltpu.VMEM)


def call(kernel, ins, outs, scratch, aliases, flops):
    moved = sum(a.size * a.dtype.itemsize for a in list(ins) + list(outs))
    return pl.pallas_call(
        kernel,
        out_shape=tuple(outs),
        in_specs=[ANY] * len(ins),
        out_specs=tuple([ANY] * len(outs)),
        scratch_shapes=scratch,
        input_output_aliases=aliases,
        cost_estimate=pl.CostEstimate(flops=flops, bytes_accessed=moved, transcendentals=0),
    )(*ins)


def flip(value, axis, bit):
    size = lax.axis_size(axis)
    return lax.ppermute(value, axis, [(i, i ^ bit) for i in range(size)])


def gather(merge, qkv, rest):
    high = lax.axis_size("dp") // 2

    def named(value, bit):
        return flip(value, "dp", bit)

    merge_low, merge_high = named(merge, 1), named(merge, high)
    qkv_low, qkv_high = named(qkv, 1), named(qkv, high)
    rest_low, rest_high = named(rest, 1), named(rest, high)
    merge_both = named(merge_low, high)
    qkv_both = named(qkv_high, 1)
    rest_both = named(rest_low, high)
    return (merge, merge_low, merge_high, merge_both, qkv, qkv_low, qkv_high, qkv_both,
            rest, rest_low, rest_high, rest_both)


def body(fields, cell_mask, merge_weight, qkv_weight, out_weight, norm_gain, out_cotangent):
    _, micro, row_count, lon_count, feature = fields.shape
    shards, bands = lax.axis_size("dp"), lax.axis_size("band")
    assert lax.axis_size("segment") == 2 and row_count == WH and shards == 4
    segment, band = lax.axis_index("segment"), lax.axis_index("band")
    cells = row_count * lon_count
    total = micro * cells
    _, _, half = layout(feature, shards)
    rows = feature // shards

    def shape(*dims, dtype=BF16):
        return jax.ShapeDtypeStruct(dims, dtype)

    def room(*dims, dtype=BF16):
        return pltpu.VMEM(dims, dtype)

    merge, qkv, out = merge_weight[0], qkv_weight[0], out_weight[0]
    rest = pl.pallas_call(
        rest_kernel,
        out_shape=shape(rows + PAD, feature),
        in_specs=[VMEM, VMEM],
        out_specs=VMEM,
        name="pack",
    )(out, norm_gain)
    pieces = gather(merge, qkv, rest)

    down = [(i, (i + 1) % bands) for i in range(bands)]
    up = [(j, i) for i, j in down]
    flat = (micro, cells, feature)
    source = jnp.where(segment == 0, fields[0, :, row_count - SH :], out_cotangent[0, :, row_count - SH :])
    moved = lax.ppermute(source, "band", down)
    moved = moved.reshape(micro, SH * lon_count, feature)
    mask_moved = lax.ppermute(cell_mask[0, :, row_count - SH :], "band", down)
    mask = jnp.concatenate([mask_moved, cell_mask[0, :, : row_count - SH]], axis=1).reshape(micro, cells)
    own_fields = fields.reshape(flat)
    own_cotangent = out_cotangent.reshape(flat)

    square = room(feature, feature)
    tokens = room(total, feature)
    wide = room(total, 3 * feature)
    mask_room = pltpu.VMEM((micro, cells), jnp.int32)
    weights = [square] * 4 + [room(shards * PAD, feature)]
    merge_room = room(2 * feature, feature)
    record_rooms = [
        room(total, feature, dtype=F32), room(total, 128, dtype=F32), tokens, wide, tokens,
        room(micro * HEADS // 2, 2 * cells, cells),
    ]
    grad_rooms = [room(shards, half, feature)] * 2
    sems = [pltpu.SemaphoreType.DMA((128,))]
    unit = 2 * total * feature * feature
    token_shape, wide_shape = shape(total, feature), shape(total, 3 * feature)

    y, *records = call(
        forward_kernel,
        (mask, moved, own_fields) + pieces,
        [token_shape, shape(total, feature, dtype=F32), shape(total, 128, dtype=F32),
         token_shape, wide_shape, token_shape, shape(micro * HEADS // 2, 2 * cells, cells)],
        [mask_room, tokens, merge_room] + weights + [tokens] + record_rooms + sems,
        {}, 6 * unit,
    )
    y0 = lax.ppermute(y, "segment", [(0, 1)])
    gain_room = room(8, feature, dtype=F32)
    y, g_out, *operands = call(
        last_kernel,
        (mask, moved, own_cotangent, y0) + pieces + (y,),
        [token_shape, token_shape, shape(8, feature, dtype=F32), token_shape, token_shape, token_shape,
         wide_shape, token_shape],
        [mask_room, tokens, tokens, merge_room] + weights + [tokens, tokens] + record_rooms
        + [tokens, wide, gain_room, tokens] + sems,
        {16: 0}, 13 * unit,
    )
    g0 = lax.ppermute(g_out, "segment", [(1, 0)])
    shard_shapes = [shape(2, half, feature // CHUNKS)] * (4 * CHUNKS)
    grads = call(
        weight_kernel,
        (y0,) + tuple(operands),
        shard_shapes,
        [tokens, gain_room, tokens, tokens, tokens, wide, tokens] + grad_rooms + sems,
        {}, 5 * unit,
    )

    y = y.reshape(micro, cells, feature)
    part = SH * lon_count
    back = lax.ppermute(y[:, :part], "band", up)
    section_out = jnp.concatenate([y[:, part:], back], axis=1)
    section_out = section_out.reshape(1, 1, micro, row_count, lon_count, feature)

    inputs = (mask, moved, own_fields, g0) + pieces + tuple(records)
    grads = call(
        first_kernel,
        inputs + tuple(grads),
        shard_shapes,
        [tokens, tokens] + weights + record_rooms + [tokens, wide] + grad_rooms + sems,
        {len(inputs) + i: i for i in range(4 * CHUNKS)}, 12 * unit,
    )

    high = shards // 2
    even = band % 2 == 0
    side = feature // CHUNKS // 2
    halves = []

    def named(value, axis, bit):
        return flip(value, axis, bit).astype(F32)

    for chunk in range(CHUNKS):
        for which, bits in (("p", (high, 1)), ("q", (1, high))):
            keep, send = grads[4 * chunk + 2 * (which == "q") :][:2]
            got = named(send, "dp", bits[0])
            on = (keep[1].astype(F32) + got[1]).astype(BF16)
            total_here = keep[0].astype(F32) + got[0] + named(on, "dp", bits[1])
            left, right = total_here[:, :side], total_here[:, side:]
            mine = jnp.where(even, left, right)
            theirs = jnp.where(even, right, left).astype(BF16)
            mine = (mine + named(theirs, "band", 1)).astype(BF16)
            bit = 2
            while bit < bands:
                mine = (mine.astype(F32) + named(mine, "band", bit)).astype(BF16)
                bit *= 2
            halves += [mine, flip(mine, "band", 1)]
    pieces = jnp.concatenate([halves[4 * chunk][:rows] for chunk in range(CHUNKS)], axis=1)
    pairs_far = [
        (i * bands + j, (i ^ high) * bands + (j ^ 1)) for i in range(shards) for j in range(bands)
    ]
    halves.append(flip(pieces, "dp", high))
    halves.append(lax.ppermute(pieces, ("dp", "band"), pairs_far))
    merge_grad, qkv_grad, out_grad, gain_grad = pl.pallas_call(
        final_kernel,
        out_shape=(
            shape(1, 2 * rows, feature, dtype=F32), shape(1, rows, 3 * feature, dtype=F32),
            shape(1, rows, feature, dtype=F32), shape(1, rows, dtype=F32),
        ),
        in_specs=[VMEM] * len(halves),
        out_specs=(VMEM,) * 4,
        name="unpack",
    )(*halves)
    return (section_out, merge_grad, qkv_grad, out_grad, gain_grad)


def solution(mesh):
    return jax.shard_map(
        body,
        mesh=mesh,
        in_specs=(
            P("dp", None, "band", None, None),
            P("dp", None, "band", None),
            P("segment", "dp", None),
            P("segment", "dp", None),
            P("segment", "dp", None),
            P("segment", "dp"),
            P("dp", None, "band", None, None),
        ),
        out_specs=(
            P("segment", "dp", None, "band", None, None),
            P("segment", "dp", None),
            P("segment", "dp", None),
            P("segment", "dp", None),
            P("segment", "dp"),
        ),
        check_vma=False,
    )
```

```python
import jax
import jax.numpy as jnp
from jax import lax
from jax.experimental import pallas as pl
from jax.experimental.pallas import tpu as pltpu
from jax.sharding import PartitionSpec as P


HEADS = 8
WH = 8
WW = 16
SH = 4
SW = 8
PAD = 16
CHUNKS = 2

EPSILON = 1e-05
MASKED = -1e30


F32 = jnp.float32
BF16 = jnp.bfloat16


def dot(a, b):
    return lax.dot_general(a, b, (((1,), (0,)), ((), ())), preferred_element_type=F32)


def dot_nt(a, b):
    return lax.dot_general(a, b, (((1,), (1,)), ((), ())), preferred_element_type=F32)


def dot_tn(a, b):
    return lax.dot_general(a, b, (((0,), (0,)), ((), ())), preferred_element_type=F32)


class Copies:
    def __init__(self, sems):
        self.sems = sems
        self.used = 0

    def start(self, src, dst):
        copy = pltpu.make_async_copy(src, dst, self.sems.at[self.used])
        self.used += 1
        copy.start()
        return copy


def wait_all(copies):
    for copy in copies:
        copy.wait()


def layout(feature, shards):
    rows = feature // shards
    part = rows // 2
    first = {"merge": (0, rows), "q": (rows, rows), "gain": (2 * rows, PAD), "k0": (2 * rows + PAD, part)}
    second = {"k1": (0, part), "v": (part, rows), "out": (part + rows, rows), "pad": (part + 2 * rows, PAD)}
    return (first, second, 2 * rows + part + PAD)


def load_weights(copies, pieces, names, dst):
    me = lax.axis_index("dp")
    shards = len(pieces) // 2
    started = {}
    for name in names:
        kind, column = WHERE[name]
        arrays = pieces[:shards] if kind == "qkv" else pieces[shards:]
        started[name] = []
        for flip, ref in zip((0, 1, shards // 2, shards - 1), arrays):
            owner = me ^ flip
            rows = dst[name].shape[0] // shards
            if name == "merge":
                owner = (owner % 2) * (shards // 2) + owner // 2
            at = pl.multiple_of(owner * rows, rows)
            if kind == "rest":
                source = ref.at[pl.ds(column * ((ref.shape[0] - PAD) // 2), rows)]
            else:
                width = dst[name].shape[1]
                source = ref.at[:, pl.ds(column * width, width)]
            started[name].append(copies.start(source, dst[name].at[pl.ds(at, rows)]))
    return started


WHERE = {
    "q": ("qkv", 0), "k": ("qkv", 1), "v": ("qkv", 2),
    "merge": ("rest", 0), "out": ("rest", 1), "gain": ("rest", 2),
}


def load_tokens(copies, moved, own, dst):
    started = []
    for m in range(moved.shape[0]):
        part = moved.shape[1]
        size = own.shape[1]
        started.append(copies.start(moved.at[m], dst.at[pl.ds(m * size, part)]))
        started.append(
            copies.start(
                own.at[m, pl.ds(0, size - part)], dst.at[pl.ds(m * size + part, size - part)]
            )
        )
    return started


def full_gain(gain, shards):
    feature = gain.shape[1]
    rows = feature // shards
    parts = [gain[i * PAD : i * PAD + 1, :rows] for i in range(shards)]
    return jnp.concatenate(parts, axis=1).astype(F32)


def window_allowed(mask_row, first_band, lon_count):
    cells = mask_row.shape[1]
    query = lax.broadcasted_iota(jnp.int32, (cells, cells), 0)
    key = lax.broadcasted_iota(jnp.int32, (cells, cells), 1)
    lon_same = (query % lon_count + SW) // WW == (key % lon_count + SW) // WW
    lat_same = (query // lon_count) // SH == (key // lon_count) // SH
    inside = lon_same & (lat_same | jnp.logical_not(first_band))
    usable = jnp.broadcast_to(mask_row, (cells, cells)) == 1
    return inside & (usable | (query == key))


def stacked_heads(pair, head_dim):
    lane = lax.broadcasted_iota(jnp.int32, pair.shape, 1)
    zero = jnp.zeros_like(pair)
    return jnp.concatenate(
        [jnp.where(lane < head_dim, pair, zero), jnp.where(lane < head_dim, zero, pair)], axis=0
    )


def unstacked_heads(stacked, head_dim):
    cells = stacked.shape[0] // 2
    low, high = stacked[:cells], stacked[cells:]
    lane = lax.broadcasted_iota(jnp.int32, low.shape, 1)
    return jnp.where(lane < head_dim, low, high)


def probabilities(scores, allowed2, head_dim):
    scores = jnp.where(allowed2, scores * head_dim ** (-0.5), MASKED)
    weights = jnp.exp(scores - jnp.max(scores, axis=-1, keepdims=True))
    return weights * (1.0 / jnp.sum(weights, axis=-1, keepdims=True))


def masks(mask, first_band, lon_count):
    out = []
    for m in range(mask.shape[0]):
        allowed = window_allowed(mask[m : m + 1, :], first_band, lon_count)
        out.append(jnp.concatenate([allowed, allowed], axis=0))
    return out


def pairs(micro, cells, feature):
    lanes = 2 * (feature // HEADS)
    count = feature // lanes
    rows = slice(micro * cells, (micro + 1) * cells)
    return [(micro * count + p, rows, p * lanes, lanes) for p in range(count)]


def part_of(qkv, which, rows, at, lanes):
    feature = qkv.shape[1] // 3
    return qkv[rows, which * feature + at : which * feature + at + lanes]


def attend(qkv, mix, probs, allowed, mask_shape, feature):
    head_dim = feature // HEADS
    for m in range(mask_shape[0]):
        group = pairs(m, mask_shape[1], feature)
        scores = [
            dot_nt(stacked_heads(part_of(qkv, 0, *where), head_dim), part_of(qkv, 1, *where))
            for _, *where in group
        ]
        for (n, *_), score in zip(group, scores):
            probs[n] = probabilities(score, allowed[m], head_dim).astype(BF16)
        for n, rows, at, lanes in group:
            mixed = dot(probs[n], part_of(qkv, 2, rows, at, lanes))
            mix[rows, at : at + lanes] = unstacked_heads(mixed, head_dim).astype(BF16)


def attend_back(qkv, probs, grad_mix, grad_proj, mask_shape, feature):
    head_dim = feature // HEADS

    def put(which, grad, rows, at, lanes):
        grad_proj[rows, which * feature + at : which * feature + at + lanes] = grad.astype(BF16)

    for m in range(mask_shape[0]):
        group = pairs(m, mask_shape[1], feature)
        grad_probs = []
        for n, rows, at, lanes in group:
            g_stack = stacked_heads(grad_mix[rows, at : at + lanes], head_dim)
            grad_probs.append(dot_nt(g_stack, part_of(qkv, 2, rows, at, lanes)))
            put(2, dot_tn(probs[n], g_stack), rows, at, lanes)
        grad_scores = []
        for (n, *_), grad in zip(group, grad_probs):
            prob = probs[n].astype(F32)
            inner = jnp.sum(grad * prob, axis=-1, keepdims=True)
            grad_scores.append((prob * (grad - inner) * head_dim ** (-0.5)).astype(BF16))
        for (n, rows, at, lanes), grad in zip(group, grad_scores):
            q_stack = stacked_heads(part_of(qkv, 0, rows, at, lanes), head_dim)
            put(0, unstacked_heads(dot(grad, part_of(qkv, 1, rows, at, lanes)), head_dim), rows, at, lanes)
            put(1, dot_tn(grad, q_stack), rows, at, lanes)


def normalize(update):
    average = jnp.mean(update, axis=-1, keepdims=True)
    centered = update - average
    spread = jnp.mean(centered * centered, axis=-1, keepdims=True)
    inverse = lax.rsqrt(spread + EPSILON)
    return (centered * inverse, inverse)


def forward(x, w, waits, gain_of, allowed, mask_shape, room, kept):
    feature = x.shape[1]
    wait_all(waits["merge"])
    update = dot(x[...], w["merge"][...])
    normed, inverse = normalize(update)
    room["normed"][...] = normed
    kept("normed")
    room["inverse"][...] = jnp.broadcast_to(inverse, room["inverse"].shape)
    kept("inverse")
    hidden, qkv, mix = room["hidden"], room["qkv"], room["mix"]
    hidden[...] = (normed * gain_of()).astype(BF16)
    kept("hidden")
    for i, name in enumerate(("q", "k", "v")):
        wait_all(waits[name])
        qkv[:, i * feature : (i + 1) * feature] = dot(hidden[...], w[name][...]).astype(BF16)
    kept("qkv")
    attend(qkv, mix, room["probs"], allowed, mask_shape, feature)
    kept("probs")
    kept("mix")
    wait_all(waits["out"])
    return update + dot(mix[...], w["out"][...])


RECORDS = ("normed", "inverse", "hidden", "qkv", "mix", "probs")


def backward(grad_out, w, gain, mask_shape, room, grad_mix, grad_proj):
    feature = grad_out.shape[1]
    grad_mix[...] = dot_nt(grad_out[...], w["out"][...]).astype(BF16)
    attend_back(room["qkv"], room["probs"], grad_mix, grad_proj, mask_shape, feature)
    grad_hidden = sum(
        dot_nt(grad_proj[:, i * feature : (i + 1) * feature], w[name][...])
        for i, name in enumerate(("q", "k", "v"))
    )
    normed, inverse = room["normed"][...], room["inverse"]
    grad_gain = jnp.sum(grad_hidden * normed, axis=0, keepdims=True)
    grad_normed = grad_hidden * gain
    centered = (
        grad_normed
        - jnp.mean(grad_normed, axis=-1, keepdims=True)
        - normed * jnp.mean(grad_normed * normed, axis=-1, keepdims=True)
    )
    grad_update = grad_out[...].astype(F32) + inverse[:, :1] * centered
    return (grad_update.astype(BF16), grad_gain)


def send_grads(copies, x, hidden, mix, grad_out, grad_proj, grad_update, grad_gain, dw, outs):
    feature = x.shape[1]
    shards = 2 * outs[0].shape[0]
    first, second, half = layout(feature, shards)
    me = lax.axis_index("dp")
    low, high = me % 2, me // 2
    rows = feature // shards
    width = feature // CHUNKS
    dw_first, dw_second = dw
    started = []

    def put(name, value, row_of):
        block = dw_first if name in first else dw_second
        start, size = first[name] if name in first else second[name]
        for i in range(shards):
            block[i, start : start + size, :] = value[row_of(i) : row_of(i) + size]

    def emit(which, start, size):
        block = (dw_first, dw_second)[which]
        for chunk in range(CHUNKS):
            p_keep, p_send, q_keep, q_send = outs[4 * chunk : 4 * chunk + 4]
            for by_high in range(2):
                for by_low in range(2):
                    owner = (high ^ by_high) * 2 + (low ^ by_low)
                    if which:
                        ref = (q_send if by_low else q_keep).at[by_high]
                    else:
                        ref = (p_send if by_high else p_keep).at[by_low]
                    part = block.at[owner, pl.ds(start, size), pl.ds(chunk * width, width)]
                    started.append(copies.start(part, ref.at[pl.ds(start, size)]))

    def of_projection(i):
        part = grad_proj[:, i * feature : (i + 1) * feature]
        return dot_tn(hidden[...], part).astype(BF16)

    put("out", dot_tn(mix[...], grad_out[...]).astype(BF16), lambda i: i * rows)
    grad_k = of_projection(1)
    put("k1", grad_k, lambda i: i * rows + rows // 2)
    put("v", of_projection(2), lambda i: i * rows)
    dw_second[:, second["pad"][0] :, :] = jnp.zeros((shards, PAD, feature), BF16)
    emit(1, 0, half)
    put("k0", grad_k, lambda i: i * rows)
    put("q", of_projection(0), lambda i: i * rows)
    start = first["gain"][0]
    for i in range(shards):
        part = grad_gain[:, i * rows : (i + 1) * rows].astype(BF16)
        dw_first[i, start : start + PAD, :] = jnp.zeros((PAD, feature), BF16)
        dw_first[i, start : start + PAD, :rows] = jnp.broadcast_to(part, (PAD, rows))
    emit(0, first["q"][0], half - first["q"][0])
    put("merge", dot_tn(x[...], grad_update[...]).astype(BF16),
        lambda i: (i % 2) * 2 * rows + (i // 2) * rows)
    emit(0, 0, first["merge"][1])
    return started


def lon_of(cells):
    return cells // WH


def role(segment):
    return pl.when(lax.axis_index("segment") == segment)


def forward_kernel(*refs):
    mask_in, moved, own, *rest = refs
    pieces, rest = rest[:8], rest[8:]
    y, rest = rest[0], rest[1:]
    saved, rest = dict(zip(RECORDS, rest)), rest[len(RECORDS) :]
    mask, x, wm, wq, wk, wv, wo, wg, y_s, *rest = rest
    room, sems = dict(zip(RECORDS, rest)), rest[-1]

    @role(0)
    def run():
        shards = wg.shape[0] // PAD
        copies = Copies(sems)
        w = {"merge": wm, "q": wq, "k": wk, "v": wv, "out": wo, "gain": wg}
        mask_copy = copies.start(mask_in, mask)
        tokens = load_tokens(copies, moved, own, x)
        names = ("merge", "gain", "q", "k", "v", "out")
        waits = load_weights(copies, pieces, names, w)
        mask_copy.wait()
        allowed = masks(mask, lax.axis_index("band") == 0, lon_of(mask.shape[1]))
        wait_all(tokens)

        def gain_of():
            wait_all(waits["gain"])
            return full_gain(wg, shards)

        done = []

        def kept(name):
            done.append(copies.start(room[name], saved[name]))

        result = forward(x, w, waits, gain_of, allowed, mask.shape, room, kept)
        y_s[...] = result.astype(BF16)
        done.append(copies.start(y_s, y))
        wait_all(done)


def last_kernel(*refs):
    mask_in, moved, own, y0, *rest = refs
    pieces, rest = rest[:8], rest[9:]
    y, g0, gain_out, g_out, hidden, mix, proj_out, update_out, *rest = rest
    mask, x, g, wm, wq, wk, wv, wo, wg, y_s, g_s, *rest = rest
    room, rest = dict(zip(RECORDS, rest)), rest[len(RECORDS) :]
    gmix, gproj, gain_s, update_s, sems = rest

    @role(1)
    def run():
        shards = wg.shape[0] // PAD
        copies = Copies(sems)
        w = {"merge": wm, "q": wq, "k": wk, "v": wv, "out": wo, "gain": wg}
        mask_copy = copies.start(mask_in, mask)
        x_in = copies.start(y0, x)
        names = ("merge", "gain", "q", "k", "v", "out")
        waits = load_weights(copies, pieces, names, w)
        tokens = load_tokens(copies, moved, own, g)
        mask_copy.wait()
        allowed = masks(mask, lax.axis_index("band") == 0, lon_of(mask.shape[1]))
        x_in.wait()

        def gain_of():
            wait_all(waits["gain"])
            return full_gain(wg, shards)

        done = []

        def kept(name):
            if name in ("hidden", "mix"):
                done.append(copies.start(room[name], hidden if name == "hidden" else mix))

        result = forward(x, w, waits, gain_of, allowed, mask.shape, room, kept)
        y_s[...] = result.astype(BF16)
        wait_all(tokens)
        done += [copies.start(y_s, y), copies.start(g, g_out)]
        grad_update, grad_gain = backward(g, w, full_gain(wg, shards), mask.shape, room, gmix, gproj)
        done.append(copies.start(gproj, proj_out))
        gain_s[...] = jnp.broadcast_to(grad_gain, gain_s.shape)
        update_s[...] = grad_update
        done += [copies.start(gain_s, gain_out), copies.start(update_s, update_out)]
        g_s[...] = dot_nt(grad_update, wm[...]).astype(BF16)
        done.append(copies.start(g_s, g0))
        wait_all(done)


def weight_kernel(*refs):
    ins, outs, rest = refs[:7], refs[7 : 7 + 4 * CHUNKS], refs[7 + 4 * CHUNKS :]
    scratch, dw, sems = rest[:7], rest[7:9], rest[9]

    @role(1)
    def run():
        copies = Copies(sems)
        wait_all([copies.start(a, b) for a, b in zip(ins, scratch)])
        x, gain, g, hidden, mix, gproj, update = scratch
        wait_all(send_grads(copies, x, hidden, mix, g, gproj, update, gain[:1, :], dw, outs))


def first_kernel(*refs):
    cells, moved, own, g0, *rest = refs
    pieces, rest = rest[:8], rest[8:]
    saved, rest = rest[: len(RECORDS)], rest[len(RECORDS) :]
    skip = count = 4 * CHUNKS
    outs, rest = rest[skip : skip + count], rest[skip + count :]
    x, g, wq, wk, wv, wo, wg, *rest = rest
    rooms, rest = rest[: len(RECORDS)], rest[len(RECORDS) :]
    gmix, gproj, dw_first, dw_second, sems = rest

    @role(0)
    def run():
        shards = wg.shape[0] // PAD
        micro, size = own.shape[:2]
        copies = Copies(sems)
        w = {"q": wq, "k": wk, "v": wv, "out": wo, "gain": wg}
        early = [copies.start(g0, g)]
        names = ("out", "q", "k", "v", "gain")
        waits = load_weights(copies, pieces, names, w)
        early += [copies.start(a, b) for a, b in zip(saved, rooms)]
        early += load_tokens(copies, moved, own, x)
        wait_all(early)
        for name in names:
            wait_all(waits[name])
        room = dict(zip(RECORDS, rooms))
        grad_update, grad_gain = backward(g, w, full_gain(wg, shards), (micro, size), room, gmix, gproj)
        wait_all(send_grads(copies, x, room["hidden"], room["mix"], g, gproj, grad_update, grad_gain,
                            (dw_first, dw_second), outs))


def rest_kernel(merge, got, out, gain, packed):
    size, width = out.shape
    rows = gain.shape[1]
    upper = lax.axis_index("dp") >= lax.axis_size("dp") // 2
    kept = jnp.where(upper, merge[size:, :].astype(F32), merge[:size, :].astype(F32))
    packed[:size, :] = (kept + got[...].astype(F32)).astype(BF16)
    packed[size : 2 * size, :] = out[...]
    packed[2 * size :, :] = jnp.zeros((PAD, width), BF16)
    packed[2 * size :, :rows] = jnp.broadcast_to(gain[...], (PAD, rows))


def final_kernel(*refs):
    halves, (near, far), (merge, qkv, out, gain) = refs[: 4 * CHUNKS], refs[4 * CHUNKS : -4], refs[-4:]
    feature = merge.shape[2]
    size = qkv.shape[1]
    first, second, _ = layout(feature, feature // size)
    even = lax.axis_index("band") % 2 == 0
    upper = lax.axis_index("dp") >= feature // size // 2
    width = feature // CHUNKS

    def chosen(mine, theirs, side):
        a, b = (theirs, mine) if side else (mine, theirs)
        return jnp.where(even, a.astype(F32), b.astype(F32))

    def rows(name, chunk, side):
        which = 0 if name in first else 1
        own, other = halves[4 * chunk + 2 * which : 4 * chunk + 2 * which + 2]
        start, count = (second if which else first)[name]
        return chosen(own[start : start + count, :], other[start : start + count, :], side)

    for chunk in range(CHUNKS):
        for side in range(2):
            low = chunk * width + side * (width // 2)
            high = low + width // 2
            piece = slice(chunk * width // 2, (chunk + 1) * width // 2)
            here, there = rows("merge", chunk, side), chosen(near[:, piece], far[:, piece], side)
            merge[0, :size, low:high] = jnp.where(upper, there, here)
            merge[0, size:, low:high] = jnp.where(upper, here, there)
            for i, (name, begin, count) in enumerate(
                (("q", 0, size), ("k0", 0, size // 2), ("k1", size // 2, size // 2), ("v", 0, size))
            ):
                at = (0, 1, 1, 2)[i] * feature
                qkv[0, begin : begin + count, at + low : at + high] = rows(name, chunk, side)
            out[0, :, low:high] = rows("out", chunk, side)
    gain[...] = rows("gain", 0, 0)[:1, : gain.shape[1]]


ANY = pl.BlockSpec(memory_space=pl.ANY)
VMEM = pl.BlockSpec(memory_space=pltpu.VMEM)


def call(kernel, ins, outs, scratch, aliases, flops):
    moved = sum(a.size * a.dtype.itemsize for a in list(ins) + list(outs))
    return pl.pallas_call(
        kernel,
        out_shape=tuple(outs),
        in_specs=[ANY] * len(ins),
        out_specs=tuple([ANY] * len(outs)),
        scratch_shapes=scratch,
        input_output_aliases=aliases,
        cost_estimate=pl.CostEstimate(flops=flops, bytes_accessed=moved, transcendentals=0),
    )(*ins)


def flip(value, axis, bit):
    size = lax.axis_size(axis)
    return lax.ppermute(value, axis, [(i, i ^ bit) for i in range(size)])


def gather(qkv, rest):
    high = lax.axis_size("dp") // 2

    def named(value, bit):
        return flip(value, "dp", bit)

    qkv_low, qkv_high = named(qkv, 1), named(qkv, high)
    rest_low, rest_high = named(rest, 1), named(rest, high)
    qkv_both = named(qkv_high, 1)
    rest_both = named(rest_low, high)
    return (qkv, qkv_low, qkv_high, qkv_both, rest, rest_low, rest_high, rest_both)


def body(fields, cell_mask, merge_weight, qkv_weight, out_weight, norm_gain, out_cotangent):
    _, micro, row_count, lon_count, feature = fields.shape
    shards, bands = lax.axis_size("dp"), lax.axis_size("band")
    assert lax.axis_size("segment") == 2 and row_count == WH and shards == 4
    segment, band = lax.axis_index("segment"), lax.axis_index("band")
    cells = row_count * lon_count
    total = micro * cells
    _, _, half = layout(feature, shards)
    rows = feature // shards

    def shape(*dims, dtype=BF16):
        return jax.ShapeDtypeStruct(dims, dtype)

    def room(*dims, dtype=BF16):
        return pltpu.VMEM(dims, dtype)

    merge, qkv, out = merge_weight[0], qkv_weight[0], out_weight[0]
    upper = lax.axis_index("dp") >= shards // 2
    got = flip(jnp.where(upper, merge[:rows], merge[rows:]), "dp", shards // 2)
    rest = pl.pallas_call(
        rest_kernel,
        out_shape=shape(2 * rows + PAD, feature),
        in_specs=[VMEM] * 4,
        out_specs=VMEM,
        name="pack",
    )(merge, got, out, norm_gain)
    pieces = gather(qkv, rest)

    down = [(i, (i + 1) % bands) for i in range(bands)]
    up = [(j, i) for i, j in down]
    flat = (micro, cells, feature)
    source = jnp.where(segment == 0, fields[0, :, row_count - SH :], out_cotangent[0, :, row_count - SH :])
    moved = lax.ppermute(source, "band", down)
    moved = moved.reshape(micro, SH * lon_count, feature)
    mask_moved = lax.ppermute(cell_mask[0, :, row_count - SH :], "band", down)
    mask = jnp.concatenate([mask_moved, cell_mask[0, :, : row_count - SH]], axis=1).reshape(micro, cells)
    own_fields = fields.reshape(flat)
    own_cotangent = out_cotangent.reshape(flat)

    square = room(feature, feature)
    tokens = room(total, feature)
    wide = room(total, 3 * feature)
    mask_room = pltpu.VMEM((micro, cells), jnp.int32)
    weights = [square] * 4 + [room(shards * PAD, feature)]
    merge_room = square
    record_rooms = [
        room(total, feature, dtype=F32), room(total, 128, dtype=F32), tokens, wide, tokens,
        room(micro * HEADS // 2, 2 * cells, cells),
    ]
    grad_rooms = [room(shards, half, feature)] * 2
    sems = [pltpu.SemaphoreType.DMA((128,))]
    unit = 2 * total * feature * feature
    token_shape, wide_shape = shape(total, feature), shape(total, 3 * feature)

    y, *records = call(
        forward_kernel,
        (mask, moved, own_fields) + pieces,
        [token_shape, shape(total, feature, dtype=F32), shape(total, 128, dtype=F32),
         token_shape, wide_shape, token_shape, shape(micro * HEADS // 2, 2 * cells, cells)],
        [mask_room, tokens, merge_room] + weights + [tokens] + record_rooms + sems,
        {}, 6 * unit,
    )
    y0 = lax.ppermute(y, "segment", [(0, 1)])
    gain_room = room(8, feature, dtype=F32)
    y, g_out, *operands = call(
        last_kernel,
        (mask, moved, own_cotangent, y0) + pieces + (y,),
        [token_shape, token_shape, shape(8, feature, dtype=F32), token_shape, token_shape, token_shape,
         wide_shape, token_shape],
        [mask_room, tokens, tokens, merge_room] + weights + [tokens, tokens] + record_rooms
        + [tokens, wide, gain_room, tokens] + sems,
        {12: 0}, 13 * unit,
    )
    g0 = lax.ppermute(g_out, "segment", [(1, 0)])
    shard_shapes = [shape(2, half, feature // CHUNKS)] * (4 * CHUNKS)
    grads = call(
        weight_kernel,
        (y0,) + tuple(operands),
        shard_shapes,
        [tokens, gain_room, tokens, tokens, tokens, wide, tokens] + grad_rooms + sems,
        {}, 5 * unit,
    )

    y = y.reshape(micro, cells, feature)
    part = SH * lon_count
    back = lax.ppermute(y[:, :part], "band", up)
    section_out = jnp.concatenate([y[:, part:], back], axis=1)
    section_out = section_out.reshape(1, 1, micro, row_count, lon_count, feature)

    inputs = (mask, moved, own_fields, g0) + pieces + tuple(records)
    grads = call(
        first_kernel,
        inputs + tuple(grads),
        shard_shapes,
        [tokens, tokens] + weights + record_rooms + [tokens, wide] + grad_rooms + sems,
        {len(inputs) + i: i for i in range(4 * CHUNKS)}, 12 * unit,
    )

    high = shards // 2
    even = band % 2 == 0
    side = feature // CHUNKS // 2
    halves = []

    def named(value, axis, bit):
        return flip(value, axis, bit).astype(F32)

    for chunk in range(CHUNKS):
        for which, bits in (("p", (high, 1)), ("q", (1, high))):
            keep, send = grads[4 * chunk + 2 * (which == "q") :][:2]
            got = named(send, "dp", bits[0])
            on = (keep[1].astype(F32) + got[1]).astype(BF16)
            total_here = keep[0].astype(F32) + got[0] + named(on, "dp", bits[1])
            left, right = total_here[:, :side], total_here[:, side:]
            mine = jnp.where(even, left, right)
            theirs = jnp.where(even, right, left).astype(BF16)
            mine = (mine + named(theirs, "band", 1)).astype(BF16)
            bit = 2
            while bit < bands:
                mine = (mine.astype(F32) + named(mine, "band", bit)).astype(BF16)
                bit *= 2
            halves += [mine, flip(mine, "band", 1)]
    pieces = jnp.concatenate([halves[4 * chunk][:rows] for chunk in range(CHUNKS)], axis=1)
    pairs_far = [
        (i * bands + j, (i ^ high) * bands + (j ^ 1)) for i in range(shards) for j in range(bands)
    ]
    halves.append(flip(pieces, "dp", high))
    halves.append(lax.ppermute(pieces, ("dp", "band"), pairs_far))
    merge_grad, qkv_grad, out_grad, gain_grad = pl.pallas_call(
        final_kernel,
        out_shape=(
            shape(1, 2 * rows, feature, dtype=F32), shape(1, rows, 3 * feature, dtype=F32),
            shape(1, rows, feature, dtype=F32), shape(1, rows, dtype=F32),
        ),
        in_specs=[VMEM] * len(halves),
        out_specs=(VMEM,) * 4,
        name="unpack",
    )(*halves)
    return (section_out, merge_grad, qkv_grad, out_grad, gain_grad)


def solution(mesh):
    return jax.shard_map(
        body,
        mesh=mesh,
        in_specs=(
            P("dp", None, "band", None, None),
            P("dp", None, "band", None),
            P("segment", "dp", None),
            P("segment", "dp", None),
            P("segment", "dp", None),
            P("segment", "dp"),
            P("dp", None, "band", None, None),
        ),
        out_specs=(
            P("segment", "dp", None, "band", None, None),
            P("segment", "dp", None),
            P("segment", "dp", None),
            P("segment", "dp", None),
            P("segment", "dp"),
        ),
        check_vma=False,
    )
```

```python
import jax
import jax.numpy as jnp
from jax import lax
from jax.experimental import pallas as pl
from jax.experimental.pallas import tpu as pltpu
from jax.sharding import PartitionSpec as P


HEADS = 8
WH = 8
WW = 16
SH = 4
SW = 8
PAD = 16
CHUNKS = 2

EPSILON = 1e-05
MASKED = -1e30


F32 = jnp.float32
BF16 = jnp.bfloat16


def dot(a, b):
    return lax.dot_general(a, b, (((1,), (0,)), ((), ())), preferred_element_type=F32)


def dot_nt(a, b):
    return lax.dot_general(a, b, (((1,), (1,)), ((), ())), preferred_element_type=F32)


def dot_tn(a, b):
    return lax.dot_general(a, b, (((0,), (0,)), ((), ())), preferred_element_type=F32)


class Copies:
    def __init__(self, sems):
        self.sems = sems
        self.used = 0

    def start(self, src, dst):
        copy = pltpu.make_async_copy(src, dst, self.sems.at[self.used])
        self.used += 1
        copy.start()
        return copy


def waiter(started):
    def need(*names):
        for name in names:
            wait_all(started.pop(name, ()))

    return need


def wait_all(copies):
    for copy in copies:
        copy.wait()


def layout(feature, shards):
    rows = feature // shards
    part = rows // 2
    first = {"merge": (0, rows), "q": (rows, rows), "gain": (2 * rows, PAD), "k0": (2 * rows + PAD, part)}
    second = {"k1": (0, part), "v": (part, rows), "out": (part + rows, rows), "pad": (part + 2 * rows, PAD)}
    return (first, second, 2 * rows + part + PAD)


def load_weights(copies, pieces, names, dst):
    me = lax.axis_index("dp")
    shards = len(pieces) // 2
    started = {}
    for name in names:
        kind, column = WHERE[name]
        arrays = pieces[:shards] if kind == "qkv" else pieces[shards:]
        started[name] = []
        for flip, ref in zip((0, 1, shards // 2, shards - 1), arrays):
            owner = me ^ flip
            rows = dst[name].shape[0] // shards
            if name == "merge":
                owner = (owner % 2) * (shards // 2) + owner // 2
            at = pl.multiple_of(owner * rows, rows)
            if kind == "rest":
                source = ref.at[pl.ds(column * ((ref.shape[0] - PAD) // 2), rows)]
            else:
                width = dst[name].shape[1]
                source = ref.at[:, pl.ds(column * width, width)]
            started[name].append(copies.start(source, dst[name].at[pl.ds(at, rows)]))
    return started


WHERE = {
    "q": ("qkv", 0), "k": ("qkv", 1), "v": ("qkv", 2),
    "merge": ("rest", 0), "out": ("rest", 1), "gain": ("rest", 2),
}


def load_tokens(copies, moved, own, dst):
    started = []
    for m in range(moved.shape[0]):
        part = moved.shape[1]
        size = own.shape[1]
        started.append(copies.start(moved.at[m], dst.at[pl.ds(m * size, part)]))
        started.append(
            copies.start(
                own.at[m, pl.ds(0, size - part)], dst.at[pl.ds(m * size + part, size - part)]
            )
        )
    return started


def full_gain(gain, shards):
    feature = gain.shape[1]
    rows = feature // shards
    parts = [gain[i * PAD : i * PAD + 1, :rows] for i in range(shards)]
    return jnp.concatenate(parts, axis=1).astype(F32)


def window_allowed(mask_row, first_band, lon_count):
    cells = mask_row.shape[1]
    query = lax.broadcasted_iota(jnp.int32, (cells, cells), 0)
    key = lax.broadcasted_iota(jnp.int32, (cells, cells), 1)
    lon_same = (query % lon_count + SW) // WW == (key % lon_count + SW) // WW
    lat_same = (query // lon_count) // SH == (key // lon_count) // SH
    inside = lon_same & (lat_same | jnp.logical_not(first_band))
    usable = jnp.broadcast_to(mask_row, (cells, cells)) == 1
    return inside & (usable | (query == key))


def stacked_heads(pair, head_dim):
    lane = lax.broadcasted_iota(jnp.int32, pair.shape, 1)
    zero = jnp.zeros_like(pair)
    return jnp.concatenate(
        [jnp.where(lane < head_dim, pair, zero), jnp.where(lane < head_dim, zero, pair)], axis=0
    )


def unstacked_heads(stacked, head_dim):
    cells = stacked.shape[0] // 2
    low, high = stacked[:cells], stacked[cells:]
    lane = lax.broadcasted_iota(jnp.int32, low.shape, 1)
    return jnp.where(lane < head_dim, low, high)


def probabilities(scores, allowed2, head_dim):
    scores = jnp.where(allowed2, scores * head_dim ** (-0.5), MASKED)
    weights = jnp.exp(scores - jnp.max(scores, axis=-1, keepdims=True))
    return weights * (1.0 / jnp.sum(weights, axis=-1, keepdims=True))


def masks(mask, first_band, lon_count):
    out = []
    for m in range(mask.shape[0]):
        allowed = window_allowed(mask[m : m + 1, :], first_band, lon_count)
        out.append(jnp.concatenate([allowed, allowed], axis=0))
    return out


def pairs(micro, cells, feature):
    lanes = 2 * (feature // HEADS)
    count = feature // lanes
    rows = slice(micro * cells, (micro + 1) * cells)
    return [(micro * count + p, rows, p * lanes, lanes) for p in range(count)]


def part_of(qkv, which, rows, at, lanes):
    feature = qkv.shape[1] // 3
    return qkv[rows, which * feature + at : which * feature + at + lanes]


def attend(qkv, mix, probs, allowed, mask_shape, feature):
    head_dim = feature // HEADS
    for m in range(mask_shape[0]):
        group = pairs(m, mask_shape[1], feature)
        scores = [
            dot_nt(stacked_heads(part_of(qkv, 0, *where), head_dim), part_of(qkv, 1, *where))
            for _, *where in group
        ]
        for (n, *_), score in zip(group, scores):
            probs[n] = probabilities(score, allowed[m], head_dim).astype(BF16)
        for n, rows, at, lanes in group:
            mixed = dot(probs[n], part_of(qkv, 2, rows, at, lanes))
            mix[rows, at : at + lanes] = unstacked_heads(mixed, head_dim).astype(BF16)


def attend_back(qkv, probs, grad_mix, grad_proj, mask_shape, feature):
    head_dim = feature // HEADS

    def put(which, grad, rows, at, lanes):
        grad_proj[rows, which * feature + at : which * feature + at + lanes] = grad.astype(BF16)

    for m in range(mask_shape[0]):
        group = pairs(m, mask_shape[1], feature)
        grad_probs = []
        for n, rows, at, lanes in group:
            g_stack = stacked_heads(grad_mix[rows, at : at + lanes], head_dim)
            grad_probs.append(dot_nt(g_stack, part_of(qkv, 2, rows, at, lanes)))
            put(2, dot_tn(probs[n], g_stack), rows, at, lanes)
        grad_scores = []
        for (n, *_), grad in zip(group, grad_probs):
            prob = probs[n].astype(F32)
            inner = jnp.sum(grad * prob, axis=-1, keepdims=True)
            grad_scores.append((prob * (grad - inner) * head_dim ** (-0.5)).astype(BF16))
        for (n, rows, at, lanes), grad in zip(group, grad_scores):
            q_stack = stacked_heads(part_of(qkv, 0, rows, at, lanes), head_dim)
            put(0, unstacked_heads(dot(grad, part_of(qkv, 1, rows, at, lanes)), head_dim), rows, at, lanes)
            put(1, dot_tn(grad, q_stack), rows, at, lanes)


def normalize(update):
    average = jnp.mean(update, axis=-1, keepdims=True)
    centered = update - average
    spread = jnp.mean(centered * centered, axis=-1, keepdims=True)
    inverse = lax.rsqrt(spread + EPSILON)
    return (centered * inverse, inverse)


def forward(x, w, waits, gain_of, allowed, mask_shape, room, kept):
    feature = x.shape[1]
    wait_all(waits["merge"])
    update = dot(x[...], w["merge"][...])
    normed, inverse = normalize(update)
    room["normed"][...] = normed
    kept("normed")
    room["inverse"][...] = jnp.broadcast_to(inverse, room["inverse"].shape)
    kept("inverse")
    hidden, qkv, mix = room["hidden"], room["qkv"], room["mix"]
    hidden[...] = (normed * gain_of()).astype(BF16)
    kept("hidden")
    for i, name in enumerate(("q", "k", "v")):
        wait_all(waits[name])
        qkv[:, i * feature : (i + 1) * feature] = dot(hidden[...], w[name][...]).astype(BF16)
    kept("qkv")
    attend(qkv, mix, room["probs"], allowed, mask_shape, feature)
    kept("probs")
    kept("mix")
    wait_all(waits["out"])
    return update + dot(mix[...], w["out"][...])


RECORDS = ("normed", "inverse", "hidden", "qkv", "mix", "probs")


def backward(grad_out, w, gain_of, mask_shape, room, grad_mix, grad_proj, need):
    feature = grad_out.shape[1]
    need("grad_out", "out")
    grad_mix[...] = dot_nt(grad_out[...], w["out"][...]).astype(BF16)
    need("qkv", "probs")
    attend_back(room["qkv"], room["probs"], grad_mix, grad_proj, mask_shape, feature)
    need("q", "k", "v", "normed", "inverse", "gain")
    gain = gain_of()
    grad_hidden = sum(
        dot_nt(grad_proj[:, i * feature : (i + 1) * feature], w[name][...])
        for i, name in enumerate(("q", "k", "v"))
    )
    normed, inverse = room["normed"][...], room["inverse"]
    grad_gain = jnp.sum(grad_hidden * normed, axis=0, keepdims=True)
    grad_normed = grad_hidden * gain
    centered = (
        grad_normed
        - jnp.mean(grad_normed, axis=-1, keepdims=True)
        - normed * jnp.mean(grad_normed * normed, axis=-1, keepdims=True)
    )
    grad_update = grad_out[...].astype(F32) + inverse[:, :1] * centered
    return (grad_update.astype(BF16), grad_gain)


def send_grads(copies, x, hidden, mix, grad_out, grad_proj, grad_update, gain_of, dw, outs, need):
    feature = x.shape[1]
    shards = 2 * outs[0].shape[0]
    first, second, half = layout(feature, shards)
    me = lax.axis_index("dp")
    low, high = me % 2, me // 2
    rows = feature // shards
    width = feature // CHUNKS
    dw_first, dw_second = dw
    started = []

    def put(name, value, row_of):
        block = dw_first if name in first else dw_second
        start, size = first[name] if name in first else second[name]
        for i in range(shards):
            block[i, start : start + size, :] = value[row_of(i) : row_of(i) + size]

    def emit(which, start, size):
        block = (dw_first, dw_second)[which]
        for chunk in range(CHUNKS):
            p_keep, p_send, q_keep, q_send = outs[4 * chunk : 4 * chunk + 4]
            for by_high in range(2):
                for by_low in range(2):
                    owner = (high ^ by_high) * 2 + (low ^ by_low)
                    if which:
                        ref = (q_send if by_low else q_keep).at[by_high]
                    else:
                        ref = (p_send if by_high else p_keep).at[by_low]
                    part = block.at[owner, pl.ds(start, size), pl.ds(chunk * width, width)]
                    started.append(copies.start(part, ref.at[pl.ds(start, size)]))

    def of_projection(i):
        part = grad_proj[:, i * feature : (i + 1) * feature]
        return dot_tn(hidden[...], part).astype(BF16)

    need("mix", "grad_out")
    put("out", dot_tn(mix[...], grad_out[...]).astype(BF16), lambda i: i * rows)
    need("hidden", "grad_proj")
    grad_k = of_projection(1)
    put("k1", grad_k, lambda i: i * rows + rows // 2)
    put("v", of_projection(2), lambda i: i * rows)
    dw_second[:, second["pad"][0] :, :] = jnp.zeros((shards, PAD, feature), BF16)
    emit(1, 0, half)
    put("k0", grad_k, lambda i: i * rows)
    put("q", of_projection(0), lambda i: i * rows)
    start = first["gain"][0]
    need("grad_gain")
    grad_gain = gain_of()
    for i in range(shards):
        part = grad_gain[:, i * rows : (i + 1) * rows].astype(BF16)
        dw_first[i, start : start + PAD, :] = jnp.zeros((PAD, feature), BF16)
        dw_first[i, start : start + PAD, :rows] = jnp.broadcast_to(part, (PAD, rows))
    emit(0, first["q"][0], half - first["q"][0])
    need("x", "grad_update")
    put("merge", dot_tn(x[...], grad_update[...]).astype(BF16),
        lambda i: (i % 2) * 2 * rows + (i // 2) * rows)
    emit(0, 0, first["merge"][1])
    return started


def lon_of(cells):
    return cells // WH


def role(segment):
    return pl.when(lax.axis_index("segment") == segment)


def forward_kernel(*refs):
    mask_in, moved, own, *rest = refs
    pieces, rest = rest[:8], rest[8:]
    y, rest = rest[0], rest[1:]
    saved, rest = dict(zip(RECORDS, rest)), rest[len(RECORDS) :]
    mask, x, wm, wq, wk, wv, wo, wg, y_s, *rest = rest
    room, sems = dict(zip(RECORDS, rest)), rest[-1]

    @role(0)
    def run():
        shards = wg.shape[0] // PAD
        copies = Copies(sems)
        w = {"merge": wm, "q": wq, "k": wk, "v": wv, "out": wo, "gain": wg}
        mask_copy = copies.start(mask_in, mask)
        tokens = load_tokens(copies, moved, own, x)
        names = ("merge", "gain", "q", "k", "v", "out")
        waits = load_weights(copies, pieces, names, w)
        mask_copy.wait()
        allowed = masks(mask, lax.axis_index("band") == 0, lon_of(mask.shape[1]))
        wait_all(tokens)

        def gain_of():
            wait_all(waits["gain"])
            return full_gain(wg, shards)

        done = []

        def kept(name):
            done.append(copies.start(room[name], saved[name]))

        result = forward(x, w, waits, gain_of, allowed, mask.shape, room, kept)
        y_s[...] = result.astype(BF16)
        done.append(copies.start(y_s, y))
        wait_all(done)


def last_kernel(*refs):
    mask_in, moved, own, y0, *rest = refs
    pieces, rest = rest[:8], rest[9:]
    y, g0, gain_out, g_out, hidden, mix, proj_out, update_out, *rest = rest
    mask, x, g, wm, wq, wk, wv, wo, wg, y_s, g_s, *rest = rest
    room, rest = dict(zip(RECORDS, rest)), rest[len(RECORDS) :]
    gmix, gproj, gain_s, update_s, sems = rest

    @role(1)
    def run():
        shards = wg.shape[0] // PAD
        copies = Copies(sems)
        w = {"merge": wm, "q": wq, "k": wk, "v": wv, "out": wo, "gain": wg}
        mask_copy = copies.start(mask_in, mask)
        x_in = copies.start(y0, x)
        names = ("merge", "gain", "q", "k", "v", "out")
        waits = load_weights(copies, pieces, names, w)
        tokens = load_tokens(copies, moved, own, g)
        mask_copy.wait()
        allowed = masks(mask, lax.axis_index("band") == 0, lon_of(mask.shape[1]))
        x_in.wait()

        def gain_of():
            wait_all(waits["gain"])
            return full_gain(wg, shards)

        done = []

        def kept(name):
            if name in ("hidden", "mix"):
                done.append(copies.start(room[name], hidden if name == "hidden" else mix))

        result = forward(x, w, waits, gain_of, allowed, mask.shape, room, kept)
        y_s[...] = result.astype(BF16)
        wait_all(tokens)
        done += [copies.start(y_s, y), copies.start(g, g_out)]
        grad_update, grad_gain = backward(g, w, lambda: full_gain(wg, shards), mask.shape, room, gmix, gproj,
                                          waiter({}))
        done.append(copies.start(gproj, proj_out))
        gain_s[...] = jnp.broadcast_to(grad_gain, gain_s.shape)
        update_s[...] = grad_update
        done += [copies.start(gain_s, gain_out), copies.start(update_s, update_out)]
        g_s[...] = dot_nt(grad_update, wm[...]).astype(BF16)
        done.append(copies.start(g_s, g0))
        wait_all(done)


def weight_kernel(*refs):
    ins, outs, rest = refs[:7], refs[7 : 7 + 4 * CHUNKS], refs[7 + 4 * CHUNKS :]
    scratch, dw, sems = rest[:7], rest[7:9], rest[9]

    @role(1)
    def run():
        copies = Copies(sems)
        names = ("x", "grad_gain", "grad_out", "hidden", "mix", "grad_proj", "grad_update")
        arrays = dict(zip(names, zip(ins, scratch)))
        order = ("mix", "grad_out", "hidden", "grad_proj", "grad_gain", "x", "grad_update")
        need = waiter({name: [copies.start(*arrays[name])] for name in order})
        x, gain, g, hidden, mix, gproj, update = scratch
        wait_all(send_grads(copies, x, hidden, mix, g, gproj, update, lambda: gain[:1, :], dw, outs, need))


def first_kernel(*refs):
    cells, moved, own, g0, *rest = refs
    pieces, rest = rest[:8], rest[8:]
    saved, rest = rest[: len(RECORDS)], rest[len(RECORDS) :]
    skip = count = 4 * CHUNKS
    outs, rest = rest[skip : skip + count], rest[skip + count :]
    x, g, wq, wk, wv, wo, wg, *rest = rest
    rooms, rest = rest[: len(RECORDS)], rest[len(RECORDS) :]
    gmix, gproj, dw_first, dw_second, sems = rest

    @role(0)
    def run():
        shards = wg.shape[0] // PAD
        micro, size = own.shape[:2]
        copies = Copies(sems)
        w = {"q": wq, "k": wk, "v": wv, "out": wo, "gain": wg}
        room = dict(zip(RECORDS, rooms))
        started = {"grad_out": [copies.start(g0, g)]}

        def fetch(*names):
            for name in names:
                if name in w:
                    started.update(load_weights(copies, pieces, (name,), w))
                else:
                    started[name] = [copies.start(saved[RECORDS.index(name)], room[name])]

        fetch("out", "qkv", "probs", "q", "k", "v", "normed", "inverse", "gain", "mix", "hidden")
        started["x"] = load_tokens(copies, moved, own, x)
        need = waiter(started)
        grad_update, grad_gain = backward(g, w, lambda: full_gain(wg, shards), (micro, size), room,
                                          gmix, gproj, need)
        wait_all(send_grads(copies, x, room["hidden"], room["mix"], g, gproj, grad_update,
                            lambda: grad_gain, (dw_first, dw_second), outs, need))


def rest_kernel(merge, got, out, gain, packed):
    size, width = out.shape
    rows = gain.shape[1]
    upper = lax.axis_index("dp") >= lax.axis_size("dp") // 2
    kept = jnp.where(upper, merge[size:, :].astype(F32), merge[:size, :].astype(F32))
    packed[:size, :] = (kept + got[...].astype(F32)).astype(BF16)
    packed[size : 2 * size, :] = out[...]
    packed[2 * size :, :] = jnp.zeros((PAD, width), BF16)
    packed[2 * size :, :rows] = jnp.broadcast_to(gain[...], (PAD, rows))


def final_kernel(*refs):
    halves, (near, far), (merge, qkv, out, gain) = refs[: 4 * CHUNKS], refs[4 * CHUNKS : -4], refs[-4:]
    feature = merge.shape[2]
    size = qkv.shape[1]
    first, second, _ = layout(feature, feature // size)
    even = lax.axis_index("band") % 2 == 0
    upper = lax.axis_index("dp") >= feature // size // 2
    width = feature // CHUNKS

    def chosen(mine, theirs, side):
        a, b = (theirs, mine) if side else (mine, theirs)
        return jnp.where(even, a.astype(F32), b.astype(F32))

    def rows(name, chunk, side):
        which = 0 if name in first else 1
        own, other = halves[4 * chunk + 2 * which : 4 * chunk + 2 * which + 2]
        start, count = (second if which else first)[name]
        return chosen(own[start : start + count, :], other[start : start + count, :], side)

    for chunk in range(CHUNKS):
        for side in range(2):
            low = chunk * width + side * (width // 2)
            high = low + width // 2
            piece = slice(chunk * width // 2, (chunk + 1) * width // 2)
            here, there = rows("merge", chunk, side), chosen(near[:, piece], far[:, piece], side)
            merge[0, :size, low:high] = jnp.where(upper, there, here)
            merge[0, size:, low:high] = jnp.where(upper, here, there)
            for i, (name, begin, count) in enumerate(
                (("q", 0, size), ("k0", 0, size // 2), ("k1", size // 2, size // 2), ("v", 0, size))
            ):
                at = (0, 1, 1, 2)[i] * feature
                qkv[0, begin : begin + count, at + low : at + high] = rows(name, chunk, side)
            out[0, :, low:high] = rows("out", chunk, side)
    gain[...] = rows("gain", 0, 0)[:1, : gain.shape[1]]


ANY = pl.BlockSpec(memory_space=pl.ANY)
VMEM = pl.BlockSpec(memory_space=pltpu.VMEM)


def call(kernel, ins, outs, scratch, aliases, flops):
    moved = sum(a.size * a.dtype.itemsize for a in list(ins) + list(outs))
    return pl.pallas_call(
        kernel,
        out_shape=tuple(outs),
        in_specs=[ANY] * len(ins),
        out_specs=tuple([ANY] * len(outs)),
        scratch_shapes=scratch,
        input_output_aliases=aliases,
        cost_estimate=pl.CostEstimate(flops=flops, bytes_accessed=moved, transcendentals=0),
    )(*ins)


def flip(value, axis, bit):
    size = lax.axis_size(axis)
    return lax.ppermute(value, axis, [(i, i ^ bit) for i in range(size)])


def gather(qkv, rest):
    high = lax.axis_size("dp") // 2

    def named(value, bit):
        return flip(value, "dp", bit)

    qkv_low, qkv_high = named(qkv, 1), named(qkv, high)
    rest_low, rest_high = named(rest, 1), named(rest, high)
    qkv_both = named(qkv_high, 1)
    rest_both = named(rest_low, high)
    return (qkv, qkv_low, qkv_high, qkv_both, rest, rest_low, rest_high, rest_both)


def body(fields, cell_mask, merge_weight, qkv_weight, out_weight, norm_gain, out_cotangent):
    _, micro, row_count, lon_count, feature = fields.shape
    shards, bands = lax.axis_size("dp"), lax.axis_size("band")
    assert lax.axis_size("segment") == 2 and row_count == WH and shards == 4
    segment, band = lax.axis_index("segment"), lax.axis_index("band")
    cells = row_count * lon_count
    total = micro * cells
    _, _, half = layout(feature, shards)
    rows = feature // shards

    def shape(*dims, dtype=BF16):
        return jax.ShapeDtypeStruct(dims, dtype)

    def room(*dims, dtype=BF16):
        return pltpu.VMEM(dims, dtype)

    merge, qkv, out = merge_weight[0], qkv_weight[0], out_weight[0]
    upper = lax.axis_index("dp") >= shards // 2
    got = flip(jnp.where(upper, merge[:rows], merge[rows:]), "dp", shards // 2)
    rest = pl.pallas_call(
        rest_kernel,
        out_shape=shape(2 * rows + PAD, feature),
        in_specs=[VMEM] * 4,
        out_specs=VMEM,
        compiler_params=pltpu.CompilerParams(vmem_limit_bytes=16 << 20),
        name="pack",
    )(merge, got, out, norm_gain)
    pieces = gather(qkv, rest)

    down = [(i, (i + 1) % bands) for i in range(bands)]
    up = [(j, i) for i, j in down]
    flat = (micro, cells, feature)
    source = jnp.where(segment == 0, fields[0, :, row_count - SH :], out_cotangent[0, :, row_count - SH :])
    moved = lax.ppermute(source, "band", down)
    moved = moved.reshape(micro, SH * lon_count, feature)
    mask_moved = lax.ppermute(cell_mask[0, :, row_count - SH :], "band", down)
    mask = jnp.concatenate([mask_moved, cell_mask[0, :, : row_count - SH]], axis=1).reshape(micro, cells)
    own_fields = fields.reshape(flat)
    own_cotangent = out_cotangent.reshape(flat)

    square = room(feature, feature)
    tokens = room(total, feature)
    wide = room(total, 3 * feature)
    mask_room = pltpu.VMEM((micro, cells), jnp.int32)
    weights = [square] * 4 + [room(shards * PAD, feature)]
    merge_room = square
    record_rooms = [
        room(total, feature, dtype=F32), room(total, 128, dtype=F32), tokens, wide, tokens,
        room(micro * HEADS // 2, 2 * cells, cells),
    ]
    grad_rooms = [room(shards, half, feature)] * 2
    sems = [pltpu.SemaphoreType.DMA((128,))]
    unit = 2 * total * feature * feature
    token_shape, wide_shape = shape(total, feature), shape(total, 3 * feature)

    y, *records = call(
        forward_kernel,
        (mask, moved, own_fields) + pieces,
        [token_shape, shape(total, feature, dtype=F32), shape(total, 128, dtype=F32),
         token_shape, wide_shape, token_shape, shape(micro * HEADS // 2, 2 * cells, cells)],
        [mask_room, tokens, merge_room] + weights + [tokens] + record_rooms + sems,
        {}, 6 * unit,
    )
    y0 = lax.ppermute(y, "segment", [(0, 1)])
    gain_room = room(8, feature, dtype=F32)
    y, g_out, *operands = call(
        last_kernel,
        (mask, moved, own_cotangent, y0) + pieces + (y,),
        [token_shape, token_shape, shape(8, feature, dtype=F32), token_shape, token_shape, token_shape,
         wide_shape, token_shape],
        [mask_room, tokens, tokens, merge_room] + weights + [tokens, tokens] + record_rooms
        + [tokens, wide, gain_room, tokens] + sems,
        {12: 0}, 13 * unit,
    )
    g0 = lax.ppermute(g_out, "segment", [(1, 0)])
    shard_shapes = [shape(2, half, feature // CHUNKS)] * (4 * CHUNKS)
    grads = call(
        weight_kernel,
        (y0,) + tuple(operands),
        shard_shapes,
        [tokens, gain_room, tokens, tokens, tokens, wide, tokens] + grad_rooms + sems,
        {}, 5 * unit,
    )

    y = y.reshape(micro, cells, feature)
    part = SH * lon_count
    back = lax.ppermute(y[:, :part], "band", up)
    section_out = jnp.concatenate([y[:, part:], back], axis=1)
    section_out = section_out.reshape(1, 1, micro, row_count, lon_count, feature)

    inputs = (mask, moved, own_fields, g0) + pieces + tuple(records)
    grads = call(
        first_kernel,
        inputs + tuple(grads),
        shard_shapes,
        [tokens, tokens] + weights + record_rooms + [tokens, wide] + grad_rooms + sems,
        {len(inputs) + i: i for i in range(4 * CHUNKS)}, 12 * unit,
    )

    high = shards // 2
    even = band % 2 == 0
    side = feature // CHUNKS // 2
    halves = []

    def named(value, axis, bit):
        return flip(value, axis, bit).astype(F32)

    for chunk in range(CHUNKS):
        for which, bits in (("p", (high, 1)), ("q", (1, high))):
            keep, send = grads[4 * chunk + 2 * (which == "q") :][:2]
            got = named(send, "dp", bits[0])
            on = (keep[1].astype(F32) + got[1]).astype(BF16)
            total_here = keep[0].astype(F32) + got[0] + named(on, "dp", bits[1])
            left, right = total_here[:, :side], total_here[:, side:]
            mine = jnp.where(even, left, right)
            theirs = jnp.where(even, right, left).astype(BF16)
            mine = (mine + named(theirs, "band", 1)).astype(BF16)
            bit = 2
            while bit < bands:
                mine = (mine.astype(F32) + named(mine, "band", bit)).astype(BF16)
                bit *= 2
            halves += [mine, flip(mine, "band", 1)]
    pieces = jnp.concatenate([halves[4 * chunk][:rows] for chunk in range(CHUNKS)], axis=1)
    pairs_far = [
        (i * bands + j, (i ^ high) * bands + (j ^ 1)) for i in range(shards) for j in range(bands)
    ]
    halves.append(flip(pieces, "dp", high))
    halves.append(lax.ppermute(pieces, ("dp", "band"), pairs_far))
    merge_grad, qkv_grad, out_grad, gain_grad = pl.pallas_call(
        final_kernel,
        out_shape=(
            shape(1, 2 * rows, feature, dtype=F32), shape(1, rows, 3 * feature, dtype=F32),
            shape(1, rows, feature, dtype=F32), shape(1, rows, dtype=F32),
        ),
        in_specs=[VMEM] * len(halves),
        out_specs=(VMEM,) * 4,
        compiler_params=pltpu.CompilerParams(vmem_limit_bytes=16 << 20),
        name="unpack",
    )(*halves)
    return (section_out, merge_grad, qkv_grad, out_grad, gain_grad)


def solution(mesh):
    return jax.shard_map(
        body,
        mesh=mesh,
        in_specs=(
            P("dp", None, "band", None, None),
            P("dp", None, "band", None),
            P("segment", "dp", None),
            P("segment", "dp", None),
            P("segment", "dp", None),
            P("segment", "dp"),
            P("dp", None, "band", None, None),
        ),
        out_specs=(
            P("segment", "dp", None, "band", None, None),
            P("segment", "dp", None),
            P("segment", "dp", None),
            P("segment", "dp", None),
            P("segment", "dp"),
        ),
        check_vma=False,
    )
```
